32 devices in a mesh: fsdp: 8 (over y, x, core), expert: 4 (over z).
Axes of the slice: x: 2, y: 2, z: 4, core: 2. Of those that a mesh axis runs over, the one named last changes fastest.
Arguments:
- inputs: float32 [4096, 1536], P(('fsdp', 'expert')), may hold values from -6 to 6
- cotangent: float32 [4096, 1536], P(('fsdp', 'expert')), may hold values from -6 to 6
- norm1_gain: float32 [1536], P(('fsdp', 'expert')), may hold values from 0.5 to 1.5
- w_query: float32 [1536, 1536], P(('fsdp', 'expert')), may hold values from -0.15625 to 0.15625
- key_projection: float32 [1536, 512], P(('fsdp', 'expert')), may hold values from -0.15625 to 0.15625
- value_projection: float32 [1536, 512], P(('fsdp', 'expert')), may hold values from -0.15625 to 0.15625
- w_output: float32 [1536, 1536], P(('fsdp', 'expert')), may hold values from -2.5 to 2.5
- norm2_gain: float32 [1536], P(('fsdp', 'expert')), may hold values from 0.5 to 1.5
- w_router: float32 [1536, 20], P(('fsdp', 'expert')), may hold values from -0.078125 to 0.078125
- w_gate: float32 [20, 1536, 512], P('expert', 'fsdp'), may hold values from -0.15625 to 0.15625
- w_up: float32 [20, 1536, 512], P('expert', 'fsdp'), may hold values from -0.15625 to 0.15625
- w_down: float32 [20, 512, 1536], P('expert', 'fsdp'), may hold values from -1.5 to 1.5
- routes: int32 [4096, 8], P(('fsdp', 'expert')), may hold values from 0 to 19, all different within a row; in each aligned block of 128 rows (0 to 127, 128 to 255, ...) at most 80 rows name the same one
- piece_starts: int32 [8, 2], P('fsdp'), may hold values from 0 to 256, as said below
Outputs:
- output: float32 [4096, 1536], P(('fsdp', 'expert'))
- input_grad: float32 [4096, 1536], P(('fsdp', 'expert'))
- norm1_gain_grad: float32 [1536], P(('fsdp', 'expert'))
- w_query_grad: float32 [1536, 1536], P(('fsdp', 'expert'))
- w_key_grad: float32 [1536, 512], P(('fsdp', 'expert'))
- w_value_grad: float32 [1536, 512], P(('fsdp', 'expert'))
- w_output_grad: float32 [1536, 1536], P(('fsdp', 'expert'))
- norm2_gain_grad: float32 [1536], P(('fsdp', 'expert'))
- w_router_grad: float32 [1536, 20], P(('fsdp', 'expert'))
- w_gate_grad: float32 [20, 1536, 512], P('expert', 'fsdp')
- w_up_grad: float32 [20, 1536, 512], P('expert', 'fsdp')
- w_down_grad: float32 [20, 512, 1536], P('expert', 'fsdp')
The draws below stay inside these ranges and needn't reach their ends.
Inputs may be any that keep to these rules, and one draw needn't show every extreme that they name: `routes`: each row names 8 different experts. In each aligned block of 128 rows (the rows of one device) no expert is named by more than 80 rows, a bound that some block reaches. `piece_starts`: the p-th image piece of a sequence lies inside positions p * (256) to (p + 1) * 256 - 1; pieces do not intersect.
All inputs are finite; a program needn't handle non-finite values.
Results may differ from the reference program's by a relative error of at most 0.02.
Values may be sent and summed in bfloat16 or wider, within the bound.
A program may use at most 192 MiB of HBM per device.

```python
import math
import jax
import jax.numpy as jnp
import numpy as np
from jax import lax

MODEL_WIDTH = 1536
QUERY_HEADS = 24
KEY_VALUE_HEADS = 8
HEAD_WIDTH = 64
FF = 512
TOPK = 8
PIECE = 256
NPIECE = 2
DEVICE_ROWS = 128
EXPERTS = 20
SEQUENCE_LENGTH = 512
SEQS = 8
TOKENS = 4096
CAP = 80
N_EXPERT = 4


def draw_piece_starts(key, part):
    slot_width = SEQUENCE_LENGTH // NPIECE
    offsets = jax.random.randint(key, (SEQS, NPIECE), 0, slot_width - PIECE + 1, dtype=jnp.int32)
    return (jnp.arange(NPIECE, dtype=jnp.int32) * slot_width)[None, :] + offsets


def level_of(stream_key, extent, shards, least, high):
    level = 1.0
    for dim, parts in shards:
        steps = jax.random.uniform(jax.random.fold_in(jax.random.fold_in(stream_key, 6), dim), (parts,), jnp.float32, least / len(shards), high / len(shards))
        level = level * jnp.repeat(jnp.exp(steps), extent[dim] // parts).reshape((-1,) + (1,) * (len(extent) - 1 - dim))
    return level


def shared_out(own_key, own, number, rows, count, top, most, lean):
    ranking = jax.random.permutation(own_key, count)
    heavy_load, ordinary = load_shares(count, rows * top, most, lean, True), load_shares(count, rows * top, most, lean, False)
    places = jnp.arange(count)

    def named(lengths, turn):
        used = int((lengths > 0).sum())
        fixed = max(1, used // 4)
        moved = fixed + (places - fixed + turn * (used - fixed)) % max(1, count - fixed)
        return jnp.zeros((count,), jnp.int32).at[ranking[jnp.where(places < fixed, places, moved)]].set(jnp.asarray(lengths, jnp.int32))

    lengths = jnp.where(number % 4 == 0, named(heavy_load, number // 4), named(ordinary, number - number // 4 - 1))
    mixed = jax.random.permutation(jax.random.fold_in(own, 3), count)
    donor, receiver = mixed[0:count // 2 * 2:2], mixed[1:count // 2 * 2:2]
    slack = jnp.minimum(lengths[donor] - 1, most - lengths[receiver]) // 2
    slack = jnp.where((donor == ranking[0]) | (receiver == ranking[0]) | (lengths[receiver] == 0), 0, jnp.maximum(slack, 0))
    moved = jax.random.randint(jax.random.fold_in(own, 4), (count // 2,), 0, 1 << 20) % (slack + 1)
    lengths = lengths.at[donor].add(-moved).at[receiver].add(moved)
    items = jnp.searchsorted(jnp.cumsum(lengths), jnp.arange(rows * top), side="right").astype(jnp.int32)
    table = items.reshape(top, rows).T
    table = table[jax.random.permutation(jax.random.fold_in(own, 1), rows)]
    turn = jax.random.randint(jax.random.fold_in(own, 2), (rows, 1), 0, top)
    return jnp.take_along_axis(table, (jnp.arange(top)[None, :] + turn) % top, axis=1)


def load_shares(amount, total, most, slope, full):
    loads = [(1 << 20) // math.isqrt(rank ** slope) + 1 for rank in range(1, amount + 1)]
    largest = most if full else min(most, max(-(-total // amount), total * loads[0] // sum(loads)))
    least = 1 if total - largest >= amount - 1 else 0
    given, rest = [largest] + [least] * (amount - 1), total - largest - least * (amount - 1)
    while rest > 0:
        movable = [i for i in range(1, amount) if given[i] < largest] or [i for i in range(1, amount) if given[i] < most]
        whole, budget = sum([loads[i] for i in movable]), rest
        for i in movable:
            more = min(most - given[i], max(1, budget * loads[i] // whole), rest)
            given[i] = given[i] + more
            rest = rest - more
    return np.array(given)


def gaussian(stream_key, dims, width, most, pieces=(), held_as=jnp.bfloat16):
    factor_of = level_of(stream_key, dims, pieces, -0.22, 0.18) if pieces else 1.0
    values = jax.random.normal(stream_key, dims, jnp.float32) * width * factor_of
    return jnp.minimum(jnp.maximum(values, -most), most).astype(held_as)


def setup_inputs(seed: int = 0) -> dict:
    splits = jax.random.split(jax.random.key(seed), 15)
    inputs = gaussian(splits[0], (TOKENS, MODEL_WIDTH), 1.0, 6.0, ((0, 32),), jnp.float32)
    cotangent = gaussian(splits[1], (TOKENS, MODEL_WIDTH), 1.0, 6.0, ((0, 32),), jnp.float32)
    norm1_gain = jnp.clip(1.0 + 0.1 * jax.random.normal(splits[2], (MODEL_WIDTH,), jnp.float32), 0.5, 1.5)
    w_query = gaussian(splits[3], (MODEL_WIDTH, QUERY_HEADS * HEAD_WIDTH), MODEL_WIDTH ** -0.5, 0.15625, ((0, 32),), jnp.float32)
    key_projection = gaussian(splits[4], (MODEL_WIDTH, KEY_VALUE_HEADS * HEAD_WIDTH), MODEL_WIDTH ** -0.5, 0.15625, ((0, 32),), jnp.float32)
    value_projection = gaussian(splits[5], (MODEL_WIDTH, KEY_VALUE_HEADS * HEAD_WIDTH), MODEL_WIDTH ** -0.5, 0.15625, ((0, 32),), jnp.float32)
    w_output = gaussian(splits[6], (QUERY_HEADS * HEAD_WIDTH, MODEL_WIDTH), (max(QUERY_HEADS * HEAD_WIDTH // 256, 1)) ** -0.5, 2.5, ((0, 32),), jnp.float32)
    norm2_gain = jnp.clip(1.0 + 0.1 * jax.random.normal(splits[7], (MODEL_WIDTH,), jnp.float32), 0.5, 1.5)
    w_router = gaussian(splits[8], (MODEL_WIDTH, EXPERTS), (4 * MODEL_WIDTH) ** -0.5, 0.078125, ((0, 32),), jnp.float32)
    w_gate = gaussian(splits[9], (EXPERTS, MODEL_WIDTH, FF), MODEL_WIDTH ** -0.5, 0.15625, ((0, 4), (1, 8)), jnp.float32)
    w_up = gaussian(splits[10], (EXPERTS, MODEL_WIDTH, FF), MODEL_WIDTH ** -0.5, 0.15625, ((0, 4), (1, 8)), jnp.float32)
    w_down = gaussian(splits[11], (EXPERTS, FF, MODEL_WIDTH), (FF // 32) ** -0.5, 1.5, ((0, 4), (1, 8)), jnp.float32)
    routes_keys = jax.random.split(jax.random.fold_in(splits[12], 1), TOKENS // DEVICE_ROWS)
    routes_turns = jax.random.permutation(jax.random.fold_in(splits[12], 3), TOKENS // DEVICE_ROWS)
    routes = jax.vmap(lambda own, number: shared_out(jax.random.fold_in(splits[12], 2), own, number, DEVICE_ROWS, EXPERTS, TOPK, CAP, 1))(routes_keys, routes_turns).reshape((TOKENS, TOPK))
    piece_starts = draw_piece_starts(jax.random.fold_in(splits[14], 71), 0)
    return {"inputs": inputs, "cotangent": cotangent, "norm1_gain": norm1_gain, "w_query": w_query, "key_projection": key_projection, "value_projection": value_projection, "w_output": w_output, "norm2_gain": norm2_gain, "w_router": w_router, "w_gate": w_gate, "w_up": w_up, "w_down": w_down, "routes": routes, "piece_starts": piece_starts}


EPSILON = 1e-05
NEG_FILL = -1e+30

@jax.custom_vjp
def reduced_precision(v):
    return lax.optimization_barrier(v.astype(jnp.bfloat16)).astype(jnp.float32)

@jax.custom_vjp
def low_back(v):
    return v

def low_keep(v):
    return (reduced_precision(v), None)

def low_pass(kept, grad):
    return (grad,)

def back_keep(v):
    return (v, None)

def back_low(kept, grad):
    return (reduced_precision(grad),)
reduced_precision.defvjp(low_keep, low_pass)
low_back.defvjp(back_keep, back_low)

def wide_dot(left_mat, right_mat):
    return jnp.dot(left_mat, right_mat, precision=lax.Precision.HIGHEST, preferred_element_type=jnp.float32)

def rms_scale(value_rows, gain_row):
    return value_rows * lax.rsqrt(lax.optimization_barrier(jnp.mean(value_rows * value_rows, axis=-1, keepdims=True)) + EPSILON) * gain_row

def apply_rotary(value_rows, position_index):
    half_width = value_rows.shape[-1] // 2
    inverse = 10000.0 ** (-(jnp.arange(half_width, dtype=jnp.float32) * 2.0 / value_rows.shape[-1]))
    angles = position_index.astype(jnp.float32)[:, None] * inverse[None, :]
    cosine = jnp.cos(angles)[:, None, :]
    sine_part = jnp.sin(angles)[:, None, :]
    first_half = value_rows[..., :half_width]
    second_half = value_rows[..., half_width:]
    return jnp.concatenate([first_half * cosine - second_half * sine_part, second_half * cosine + first_half * sine_part], axis=-1)

def piece_ids(position_index, starts):
    inside = (position_index[:, None] >= starts[None, :]) & (position_index[:, None] < starts[None, :] + PIECE)
    labels = jnp.arange(1, starts.shape[0] + 1, dtype=jnp.int32)[None, :]
    return lax.optimization_barrier(jnp.sum(jnp.where(inside, labels, 0), axis=1, dtype=jnp.int32))

def visible_mask(query_places, key_places, starts):
    query_ids = piece_ids(query_places, starts)
    key_ids = piece_ids(key_places, starts)
    causal = key_places[None, :] <= query_places[:, None]
    shared = (query_ids[:, None] == key_ids[None, :]) & (query_ids[:, None] > 0)
    return causal | shared

def layer(weights, seq_rows, seq_routes, seq_starts):
    gain_one, query_w, key_w, value_w, output_w, gain_two, router_w, gate_w, up_w, down_w = weights
    highest = lax.Precision.HIGHEST
    position_index = jnp.arange(SEQUENCE_LENGTH, dtype=jnp.int32)
    query_group_width = QUERY_HEADS // KEY_VALUE_HEADS
    score_scale = HEAD_WIDTH ** (-0.5)
    normed_one = reduced_precision(rms_scale(seq_rows, reduced_precision(gain_one)))
    query_linear = low_back(wide_dot(normed_one, reduced_precision(query_w)))
    key_linear = low_back(wide_dot(normed_one, reduced_precision(key_w)))
    value_reduced = reduced_precision(low_back(wide_dot(normed_one, reduced_precision(value_w))))
    query_rotated = reduced_precision(apply_rotary(query_linear.reshape(SEQUENCE_LENGTH, QUERY_HEADS, HEAD_WIDTH), position_index)).reshape(SEQUENCE_LENGTH, KEY_VALUE_HEADS, query_group_width, HEAD_WIDTH)
    key_rotated = reduced_precision(apply_rotary(key_linear.reshape(SEQUENCE_LENGTH, KEY_VALUE_HEADS, HEAD_WIDTH), position_index))
    value_head_split = value_reduced.reshape(SEQUENCE_LENGTH, KEY_VALUE_HEADS, HEAD_WIDTH)
    scores = low_back(score_scale * jnp.einsum('ihgd,jhd->hgij', query_rotated, key_rotated, precision=highest))
    visible = visible_mask(position_index, position_index, seq_starts)
    scores = jnp.where(visible[None, None], scores, NEG_FILL)
    row_max = lax.optimization_barrier(jnp.max(scores, axis=-1, keepdims=True))
    weights_exp = jnp.exp(scores - row_max)
    prob_rows = reduced_precision(weights_exp / lax.optimization_barrier(jnp.sum(weights_exp, axis=-1, keepdims=True)))
    attended = jnp.einsum('hgij,jhd->ihgd', prob_rows, value_head_split, precision=highest).reshape(SEQUENCE_LENGTH, QUERY_HEADS * HEAD_WIDTH)
    attended = reduced_precision(low_back(attended))
    resid_mid = seq_rows + low_back(wide_dot(attended, reduced_precision(output_w)))
    normed_two = reduced_precision(rms_scale(resid_mid, reduced_precision(gain_two)))
    router_logits = low_back(wide_dot(normed_two, reduced_precision(router_w)))
    chosen = jnp.take_along_axis(router_logits, seq_routes, axis=1)
    chosen_exp = jnp.exp(chosen - lax.optimization_barrier(jnp.max(chosen, axis=1, keepdims=True)))
    gate_probs = chosen_exp / lax.optimization_barrier(jnp.sum(chosen_exp, axis=1, keepdims=True))
    flat_routes = seq_routes.reshape(-1).astype(jnp.int32)
    one_hot = (flat_routes[:, None] == jnp.arange(EXPERTS, dtype=jnp.int32)[None, :]).astype(jnp.int32)
    running = jnp.cumsum(one_hot.reshape(N_EXPERT, DEVICE_ROWS * TOPK, EXPERTS), axis=1, dtype=jnp.int32).reshape(SEQUENCE_LENGTH * TOPK, EXPERTS)
    slot_rank = lax.optimization_barrier(jnp.sum(one_hot * running, axis=1, dtype=jnp.int32)) - 1
    block_index = jnp.arange(SEQUENCE_LENGTH * TOPK, dtype=jnp.int32) // (DEVICE_ROWS * TOPK)
    slot_index = ((flat_routes * N_EXPERT + block_index) * CAP + slot_rank).astype(jnp.int32)
    dispatched = low_back(jnp.repeat(normed_two, TOPK, axis=0))
    slot_rows = jnp.zeros((EXPERTS * N_EXPERT * CAP, MODEL_WIDTH), jnp.float32).at[slot_index].set(dispatched)
    slot_rows = slot_rows.reshape(EXPERTS, N_EXPERT * CAP, MODEL_WIDTH)
    gate_lin = low_back(jnp.einsum('erd,edf->erf', slot_rows, reduced_precision(gate_w), precision=highest))
    up_lin = low_back(jnp.einsum('erd,edf->erf', slot_rows, reduced_precision(up_w), precision=highest))
    hidden_low = reduced_precision(jax.nn.silu(gate_lin) * up_lin)
    expert_out = reduced_precision(low_back(jnp.einsum('erf,efd->erd', hidden_low, reduced_precision(down_w), precision=highest)))
    route_out = expert_out.reshape(EXPERTS * N_EXPERT * CAP, MODEL_WIDTH)[slot_index].reshape(SEQUENCE_LENGTH, TOPK, MODEL_WIDTH)
    return resid_mid + lax.optimization_barrier(jnp.sum(gate_probs[:, :, None] * route_out, axis=1))

def reference(inputs, cotangent, norm1_gain, w_query, key_projection, value_projection, w_output, norm2_gain, w_router, w_gate, w_up, w_down, routes, piece_starts):
    params = (norm1_gain, w_query, key_projection, value_projection, w_output, norm2_gain, w_router, w_gate, w_up, w_down)

    def one_seq(grad_totals, operands):
        seq_in, seq_cot, seq_routes, seq_starts = operands
        seq_out, pullback = jax.vjp(lambda weights, seq_rows: layer(weights, seq_rows, seq_routes, seq_starts), params, seq_in)
        weight_grads, seq_grad = pullback(seq_cot)
        grad_totals = jax.tree.map(lambda total_part, new_part: total_part + new_part, grad_totals, weight_grads)
        return (grad_totals, (seq_out, seq_grad))
    zero_grads = jax.tree.map(jnp.zeros_like, params)
    operands = (inputs.reshape(SEQS, SEQUENCE_LENGTH, MODEL_WIDTH), cotangent.reshape(SEQS, SEQUENCE_LENGTH, MODEL_WIDTH), routes.reshape(SEQS, SEQUENCE_LENGTH, TOPK), piece_starts)
    totals, (seq_outs, seq_grads) = lax.scan(one_seq, zero_grads, operands)
    return (seq_outs.reshape(TOKENS, MODEL_WIDTH), seq_grads.reshape(TOKENS, MODEL_WIDTH), totals[0], totals[1], totals[2], totals[3], totals[4], totals[5], totals[6], totals[7], totals[8], totals[9])
```

```python
import functools

import jax
import jax.numpy as jnp
from jax import lax
from jax.experimental import pallas as pl
from jax.experimental.pallas import tpu as pltpu
from jax.sharding import PartitionSpec as P

QUERY_HEADS = 24
KEY_VALUE_HEADS = 8
GROUP = QUERY_HEADS // KEY_VALUE_HEADS
HEAD_WIDTH = 64
PIECE = 256
LANES = 128
EPSILON = 1e-05
NEG_FILL = -1e30
SCORE_SCALE = HEAD_WIDTH ** (-0.5)
F32 = jnp.float32
BF16 = jnp.bfloat16

VMEM = pl.BlockSpec(memory_space=pltpu.VMEM)
SMEM = pl.BlockSpec(memory_space=pltpu.SMEM)
ANY = pl.BlockSpec(memory_space=pl.ANY)


def dot(a, b):
    return lax.dot_general(a, b, (((1,), (0,)), ((), ())), preferred_element_type=F32)


def dot_nt(a, b):
    return lax.dot_general(a, b, (((1,), (1,)), ((), ())), preferred_element_type=F32)


def dot_tn(a, b):
    return lax.dot_general(a, b, (((0,), (0,)), ((), ())), preferred_element_type=F32)


def shape_of(dims, dtype):
    return jax.ShapeDtypeStruct(tuple(dims), dtype)


def params(**kw):
    return pltpu.CompilerParams(vmem_limit_bytes=60 * 1024 * 1024, **kw)


class Plane:
    def __init__(self):
        self.size = lax.axis_size("fsdp")
        self.rows = self.size // 4
        index = lax.axis_index("fsdp")
        self.index = index
        self.core = index % 2
        self.mid = (index // 2) % 2
        self.row = index // 4

    def other_core(self, x):
        return lax.ppermute(x, "fsdp", [(i, i ^ 1) for i in range(self.size)])

    def other_mid(self, x):
        return lax.ppermute(x, "fsdp", [(i, i ^ 2) for i in range(self.size)])

    def next_row(self, x, step):
        return lax.ppermute(
            x, "fsdp", [(i, (i // 4 + step) % self.rows * 4 + i % 4) for i in range(self.size)]
        )


def natural_pair(own, got, bit, axis=0):
    first = jnp.where(bit == 0, own, got)
    second = jnp.where(bit == 0, got, own)
    return jnp.stack([first, second], axis=axis)


def natural_ring(by_step, me):
    count = len(by_step)
    if count == 2:
        return natural_pair(by_step[0], by_step[1], me)
    out = []
    for place in range(count):
        value = by_step[0]
        for step in range(1, count):
            value = jnp.where((me - place) % count == step, by_step[step], value)
        out.append(value)
    return jnp.stack(out)


def plane_gather(plane, x):
    half = x.shape[1] // 2
    a, b = x[:, :half], x[:, half:]
    a_pair = natural_pair(a, plane.other_mid(a), plane.mid)
    b_rows = natural_ring([b] + [plane.next_row(b, s) for s in range(1, plane.rows)], plane.row)
    a_all = natural_ring(
        [a_pair] + [plane.next_row(a_pair, s) for s in range(1, plane.rows)], plane.row
    )
    b_all = natural_pair(b_rows, plane.other_mid(b_rows), plane.mid, axis=1)
    own = jnp.concatenate([a_all, b_all], axis=-1)
    both = natural_pair(own, plane.other_core(own), plane.core, axis=2)
    return both.reshape((plane.size,) + x.shape)


def plane_scatter(plane, x):
    n, width = x.shape[1:]
    half = width // 2
    x = x.reshape(plane.size // 2, 2, n, width)
    got = plane.other_core(lax.dynamic_index_in_dim(x, 1 - plane.core, 1, keepdims=False))
    kept = lax.dynamic_index_in_dim(x, plane.core, 1, keepdims=False)
    part = (kept.astype(F32) + got.astype(F32)).astype(BF16)
    part = part.reshape(plane.rows, 2, n, width)
    a, b = part[..., :half], part[..., half:]

    def row_of(v, step):
        return lax.dynamic_index_in_dim(v, (plane.row + step) % plane.rows, 0, keepdims=False)

    a_got = [plane.next_row(row_of(a, s), s) for s in range(1, plane.rows)]
    b_got = plane.other_mid(lax.dynamic_index_in_dim(b, 1 - plane.mid, 1, keepdims=False))
    a_sum = row_of(a, 0).astype(F32)
    for v in a_got:
        a_sum = a_sum + v.astype(F32)
    b_sum = lax.dynamic_index_in_dim(b, plane.mid, 1, keepdims=False).astype(F32)
    b_sum = b_sum + b_got.astype(F32)
    a_last = plane.other_mid(
        lax.dynamic_index_in_dim(a_sum, 1 - plane.mid, 0, keepdims=False).astype(BF16)
    )
    b_low = b_sum.astype(BF16)
    b_last = [plane.next_row(row_of(b_low, s), s) for s in range(1, plane.rows)]
    a_out = lax.dynamic_index_in_dim(a_sum, plane.mid, 0, keepdims=False) + a_last.astype(F32)
    b_out = row_of(b_sum, 0)
    for v in b_last:
        b_out = b_out + v.astype(F32)
    return jnp.concatenate([a_out, b_out], axis=-1)


def expert_shift(x, step):
    count = lax.axis_size("expert")
    return lax.ppermute(x, "expert", [(i, (i + step) % count) for i in range(count)])


def expert_gather(x):
    count = lax.axis_size("expert")
    return [x] + [expert_shift(x, s) for s in range(1, count)]


def expert_scatter(blocks):
    count = lax.axis_size("expert")
    return [expert_shift(blocks[s], count - s) for s in range(1, count)]


def pack_kernel(gate, up, down, out_a, out_b):
    width = gate.shape[2]
    half = width // 2
    for place, ref in ((0, gate), (1, up)):
        value = ref[0].astype(BF16)
        out_a[place, 0] = value[:, :half]
        out_b[place, 0] = value[:, half:]
    value = down[0].astype(BF16)
    rows = value.shape[0]
    for j in range(value.shape[1] // width):
        out_a[2, 0, j * rows : (j + 1) * rows] = value[:, j * width : j * width + half]
        out_b[2, 0, j * rows : (j + 1) * rows] = value[:, j * width + half : (j + 1) * width]


def pack_experts(w_gate, w_up, w_down):
    experts, depth, width = w_gate.shape
    out = shape_of((3, experts, depth, width // 2), BF16)
    block = pl.BlockSpec((3, 1, depth, width // 2), lambda e: (0, e, 0, 0))
    return pl.pallas_call(
        pack_kernel,
        grid=(experts,),
        in_specs=[
            pl.BlockSpec((1,) + w.shape[1:], lambda e: (e, 0, 0)) for w in (w_gate, w_up, w_down)
        ],
        out_specs=[block, block],
        out_shape=[out, out],
        name="pack_experts",
    )(w_gate, w_up, w_down)


def swap_halves(x):
    lane = lax.broadcasted_iota(jnp.int32, x.shape, 1)
    return jnp.where(
        lane % HEAD_WIDTH < HEAD_WIDTH // 2, pltpu.roll(x, LANES - 32, 1), pltpu.roll(x, 32, 1)
    )


def head_slice(ref, start):
    return ref[:, start : start + HEAD_WIDTH]


def attend_kernel(
    blocks,
    kv_heads,
    *refs,
):
    x_refs = refs[:blocks]
    gain, weights, out_weights, bias, cosine, sine = refs[blocks : blocks + 6]
    (a1, qk, val, mixed, maxes, inverse) = refs[blocks + 6 : blocks + 12]
    sums = refs[blocks + 12 : blocks + 12 + blocks]
    mixed_t = refs[blocks + 12 + blocks]
    rows = x_refs[0].shape[0]
    rope_width = qk.shape[1]
    q_width = kv_heads * GROUP * HEAD_WIDTH
    for b in range(blocks):
        a1[b * rows : (b + 1) * rows, :] = (x_refs[b][...].astype(F32) * gain[...]).astype(BF16)
    linear = dot(a1[...], weights[:, : rope_width + val.shape[1]])
    for c in range(rope_width // LANES):
        x = linear[:, c * LANES : (c + 1) * LANES]
        qk[:, c * LANES : (c + 1) * LANES] = (
            x * cosine[...] + swap_halves(x) * sine[...]
        ).astype(BF16)
    val[...] = linear[:, rope_width:].astype(BF16)
    for g in range(kv_heads):
        key = head_slice(qk, q_width + g * HEAD_WIDTH)
        value_t = head_slice(val, g * HEAD_WIDTH).T
        for j in range(GROUP):
            h = g * GROUP + j
            scores = dot_nt(key, head_slice(qk, h * HEAD_WIDTH)) * SCORE_SCALE + bias[...]
            top = jnp.max(scores, axis=0, keepdims=True)
            weight = jnp.exp(scores - top)
            inv = 1.0 / jnp.sum(weight, axis=0, keepdims=True)
            maxes[h : h + 1, :] = top
            inverse[h : h + 1, :] = inv
            mixed_t[h * HEAD_WIDTH : (h + 1) * HEAD_WIDTH, :] = dot(
                value_t, (weight * inv).astype(BF16)
            )
    mixed[...] = mixed_t[...].T.astype(BF16)
    total = dot(mixed[...], out_weights[...])
    for b in range(blocks):
        sums[b][...] = total[b * rows : (b + 1) * rows, :].astype(sums[b].dtype)


def attend(x_blocks, gain, weights, out_weights, bias, cosine, sine, kv_heads, rope_width):
    blocks = len(x_blocks)
    rows, model = x_blocks[0].shape
    seq = rows * blocks
    q_width = kv_heads * GROUP * HEAD_WIDTH
    value_width = weights.shape[1] - LANES - rope_width
    heads = kv_heads * GROUP
    outs = [
        shape_of((seq, model), BF16),
        shape_of((seq, rope_width), BF16),
        shape_of((seq, value_width), BF16),
        shape_of((seq, q_width), BF16),
        shape_of((heads, seq), F32),
        shape_of((heads, seq), F32),
    ] + [shape_of((rows, model), F32 if b == 0 else BF16) for b in range(blocks)]
    out = pl.pallas_call(
        functools.partial(attend_kernel, blocks, kv_heads),
        in_specs=[VMEM] * (blocks + 6),
        out_specs=[VMEM] * len(outs),
        out_shape=outs,
        scratch_shapes=[pltpu.VMEM((q_width, seq), F32)],
        compiler_params=params(),
        name="attend",
    )(*x_blocks, gain, weights, out_weights, bias, cosine, sine)
    return out[:6], out[6:]


def middle_kernel(parts, x, gain, *refs):
    h, a2 = refs[parts:]
    total = x[...] + refs[0][...]
    for i in range(1, parts):
        total = total + refs[i][...].astype(F32)
    h[...] = total
    scale = lax.rsqrt(jnp.mean(total * total, axis=-1, keepdims=True) + EPSILON)
    a2[...] = (total * scale * gain[...]).astype(BF16)


def middle(x, gain, parts):
    return pl.pallas_call(
        functools.partial(middle_kernel, len(parts)),
        in_specs=[VMEM] * (2 + len(parts)),
        out_specs=[VMEM] * 2,
        out_shape=[shape_of(x.shape, F32), shape_of(x.shape, BF16)],
        name="middle",
    )(x, gain, *parts)


def experts_kernel(blocks, pieces, place, row_block, *refs):
    a2_in = refs[:blocks]
    grads_in, router_t, where_ref = refs[blocks : blocks + 3]
    piece_refs = refs[blocks + 3 : blocks + 3 + pieces]
    rest = refs[blocks + 3 + pieces :]
    outs = rest[:blocks]
    dxs = rest[blocks : 2 * blocks]
    gates_out, a2_t, hidden_t, d_gate, d_up = rest[2 * blocks : 2 * blocks + 5]
    (a2, gate_w, up_w, down_w, out_sum, dx_sum, gates, dgates, in_sem, w_sem) = rest[
        2 * blocks + 5 :
    ]
    step, steps = pl.program_id(0), pl.num_programs(0)
    rows = a2_in[0].shape[0]
    seq, model = a2.shape
    depth, width = piece_refs[0].shape[2], gate_w.shape[2]
    half = width // 2
    down_rows = depth * width // model
    slot = lax.rem(step, 2)

    def fetch(e, to):
        for i, (row_step, mid, core, part) in enumerate(place):
            source = where_ref[1 + (row_step * 2 + mid) * 2 + core]
            col = part * half
            at = pl.multiple_of(source * depth, 32)
            for which, buf in ((0, gate_w), (1, up_w)):
                pltpu.make_async_copy(
                    piece_refs[i].at[which, e],
                    buf.at[to, pl.ds(at, depth), pl.ds(col, half)],
                    w_sem.at[which, to],
                ).start()
            at = pl.multiple_of(source * down_rows, 32)
            for j in range(model // width):
                pltpu.make_async_copy(
                    piece_refs[i].at[2, e, pl.ds(j * down_rows, down_rows)],
                    down_w.at[to, pl.ds(at, down_rows), pl.ds(j * width + col, half)],
                    w_sem.at[2, to],
                ).start()

    @pl.when(step == 0)
    def _():
        for b in range(blocks):
            pltpu.make_async_copy(
                a2_in[b], a2.at[pl.ds(b * rows, rows)], in_sem.at[0]
            ).start()
        fetch(0, 0)
        pltpu.make_async_copy(a2, a2, in_sem.at[0]).wait()
        logits = dot_nt(a2[...], router_t[...])
        routed = grads_in[:, model:].astype(F32) > 0.5
        top = jnp.max(jnp.where(routed, logits, NEG_FILL), axis=1, keepdims=True)
        weight = jnp.where(routed, jnp.exp(jnp.where(routed, logits, top) - top), 0.0)
        gates[...] = weight / jnp.sum(weight, axis=1, keepdims=True)
        gates_out[...] = gates[:rows, :]
        dgates[...] = jnp.zeros_like(dgates)
        a2_t[...] = a2[...].T

    @pl.when(step + 1 < steps)
    def _():
        fetch(step + 1, 1 - slot)

    for which, buf in ((0, gate_w), (1, up_w), (2, down_w)):
        pltpu.make_async_copy(buf.at[slot], buf.at[slot], w_sem.at[which, slot]).wait()

    mine = where_ref[0] * steps + step

    def block(i, carry):
        at = pl.ds(pl.multiple_of(i * row_block, row_block), row_block)
        left = a2[at, :]
        gate_lin = dot(left, gate_w[slot])
        up_lin = dot(left, up_w[slot])
        back = dot_nt(grads_in[at, :model], down_w[slot])
        lane = lax.broadcasted_iota(jnp.int32, (row_block, LANES), 1)
        here = lane == mine
        gate = jnp.sum(jnp.where(here, gates[at, :], 0.0), axis=1, keepdims=True)
        sig = 1.0 / (1.0 + jnp.exp(-gate_lin))
        silu = gate_lin * sig
        hidden = silu * up_lin
        dgates[at, :] += jnp.where(here, jnp.sum(hidden * back, axis=1, keepdims=True), 0.0)
        hidden_low = (hidden * gate).astype(BF16)
        d_hidden = back * gate
        d_gate_low = (d_hidden * up_lin * (sig + silu * (1.0 - sig))).astype(BF16)
        d_up_low = (d_hidden * silu).astype(BF16)
        d_gate[at, :] = d_gate_low
        d_up[at, :] = d_up_low
        hidden_t[0, :, at] = hidden_low.T
        out_new = dot(hidden_low, down_w[slot])
        dx_new = dot_nt(d_gate_low, gate_w[slot]) + dot_nt(d_up_low, up_w[slot])

        @pl.when(step == 0)
        def _():
            out_sum[at, :] = out_new
            dx_sum[at, :] = dx_new

        @pl.when(step > 0)
        def _():
            out_sum[at, :] += out_new
            dx_sum[at, :] += dx_new

        return carry

    lax.fori_loop(0, seq // row_block, block, 0)

    @pl.when(step == steps - 1)
    def _():
        high = dgates[...].astype(BF16).astype(F32)
        low = dgates[...] - high
        lane = lax.broadcasted_iota(jnp.int32, high.shape, 1)
        tail = jnp.where(lane < LANES // 2, high, pltpu.roll(low, LANES // 2, 1))
        for b in range(blocks):
            at = slice(b * rows, (b + 1) * rows)
            outs[b][...] = out_sum[at, :].astype(outs[b].dtype)
            dxs[b][:, :model] = dx_sum[at, :].astype(dxs[b].dtype)
            dxs[b][:, model:] = tail[at, :].astype(dxs[b].dtype)


def experts(a2_blocks, grads, router_t, where, pieces, place, width):
    blocks = len(a2_blocks)
    rows, model = a2_blocks[0].shape
    seq = rows * blocks
    local, depth = pieces[0].shape[1:3]
    outs = (
        [shape_of((rows, model), F32 if b == 0 else BF16) for b in range(blocks)]
        + [shape_of((rows, model + LANES), F32 if b == 0 else BF16) for b in range(blocks)]
        + [
            shape_of((rows, LANES), F32),
            shape_of((model, seq), BF16),
            shape_of((local, width, seq), BF16),
            shape_of((seq, local * width), BF16),
            shape_of((seq, local * width), BF16),
        ]
    )
    whole = lambda dims: pl.BlockSpec(dims, lambda e: (0,) * len(dims))
    once = lambda dims: pl.BlockSpec(
        dims, lambda e: (0,) * len(dims), pipeline_mode=pl.Buffered(1)
    )
    out_specs = (
        [whole(o.shape) for o in outs[: 2 * blocks + 2]]
        + [pl.BlockSpec((1, width, seq), lambda e: (e, 0, 0))]
        + [pl.BlockSpec((seq, width), lambda e: (0, e))] * 2
    )
    out = pl.pallas_call(
        functools.partial(experts_kernel, blocks, len(pieces), place, 256),
        grid=(local,),
        in_specs=[ANY] * blocks
        + [once(grads.shape), once(router_t.shape), SMEM]
        + [ANY] * len(pieces),
        out_specs=out_specs,
        out_shape=outs,
        scratch_shapes=[
            pltpu.VMEM((seq, model), BF16),
            pltpu.VMEM((2, model, width), BF16),
            pltpu.VMEM((2, model, width), BF16),
            pltpu.VMEM((2, width, model), BF16),
            pltpu.VMEM((seq, model), F32),
            pltpu.VMEM((seq, model), F32),
            pltpu.VMEM((seq, LANES), F32),
            pltpu.VMEM((seq, LANES), F32),
            pltpu.SemaphoreType.DMA((1,)),
            pltpu.SemaphoreType.DMA((3, 2)),
        ],
        compiler_params=params(dimension_semantics=("arbitrary",)),
        name="experts",
    )(*a2_blocks, grads, router_t, where, *pieces)
    return out[:blocks], out[blocks : 2 * blocks], out[2 * blocks :]


def expert_grads_kernel(depth, down_rows, where_ref, a2_t, hidden_t, grads, d_gate, d_up, *outs):
    model, width = a2_t.shape[0], d_gate.shape[1]
    for place, out in enumerate(outs):
        source = where_ref[place]
        at = pl.ds(pl.multiple_of(source * depth, 32), depth)
        out[0, 0] = dot(a2_t[at, :], d_gate[...]).astype(BF16)
        out[1, 0] = dot(a2_t[at, :], d_up[...]).astype(BF16)
        at = pl.ds(pl.multiple_of(source * down_rows, 32), down_rows)
        down = dot(hidden_t[0, at, :], grads[...]).astype(BF16)
        for j in range(model // width):
            out[2, 0, j * down_rows : (j + 1) * down_rows, :] = down[
                :, j * width : (j + 1) * width
            ]


def expert_grads(a2_t, hidden_t, grads, d_gate, d_up, where, plane_size):
    model, seq = a2_t.shape
    local, width = hidden_t.shape[:2]
    depth, down_rows = model // plane_size, width // plane_size
    out = shape_of((3, local, depth, width), BF16)
    block = pl.BlockSpec((3, 1, depth, width), lambda e: (0, e, 0, 0))
    return pl.pallas_call(
        functools.partial(expert_grads_kernel, depth, down_rows),
        grid=(local,),
        in_specs=[
            SMEM,
            pl.BlockSpec((model, seq), lambda e: (0, 0), pipeline_mode=pl.Buffered(1)),
            pl.BlockSpec((1, width, seq), lambda e: (e, 0, 0)),
            pl.BlockSpec((seq, model), lambda e: (0, 0), pipeline_mode=pl.Buffered(1)),
            pl.BlockSpec((seq, width), lambda e: (0, e)),
            pl.BlockSpec((seq, width), lambda e: (0, e)),
        ],
        out_specs=[block, block],
        out_shape=[out, out],
        name="expert_grads",
    )(where, a2_t, hidden_t, grads, d_gate, d_up)


def finish_kernel(kept_a, got_a, kept_b, got_b, gate, up, down):
    half = kept_a.shape[3]
    for part, kept, got in ((0, kept_a, got_a), (1, kept_b, got_b)):
        at = slice(part * half, (part + 1) * half)
        gate[0, :, at] = kept[0, 0].astype(F32) + got[0, 0].astype(F32)
        up[0, :, at] = kept[1, 0].astype(F32) + got[1, 0].astype(F32)
        value = kept[2, 0].astype(F32) + got[2, 0].astype(F32)
        rows = down.shape[1]
        for j in range(value.shape[0] // rows):
            start = j * 2 * half + part * half
            down[0, :, start : start + half] = value[j * rows : (j + 1) * rows]


def finish(kept_a, got_a, kept_b, got_b, down_rows, model):
    local, depth, half = kept_a.shape[1:]
    block = pl.BlockSpec((3, 1, depth, half), lambda e: (0, e, 0, 0))
    outs = [
        shape_of((local, depth, 2 * half), F32),
        shape_of((local, depth, 2 * half), F32),
        shape_of((local, down_rows, model), F32),
    ]
    return pl.pallas_call(
        finish_kernel,
        grid=(local,),
        in_specs=[block] * 4,
        out_specs=[pl.BlockSpec((1,) + o.shape[1:], lambda e: (e, 0, 0)) for o in outs],
        out_shape=outs,
        name="finish",
    )(kept_a, got_a, kept_b, got_b)


def rejoin_kernel(parts, gain_row, gates, h, dz, router_t, a2, *refs):
    dh, dh_low, extra = refs[parts:]
    model = h.shape[1]
    total = refs[0][...]
    for i in range(1, parts):
        total = total + refs[i][...].astype(F32)
    tail = total[:, model:]
    dgates = tail + pltpu.roll(tail, LANES // 2, 1)
    gate = gates[...]
    mean = jnp.sum(gate * dgates, axis=1, keepdims=True)
    d_logits = (gate * (dgates - mean)).astype(BF16)
    da2 = total[:, :model] + dot(d_logits, router_t[...])
    value = h[...]
    scale = lax.rsqrt(jnp.mean(value * value, axis=-1, keepdims=True) + EPSILON)
    normed = value * scale
    gain = router_t[gain_row : gain_row + 1, :].astype(F32)
    weighted = da2 * gain
    grad = dz[...] + scale * (
        weighted - normed * jnp.mean(weighted * normed, axis=-1, keepdims=True)
    )
    dh[...] = grad
    dh_low[...] = grad.astype(BF16)
    gain_grad = jnp.sum(da2 * normed, axis=0, keepdims=True)
    line = lax.broadcasted_iota(jnp.int32, (LANES, model), 0)
    extra[...] = jnp.where(line == gain_row, gain_grad, dot_tn(d_logits, a2[...]))


def rejoin(parts, gates, h, dz, router_t, a2, gain_row):
    return pl.pallas_call(
        functools.partial(rejoin_kernel, len(parts), gain_row),
        in_specs=[VMEM] * (5 + len(parts)),
        out_specs=[VMEM] * 3,
        out_shape=[
            shape_of(h.shape, F32),
            shape_of(h.shape, BF16),
            shape_of((LANES, h.shape[1]), F32),
        ],
        name="rejoin",
    )(gates, h, dz, router_t, a2, *parts)


def attend_back_kernel(blocks, kv_heads, gain_row, *refs):
    dh_refs, x_refs = refs[:blocks], refs[blocks : 2 * blocks]
    (weights, out_weights, a1, qk, val, mixed, maxes, inverse, bias, cosine, sine, extra) = refs[
        2 * blocks : 2 * blocks + 12
    ]
    d_weights, d_out_weights = refs[2 * blocks + 12 : 2 * blocks + 14]
    sums = refs[2 * blocks + 14 : 3 * blocks + 14]
    grads, d_mixed, dq_t, d_qk, d_lin = refs[3 * blocks + 14 :]
    rows = x_refs[0].shape[0]
    rope_width, value_width = qk.shape[1], val.shape[1]
    q_width = kv_heads * GROUP * HEAD_WIDTH
    for b in range(blocks):
        grads[b * rows : (b + 1) * rows, :] = dh_refs[b][...]
    d_mixed[...] = dot_nt(grads[...], out_weights[...]).astype(BF16)
    d_out_weights[...] = dot_tn(mixed[...], grads[...]).astype(BF16)
    if value_width > kv_heads * HEAD_WIDTH:
        d_lin[:, rope_width:] = jnp.zeros((d_lin.shape[0], value_width), BF16)
    for g in range(kv_heads):
        key = head_slice(qk, q_width + g * HEAD_WIDTH)
        key_t = key.T
        value = head_slice(val, g * HEAD_WIDTH)
        d_key, d_value = None, None
        for j in range(GROUP):
            h = g * GROUP + j
            query = head_slice(qk, h * HEAD_WIDTH)
            grad = head_slice(d_mixed, h * HEAD_WIDTH)
            scores = dot_nt(key, query) * SCORE_SCALE + bias[...]
            prob = jnp.exp(scores - maxes[h : h + 1, :]) * inverse[h : h + 1, :]
            d_prob = dot_nt(value, grad)
            inner = jnp.sum(prob * d_prob, axis=0, keepdims=True)
            d_scores = (prob * (d_prob - inner)).astype(BF16)
            dk = dot(d_scores, query)
            dv = dot(prob.astype(BF16), grad)
            d_key = dk if d_key is None else d_key + dk
            d_value = dv if d_value is None else d_value + dv
            dq_t[h * HEAD_WIDTH : (h + 1) * HEAD_WIDTH, :] = dot(key_t, d_scores)
        start = q_width + g * HEAD_WIDTH
        d_qk[:, start : start + HEAD_WIDTH] = d_key * SCORE_SCALE
        start = rope_width + g * HEAD_WIDTH
        d_lin[:, start : start + HEAD_WIDTH] = d_value.astype(BF16)
    d_qk[:, :q_width] = dq_t[...].T * SCORE_SCALE
    for c in range(rope_width // LANES):
        at = slice(c * LANES, (c + 1) * LANES)
        x = d_qk[:, at]
        d_lin[:, at] = (x * cosine[...] - swap_halves(x) * sine[...]).astype(BF16)
    total = dot_nt(d_lin[...], weights[:, : rope_width + value_width])
    gain_grad = None
    for b in range(blocks):
        part = total[b * rows : (b + 1) * rows, :]
        sums[b][...] = part.astype(sums[b].dtype)
        new = jnp.sum(part * x_refs[b][...].astype(F32), axis=0, keepdims=True)
        gain_grad = new if gain_grad is None else gain_grad + new
    d_weights[:, : rope_width + value_width] = dot_tn(a1[...], d_lin[...]).astype(BF16)
    line = lax.broadcasted_iota(jnp.int32, extra.shape, 0)
    tail = jnp.where(line == gain_row, gain_grad, extra[...])
    d_weights[:, rope_width + value_width :] = tail.T.astype(BF16)


def attend_back(dh_blocks, x_blocks, weights, out_weights, kept, bias, cosine, sine, extra, kv_heads, gain_row):
    blocks = len(dh_blocks)
    rows, model = dh_blocks[0].shape
    seq = rows * blocks
    q_width = out_weights.shape[0]
    rope_width, value_width = kept[1].shape[1], kept[2].shape[1]
    outs = [shape_of(weights.shape, BF16), shape_of(out_weights.shape, BF16)] + [
        shape_of((rows, model), F32 if b == 0 else BF16) for b in range(blocks)
    ]
    out = pl.pallas_call(
        functools.partial(attend_back_kernel, blocks, kv_heads, gain_row),
        in_specs=[VMEM] * (2 * blocks + 12),
        out_specs=[VMEM] * len(outs),
        out_shape=outs,
        scratch_shapes=[
            pltpu.VMEM((seq, model), BF16),
            pltpu.VMEM((seq, q_width), BF16),
            pltpu.VMEM((q_width, seq), F32),
            pltpu.VMEM((seq, rope_width), F32),
            pltpu.VMEM((seq, rope_width + value_width), BF16),
        ],
        compiler_params=params(),
        name="attend_back",
    )(*dh_blocks, *x_blocks, weights, out_weights, *kept, bias, cosine, sine, extra)
    return out[0], out[1], out[2:]


def last_kernel(parts, x, dh, gain, *refs):
    out = refs[parts]
    total = refs[0][...]
    for i in range(1, parts):
        total = total + refs[i][...].astype(F32)
    value = x[...]
    scale = lax.rsqrt(jnp.mean(value * value, axis=-1, keepdims=True) + EPSILON)
    normed = value * scale
    weighted = total * gain[...]
    out[...] = dh[...] + scale * (
        weighted - normed * jnp.mean(weighted * normed, axis=-1, keepdims=True)
    )


def last(x, dh, gain, parts):
    return pl.pallas_call(
        functools.partial(last_kernel, len(parts)),
        in_specs=[VMEM] * (3 + len(parts)),
        out_specs=VMEM,
        out_shape=shape_of(x.shape, F32),
        name="last",
    )(x, dh, gain, *parts)


def piece_ids(position_index, starts):
    inside = (position_index[:, None] >= starts[None, :]) & (
        position_index[:, None] < starts[None, :] + PIECE
    )
    labels = jnp.arange(1, starts.shape[0] + 1, dtype=jnp.int32)[None, :]
    return jnp.sum(jnp.where(inside, labels, 0), axis=1, dtype=jnp.int32)


def on_device(
    inputs,
    cotangent,
    norm1_gain,
    w_query,
    key_projection,
    value_projection,
    w_output,
    norm2_gain,
    w_router,
    w_gate,
    w_up,
    w_down,
    routes,
    piece_starts,
):
    plane = Plane()
    ranks = lax.axis_size("expert")
    me = lax.axis_index("expert")
    rows, model = inputs.shape
    seq = rows * ranks
    weight_rows = w_query.shape[0]
    n_experts = w_router.shape[1]
    ff = w_gate.shape[2]
    kv_heads = KEY_VALUE_HEADS // ranks
    q_cols, kv_cols = kv_heads * GROUP * HEAD_WIDTH, kv_heads * HEAD_WIDTH
    rope_width = q_cols + kv_cols
    value_width = -(-kv_cols // LANES) * LANES
    columns = rope_width + value_width + LANES
    gain_one_row, gain_two_row = n_experts, n_experts + 1

    scale_one = lax.rsqrt(jnp.mean(inputs * inputs, axis=-1, keepdims=True) + EPSILON)
    x_blocks = expert_gather((inputs * scale_one).astype(BF16))

    extra_cols = jnp.concatenate(
        [
            w_router,
            norm1_gain[:, None],
            norm2_gain[:, None],
            jnp.zeros((weight_rows, LANES - n_experts - 2), F32),
        ],
        axis=1,
    )
    by_rank = jnp.concatenate(
        [
            w_query.reshape(weight_rows, ranks, q_cols),
            key_projection.reshape(weight_rows, ranks, kv_cols),
            jnp.pad(
                value_projection.reshape(weight_rows, ranks, kv_cols),
                ((0, 0), (0, 0), (0, value_width - kv_cols)),
            ),
            jnp.broadcast_to(extra_cols[:, None, :], (weight_rows, ranks, LANES)),
        ],
        axis=2,
    ).astype(BF16)
    by_rank = jnp.transpose(by_rank, (1, 0, 2))
    from_ranks = [
        expert_shift(
            lax.dynamic_index_in_dim(by_rank, (me + s) % ranks, 0, keepdims=False), s
        )
        if s
        else lax.dynamic_index_in_dim(by_rank, me, 0, keepdims=False)
        for s in range(ranks)
    ]
    column_shard = natural_ring(from_ranks, me).reshape(ranks * weight_rows, columns)
    weights = plane_gather(plane, column_shard).reshape(model, columns)

    axes = ("fsdp", "expert")
    total = plane.size * ranks
    move = [
        (j, (j % plane.size) * ranks + j // plane.size) for j in range(total)
    ]
    out_shard = lax.ppermute(w_output.astype(BF16), axes, move)
    out_weights = plane_gather(plane, out_shard).reshape(q_cols, model)

    lane_ids = jnp.arange(LANES, dtype=jnp.int32)
    routed = jnp.sum((routes[:, :, None] == lane_ids[None, None, :]).astype(F32), axis=1)
    grads = jnp.concatenate(
        expert_gather(jnp.concatenate([cotangent, routed], axis=1).astype(BF16)), axis=0
    )

    part_a, part_b = pack_experts(w_gate, w_up, w_down)
    found = {(0, 0, 0): part_a, (0, 1, 0): plane.other_mid(part_a)}
    found[0, 0, 1] = part_b
    for s in range(1, plane.rows):
        found[s, 0, 1] = plane.next_row(part_b, s)
        for mid in range(2):
            found[s, mid, 0] = plane.next_row(found[0, mid, 0], s)
    for s in range(plane.rows):
        found[s, 1, 1] = plane.other_mid(found[s, 0, 1])
    place, pieces = [], []
    for (s, mid, part), value in found.items():
        place += [(s, mid, 0, part), (s, mid, 1, part)]
        pieces += [value, plane.other_core(value)]
    sources = [
        (((plane.row - s) % plane.rows) * 2 + (plane.mid + mid) % 2) * 2 + (plane.core + core) % 2
        for s in range(plane.rows)
        for mid in range(2)
        for core in range(2)
    ]
    where = jnp.stack([me] + sources).astype(jnp.int32)

    block_ids = jnp.arange(seq, dtype=jnp.int32) // rows
    places = ((me - block_ids) % ranks) * rows + jnp.arange(seq, dtype=jnp.int32) % rows
    ids = piece_ids(places, piece_starts[0])
    visible = (places[:, None] <= places[None, :]) | (
        (ids[:, None] == ids[None, :]) & (ids[None, :] > 0)
    )
    bias = jnp.where(visible, 0.0, NEG_FILL).astype(F32)
    half = HEAD_WIDTH // 2
    inverse = 10000.0 ** (-(jnp.arange(half, dtype=F32) * 2.0 / HEAD_WIDTH))
    angles = places.astype(F32)[:, None] * inverse[None, :]
    cosine = jnp.tile(jnp.cos(angles), (1, LANES // half))
    sine = jnp.tile(jnp.sin(angles), (1, LANES // half)) * jnp.where(
        lane_ids % HEAD_WIDTH < half, -1.0, 1.0
    )
    extra_t = weights[:, columns - LANES :].T
    gain_one = extra_t[gain_one_row : gain_one_row + 1].astype(F32)
    gain_two = extra_t[gain_two_row : gain_two_row + 1].astype(F32)
    kept, sums = attend(
        x_blocks, gain_one, weights, out_weights, bias, cosine, sine, kv_heads, rope_width
    )
    mid_rows, a2 = middle(inputs, gain_two, [sums[0]] + expert_scatter(sums))

    a2_blocks = expert_gather(a2)
    outs, dxs, (gates, a2_t, hidden_t, d_gate, d_up) = experts(
        a2_blocks, grads, extra_t, where, pieces, tuple(place), ff
    )
    dx_got = expert_scatter(dxs)
    grad_rows = grads[:, :model]
    summed = {}
    for s in reversed(range(plane.rows)):
        for mid in (1, 0):
            chip = ((plane.row + s) % plane.rows) * 2 + (plane.mid + mid) % 2
            target = jnp.stack([chip * 2 + plane.core, chip * 2 + 1 - plane.core])
            mine, theirs = expert_grads(
                a2_t, hidden_t, grad_rows, d_gate, d_up, target.astype(jnp.int32), plane.size
            )
            got = plane.other_core(theirs)
            for part in range(2):
                at = slice(part * ff // 2, (part + 1) * ff // 2)
                summed[s, mid, part] = (
                    mine[..., at].astype(F32) + got[..., at].astype(F32)
                ).astype(BF16)

    def add(first, *others):
        value = first.astype(F32)
        for v in others:
            value = value + v.astype(F32)
        return value.astype(BF16)

    steps = range(1, plane.rows)
    a_sums = [
        add(summed[0, mid, 0], *[plane.next_row(summed[s, mid, 0], s) for s in steps])
        for mid in range(2)
    ]
    b_sums = [
        add(summed[s, 0, 1], plane.other_mid(summed[s, 1, 1])) for s in range(plane.rows)
    ]
    a_got = plane.other_mid(a_sums[1])
    b_got = [plane.next_row(b_sums[s], s) for s in steps]
    b_kept = b_sums[0]
    if len(b_got) > 1:
        b_kept = add(b_kept, *b_got[:-1])
    gate_grad, up_grad, down_grad = finish(
        a_sums[0], a_got, b_kept, b_got[-1], w_down.shape[1], model
    )

    dh, dh_low, extra = rejoin(
        [dxs[0]] + dx_got, gates, mid_rows, cotangent, extra_t, a2, gain_two_row
    )

    d_weights, d_out_weights, da1 = attend_back(
        expert_gather(dh_low),
        x_blocks,
        weights,
        out_weights,
        kept,
        bias,
        cosine,
        sine,
        extra,
        kv_heads,
        gain_one_row,
    )
    input_grad = last(inputs, dh, gain_one, [da1[0]] + expert_scatter(da1))
    output = mid_rows + outs[0]
    for v in expert_scatter(outs):
        output = output + v.astype(F32)

    out_part = plane_scatter(
        plane, d_out_weights.reshape(plane.size, q_cols // plane.size, model)
    )
    w_output_grad = lax.ppermute(
        out_part.astype(BF16), axes, [(b, a) for a, b in move]
    ).astype(F32)
    d_shard = plane_scatter(
        plane, d_weights.reshape(plane.size, model // plane.size, columns)
    ).astype(BF16)
    d_shard = d_shard.reshape(ranks, weight_rows, columns)
    own = lax.dynamic_index_in_dim(d_shard, me, 0, keepdims=False)
    arrived = [own] + [
        expert_shift(
            lax.dynamic_index_in_dim(d_shard, (me + s) % ranks, 0, keepdims=False), s
        )
        for s in range(1, ranks)
    ]
    by_rank = natural_ring(arrived, me).astype(F32)

    def columns_of(start, width):
        piece = by_rank[:, :, start : start + width]
        return jnp.transpose(piece, (1, 0, 2)).reshape(weight_rows, ranks * width)

    extra_grad = jnp.sum(by_rank[:, :, columns - LANES :], axis=0)
    return (
        output,
        input_grad,
        extra_grad[:, gain_one_row],
        columns_of(0, q_cols),
        columns_of(q_cols, kv_cols),
        columns_of(rope_width, kv_cols),
        w_output_grad,
        extra_grad[:, gain_two_row],
        extra_grad[:, :n_experts],
        gate_grad,
        up_grad,
        down_grad,
    )


def solution(mesh):
    both = ("fsdp", "expert")
    rows, flat, stack = P(both, None), P(both), P("expert", "fsdp", None)
    weights = (flat, rows, rows, rows, rows, flat, rows, stack, stack, stack)
    return jax.shard_map(
        on_device,
        mesh=mesh,
        in_specs=(rows, rows) + weights + (rows, P("fsdp", None)),
        out_specs=(rows, rows) + weights,
        check_vma=False,
    )
```

```python
import functools

import jax
import jax.numpy as jnp
from jax import lax
from jax.experimental import pallas as pl
from jax.experimental.pallas import tpu as pltpu
from jax.sharding import PartitionSpec as P

QUERY_HEADS = 24
KEY_VALUE_HEADS = 8
GROUP = QUERY_HEADS // KEY_VALUE_HEADS
HEAD_WIDTH = 64
PIECE = 256
LANES = 128
DEVICE_ROWS = 128
EPSILON = 1e-05
NEG_FILL = -1e30
SCORE_SCALE = HEAD_WIDTH ** (-0.5)
F32 = jnp.float32
BF16 = jnp.bfloat16

VMEM = pl.BlockSpec(memory_space=pltpu.VMEM)
SMEM = pl.BlockSpec(memory_space=pltpu.SMEM)
ANY = pl.BlockSpec(memory_space=pl.ANY)
MESH = pl.DeviceIdType.MESH


def dot(a, b):
    return lax.dot_general(a, b, (((1,), (0,)), ((), ())), preferred_element_type=F32)


def dot_nt(a, b):
    return lax.dot_general(a, b, (((1,), (1,)), ((), ())), preferred_element_type=F32)


def dot_tn(a, b):
    return lax.dot_general(a, b, (((0,), (0,)), ((), ())), preferred_element_type=F32)


def shape_of(dims, dtype):
    return jax.ShapeDtypeStruct(tuple(dims), dtype)


def params(**kw):
    return pltpu.CompilerParams(vmem_limit_bytes=60 * 1024 * 1024, **kw)


class Plane:
    def __init__(self):
        self.size = lax.axis_size("fsdp")
        self.rows = self.size // 4
        index = lax.axis_index("fsdp")
        self.index = index
        self.core = index % 2
        self.mid = (index // 2) % 2
        self.row = index // 4

    def other_core(self, x):
        return lax.ppermute(x, "fsdp", [(i, i ^ 1) for i in range(self.size)])

    def other_mid(self, x):
        return lax.ppermute(x, "fsdp", [(i, i ^ 2) for i in range(self.size)])

    def next_row(self, x, step):
        return lax.ppermute(
            x, "fsdp", [(i, (i // 4 + step) % self.rows * 4 + i % 4) for i in range(self.size)]
        )


def expert_shift(x, step):
    count = lax.axis_size("expert")
    return lax.ppermute(x, "expert", [(i, (i + step) % count) for i in range(count)])


def expert_gather(x):
    count = lax.axis_size("expert")
    return [x] + [expert_shift(x, s) for s in range(1, count)]


def expert_scatter(blocks):
    count = lax.axis_size("expert")
    return [expert_shift(blocks[s], count - s) for s in range(1, count)]


def chooser(width, blocks, part, dtype=BF16):
    n = width // blocks
    line = lax.broadcasted_iota(jnp.int32, (width // 2, width), 0)
    column = lax.broadcasted_iota(jnp.int32, (width // 2, width), 1)
    want = (2 * (line // n) + part) * n + line % n
    return jnp.where(column == want, 1.0, 0.0).astype(dtype)


def pack_kernel(blocks, core, gate, up, down, keep, send, halves):
    width = gate.shape[2]
    mine = chooser(width, blocks, core[0])
    theirs = chooser(width, blocks, 1 - core[0])
    for place, ref in ((0, gate), (1, up)):
        value = ref[0].astype(BF16)
        keep[place, 0] = dot_nt(value, mine).astype(BF16)
        send[place, 0] = dot_nt(value, theirs).astype(BF16)
    value = down[0].astype(BF16)
    rows, wide = value.shape[0] // 2, width // 2
    for part in range(2):
        for j in range(value.shape[1] // wide):
            halves[part, 0, j * rows : (j + 1) * rows] = value[
                part * rows : (part + 1) * rows, j * wide : (j + 1) * wide
            ]


def pack_experts(core, w_gate, w_up, w_down, blocks):
    local, depth, width = w_gate.shape
    out = shape_of((2, local, depth, width // 2), BF16)
    block = pl.BlockSpec((2, 1, depth, width // 2), lambda e: (0, e, 0, 0))
    return pl.pallas_call(
        functools.partial(pack_kernel, blocks),
        grid=(local,),
        in_specs=[SMEM]
        + [pl.BlockSpec((1,) + w.shape[1:], lambda e: (e, 0, 0)) for w in (w_gate, w_up, w_down)],
        out_specs=[block] * 3,
        out_shape=[out] * 3,
        name="pack_experts",
    )(core, w_gate, w_up, w_down)


def swap_halves(x):
    lane = lax.broadcasted_iota(jnp.int32, x.shape, 1)
    return jnp.where(
        lane % HEAD_WIDTH < HEAD_WIDTH // 2, pltpu.roll(x, LANES - 32, 1), pltpu.roll(x, 32, 1)
    )


def head_slice(ref, start):
    return ref[:, start : start + HEAD_WIDTH]


def attend_kernel(
    blocks,
    kv_heads,
    *refs,
):
    x_refs = refs[:blocks]
    gain, weights, out_weights, bias, cosine, sine = refs[blocks : blocks + 6]
    (a1, qk, val, mixed, maxes, inverse) = refs[blocks + 6 : blocks + 12]
    sums = refs[blocks + 12 : blocks + 12 + blocks]
    mixed_t = refs[blocks + 12 + blocks]
    rows = x_refs[0].shape[0]
    rope_width = qk.shape[1]
    q_width = kv_heads * GROUP * HEAD_WIDTH
    for b in range(blocks):
        a1[b * rows : (b + 1) * rows, :] = (x_refs[b][...].astype(F32) * gain[...]).astype(BF16)
    linear = dot(a1[...], weights[:, : rope_width + val.shape[1]])
    for c in range(rope_width // LANES):
        x = linear[:, c * LANES : (c + 1) * LANES]
        qk[:, c * LANES : (c + 1) * LANES] = (
            x * cosine[...] + swap_halves(x) * sine[...]
        ).astype(BF16)
    val[...] = linear[:, rope_width:].astype(BF16)
    for g in range(kv_heads):
        key = head_slice(qk, q_width + g * HEAD_WIDTH)
        value_t = head_slice(val, g * HEAD_WIDTH).T
        for j in range(GROUP):
            h = g * GROUP + j
            scores = dot_nt(key, head_slice(qk, h * HEAD_WIDTH)) * SCORE_SCALE + bias[...]
            top = jnp.max(scores, axis=0, keepdims=True)
            weight = jnp.exp(scores - top)
            inv = 1.0 / jnp.sum(weight, axis=0, keepdims=True)
            maxes[h : h + 1, :] = top
            inverse[h : h + 1, :] = inv
            mixed_t[h * HEAD_WIDTH : (h + 1) * HEAD_WIDTH, :] = dot(
                value_t, (weight * inv).astype(BF16)
            )
    mixed[...] = mixed_t[...].T.astype(BF16)
    total = dot(mixed[...], out_weights[...])
    for b in range(blocks):
        sums[b][...] = total[b * rows : (b + 1) * rows, :].astype(sums[b].dtype)


def attend(x_blocks, gain, weights, out_weights, bias, cosine, sine, kv_heads, rope_width):
    blocks = len(x_blocks)
    rows, model = x_blocks[0].shape
    seq = rows * blocks
    q_width = kv_heads * GROUP * HEAD_WIDTH
    value_width = weights.shape[1] - LANES - rope_width
    heads = kv_heads * GROUP
    outs = [
        shape_of((seq, model), BF16),
        shape_of((seq, rope_width), BF16),
        shape_of((seq, value_width), BF16),
        shape_of((seq, q_width), BF16),
        shape_of((heads, seq), F32),
        shape_of((heads, seq), F32),
    ] + [shape_of((rows, model), F32 if b == 0 else BF16) for b in range(blocks)]
    out = pl.pallas_call(
        functools.partial(attend_kernel, blocks, kv_heads),
        in_specs=[VMEM] * (blocks + 6),
        out_specs=[VMEM] * len(outs),
        out_shape=outs,
        scratch_shapes=[pltpu.VMEM((q_width, seq), F32)],
        compiler_params=params(),
        name="attend",
    )(*x_blocks, gain, weights, out_weights, bias, cosine, sine)
    return out[:6], out[6:]


def experts_kernel(blocks, pieces, place, row_block, *refs):
    a2_in = refs[:blocks]
    grads_in, router_t, where_ref = refs[blocks : blocks + 3]
    piece_refs = refs[blocks + 3 : blocks + 3 + pieces]
    (out_all, dx_all, gates_out, a2_t, hidden_t, d_gate, d_up) = refs[
        blocks + 3 + pieces : blocks + 10 + pieces
    ]
    (a2, gate_w, up_w, down_w, out_sum, dx_sum, gates, dgates, in_sem, w_sem) = refs[
        blocks + 10 + pieces :
    ]
    step, steps = pl.program_id(0), pl.num_programs(0)
    rows = a2_in[0].shape[0]
    seq, model = a2.shape
    depth, width = piece_refs[0].shape[2], gate_w.shape[2]
    down_rows = depth * width // model
    slot = lax.rem(step, 2)

    def fetch(e, to):
        for i, (row_step, mid, part) in enumerate(place):
            source = where_ref[1 + row_step * 2 + mid] * 2 + part
            at = pl.multiple_of(source * depth, 32)
            for which, buf in ((0, gate_w), (1, up_w)):
                pltpu.make_async_copy(
                    piece_refs[i].at[which, e], buf.at[to, pl.ds(at, depth)], w_sem.at[which, to]
                ).start()
            at = pl.multiple_of(source * down_rows, 16)
            for j in range(model // width):
                pltpu.make_async_copy(
                    piece_refs[i].at[2, e, pl.ds(j * down_rows, down_rows)],
                    down_w.at[to, pl.ds(at, down_rows), pl.ds(j * width, width)],
                    w_sem.at[2, to],
                ).start()

    @pl.when(step == 0)
    def _():
        for b in range(blocks):
            pltpu.make_async_copy(
                a2_in[b], a2.at[pl.ds(b * rows, rows)], in_sem.at[0]
            ).start()
        fetch(0, 0)
        pltpu.make_async_copy(a2, a2, in_sem.at[0]).wait()
        logits = dot_nt(a2[...], router_t[...])
        routed = grads_in[:, model:].astype(F32) > 0.5
        top = jnp.max(jnp.where(routed, logits, NEG_FILL), axis=1, keepdims=True)
        weight = jnp.where(routed, jnp.exp(jnp.where(routed, logits, top) - top), 0.0)
        gates[...] = weight / jnp.sum(weight, axis=1, keepdims=True)
        gates_out[...] = gates[: gates_out.shape[0], :]
        dgates[...] = jnp.zeros_like(dgates)
        a2_t[...] = a2[...].T

    @pl.when(step + 1 < steps)
    def _():
        fetch(step + 1, 1 - slot)

    for which, buf in ((0, gate_w), (1, up_w), (2, down_w)):
        pltpu.make_async_copy(buf.at[slot], buf.at[slot], w_sem.at[which, slot]).wait()

    mine = where_ref[0] * steps + step

    def block(i, carry):
        at = pl.ds(pl.multiple_of(i * row_block, row_block), row_block)
        left = a2[at, :]
        gate_lin = dot(left, gate_w[slot])
        up_lin = dot(left, up_w[slot])
        back = dot_nt(grads_in[at, :model], down_w[slot])
        lane = lax.broadcasted_iota(jnp.int32, (row_block, LANES), 1)
        here = lane == mine
        gate = jnp.sum(jnp.where(here, gates[at, :], 0.0), axis=1, keepdims=True)
        sig = 1.0 / (1.0 + jnp.exp(-gate_lin))
        silu = gate_lin * sig
        hidden = silu * up_lin
        dgates[at, :] += jnp.where(here, jnp.sum(hidden * back, axis=1, keepdims=True), 0.0)
        hidden_low = (hidden * gate).astype(BF16)
        d_hidden = back * gate
        d_gate_low = (d_hidden * up_lin * (sig + silu * (1.0 - sig))).astype(BF16)
        d_up_low = (d_hidden * silu).astype(BF16)
        d_gate[at, :] = d_gate_low
        d_up[at, :] = d_up_low
        hidden_t[0, :, at] = hidden_low.T
        out_new = dot(hidden_low, down_w[slot])
        dx_new = dot_nt(d_gate_low, gate_w[slot]) + dot_nt(d_up_low, up_w[slot])

        @pl.when(step == 0)
        def _():
            out_sum[at, :] = out_new
            dx_sum[at, :] = dx_new

        @pl.when(step > 0)
        def _():
            out_sum[at, :] += out_new
            dx_sum[at, :] += dx_new

        return carry

    lax.fori_loop(0, seq // row_block, block, 0)

    @pl.when(step == steps - 1)
    def _():
        high = dgates[...].astype(BF16).astype(F32)
        low = dgates[...] - high
        lane = lax.broadcasted_iota(jnp.int32, high.shape, 1)
        tail = jnp.where(lane < LANES // 2, high, pltpu.roll(low, LANES // 2, 1))
        out_all[...] = out_sum[...].astype(out_all.dtype)
        dx_all[:, :model] = dx_sum[...].astype(dx_all.dtype)
        dx_all[:, model:] = tail.astype(dx_all.dtype)


def experts(a2_blocks, grads, router_t, where, pieces, place, dtype):
    blocks = len(a2_blocks)
    rows, model = a2_blocks[0].shape
    seq = rows * blocks
    local, depth, width = pieces[0].shape[1:]
    outs = [
        shape_of((seq, model), dtype),
        shape_of((seq, model + LANES), dtype),
        shape_of((DEVICE_ROWS, LANES), F32),
        shape_of((model, seq), BF16),
        shape_of((local, width, seq), BF16),
        shape_of((seq, local * width), BF16),
        shape_of((seq, local * width), BF16),
    ]
    whole = lambda dims: pl.BlockSpec(
        dims, lambda e: (0,) * len(dims), pipeline_mode=pl.Buffered(1)
    )
    out_specs = (
        [whole(o.shape) for o in outs[:4]]
        + [pl.BlockSpec((1, width, seq), lambda e: (e, 0, 0))]
        + [pl.BlockSpec((seq, width), lambda e: (0, e))] * 2
    )
    return pl.pallas_call(
        functools.partial(experts_kernel, blocks, len(pieces), place, 256),
        grid=(local,),
        in_specs=[ANY] * blocks
        + [whole(grads.shape), whole(router_t.shape), SMEM]
        + [ANY] * len(pieces),
        out_specs=out_specs,
        out_shape=outs,
        scratch_shapes=[
            pltpu.VMEM((seq, model), BF16),
            pltpu.VMEM((2, model, width), BF16),
            pltpu.VMEM((2, model, width), BF16),
            pltpu.VMEM((2, width, model), BF16),
            pltpu.VMEM((seq, model), F32),
            pltpu.VMEM((seq, model), F32),
            pltpu.VMEM((seq, LANES), F32),
            pltpu.VMEM((seq, LANES), F32),
            pltpu.SemaphoreType.DMA((1,)),
            pltpu.SemaphoreType.DMA((3, 2)),
        ],
        compiler_params=params(dimension_semantics=("arbitrary",)),
        name="experts",
    )(*a2_blocks, grads, router_t, where, *pieces)


def expert_grads_kernel(chips, depth, down_rows, where_ref, *refs):
    (a2_t0, a2_t1, hid0, hid1, grads0, grads1, dg0, dg1, du0, du1) = refs[:10]
    outs, down_sum = refs[10 : 10 + 2 * chips], refs[10 + 2 * chips]
    model, width = a2_t0.shape[0], dg0.shape[1]
    down_sum[...] = (dot(hid0[0], grads0[...]) + dot(hid1[0], grads1[...])).astype(BF16)
    for place in range(chips):
        source = where_ref[place]
        at = pl.ds(pl.multiple_of(source * 2 * depth, 32), 2 * depth)
        left0, left1 = a2_t0[at, :], a2_t1[at, :]
        gate = (dot(left0, dg0[...]) + dot(left1, dg1[...])).astype(BF16)
        up = (dot(left0, du0[...]) + dot(left1, du1[...])).astype(BF16)
        for part in range(2):
            out = outs[2 * place + part]
            out[0, 0] = gate[part * depth : (part + 1) * depth]
            out[1, 0] = up[part * depth : (part + 1) * depth]
            at = pl.ds(pl.multiple_of((source * 2 + part) * down_rows, 16), down_rows)
            down = down_sum[at, :]
            for j in range(model // width):
                out[2, 0, j * down_rows : (j + 1) * down_rows, :] = down[
                    :, j * width : (j + 1) * width
                ]


def expert_grads(where, first, second, plane_size):
    model, seq = first[0].shape
    local, width = first[1].shape[:2]
    chips = plane_size // 2
    depth, down_rows = model // plane_size, width // plane_size
    out = shape_of((3, local, depth, width), BF16)
    block = pl.BlockSpec((3, 1, depth, width), lambda e: (0, e, 0, 0))
    once = lambda dims: pl.BlockSpec(dims, lambda e: (0, 0), pipeline_mode=pl.Buffered(1))
    specs = [
        once((model, seq)),
        pl.BlockSpec((1, width, seq), lambda e: (e, 0, 0)),
        once((seq, model)),
        pl.BlockSpec((seq, width), lambda e: (0, e)),
        pl.BlockSpec((seq, width), lambda e: (0, e)),
    ]
    operands = [v for pair in zip(first, second) for v in pair]
    return pl.pallas_call(
        functools.partial(expert_grads_kernel, chips, depth, down_rows),
        grid=(local,),
        in_specs=[SMEM] + [spec for spec in specs for _ in range(2)],
        out_specs=[block] * (2 * chips),
        out_shape=[out] * (2 * chips),
        scratch_shapes=[pltpu.VMEM((width, model), BF16)],
        compiler_params=params(),
        name="expert_grads",
    )(where, *operands)


def finish_kernel(blocks, core, kept_a, got_a, kept_b, got_b, other, gate, up, down):
    width, wide = gate.shape[2], kept_a.shape[3]
    mine = chooser(width, blocks, core[0])
    theirs = chooser(width, blocks, 1 - core[0])
    first = core[0] == 0
    for place, out in ((0, gate), (1, up)):
        kept = jnp.where(first, kept_a[place, 0].astype(F32), kept_b[place, 0].astype(F32))
        got = jnp.where(first, got_a[place, 0].astype(F32), got_b[place, 0].astype(F32))
        out[0] = (
            dot(kept.astype(BF16), mine)
            + dot(got.astype(BF16), mine)
            + dot(other[place, 0], theirs)
        )
    rows = down.shape[1] // 2
    for part, kept, got in ((0, kept_a, got_a), (1, kept_b, got_b)):
        value = kept[2, 0].astype(F32) + got[2, 0].astype(F32)
        for j in range(value.shape[0] // rows):
            down[0, part * rows : (part + 1) * rows, j * wide : (j + 1) * wide] = value[
                j * rows : (j + 1) * rows
            ]


def finish(core, kept_a, got_a, kept_b, got_b, other, down_rows, model, blocks):
    local, depth, wide = kept_a.shape[1:]
    block = pl.BlockSpec((3, 1, depth, wide), lambda e: (0, e, 0, 0))
    outs = [
        shape_of((local, depth, 2 * wide), F32),
        shape_of((local, depth, 2 * wide), F32),
        shape_of((local, down_rows, model), F32),
    ]
    return pl.pallas_call(
        functools.partial(finish_kernel, blocks),
        grid=(local,),
        in_specs=[SMEM]
        + [block] * 4
        + [pl.BlockSpec((2, 1, depth, wide), lambda e: (0, e, 0, 0))],
        out_specs=[pl.BlockSpec((1,) + o.shape[1:], lambda e: (e, 0, 0)) for o in outs],
        out_shape=outs,
        name="finish",
    )(core, kept_a, got_a, kept_b, got_b, other)


def attend_back_kernel(blocks, kv_heads, gain_row, *refs):
    dh_ref, x_refs = refs[0], refs[1 : blocks + 1]
    (weights, out_weights, a1, qk, val, mixed, maxes, inverse, bias, cosine, sine, extra) = refs[
        blocks + 1 : blocks + 13
    ]
    d_weights, d_out_weights = refs[blocks + 13 : blocks + 15]
    sums = refs[blocks + 15 : 2 * blocks + 15]
    grads, d_mixed, dq_t, d_qk, d_lin = refs[2 * blocks + 15 :]
    rows = x_refs[0].shape[0]
    rope_width, value_width = qk.shape[1], val.shape[1]
    q_width = kv_heads * GROUP * HEAD_WIDTH
    for b in range(blocks):
        grads[b * rows : (b + 1) * rows, :] = dh_ref[b]
    d_mixed[...] = dot_nt(grads[...], out_weights[...]).astype(BF16)
    d_out_weights[...] = dot_tn(mixed[...], grads[...]).astype(BF16)
    if value_width > kv_heads * HEAD_WIDTH:
        d_lin[:, rope_width:] = jnp.zeros((d_lin.shape[0], value_width), BF16)
    for g in range(kv_heads):
        key = head_slice(qk, q_width + g * HEAD_WIDTH)
        key_t = key.T
        value = head_slice(val, g * HEAD_WIDTH)
        d_key, d_value = None, None
        for j in range(GROUP):
            h = g * GROUP + j
            query = head_slice(qk, h * HEAD_WIDTH)
            grad = head_slice(d_mixed, h * HEAD_WIDTH)
            scores = dot_nt(key, query) * SCORE_SCALE + bias[...]
            prob = jnp.exp(scores - maxes[h : h + 1, :]) * inverse[h : h + 1, :]
            d_prob = dot_nt(value, grad)
            inner = jnp.sum(prob * d_prob, axis=0, keepdims=True)
            d_scores = (prob * (d_prob - inner)).astype(BF16)
            dk = dot(d_scores, query)
            dv = dot(prob.astype(BF16), grad)
            d_key = dk if d_key is None else d_key + dk
            d_value = dv if d_value is None else d_value + dv
            dq_t[h * HEAD_WIDTH : (h + 1) * HEAD_WIDTH, :] = dot(key_t, d_scores)
        start = q_width + g * HEAD_WIDTH
        d_qk[:, start : start + HEAD_WIDTH] = d_key * SCORE_SCALE
        start = rope_width + g * HEAD_WIDTH
        d_lin[:, start : start + HEAD_WIDTH] = d_value.astype(BF16)
    d_qk[:, :q_width] = dq_t[...].T * SCORE_SCALE
    for c in range(rope_width // LANES):
        at = slice(c * LANES, (c + 1) * LANES)
        x = d_qk[:, at]
        d_lin[:, at] = (x * cosine[...] - swap_halves(x) * sine[...]).astype(BF16)
    total = dot_nt(d_lin[...], weights[:, : rope_width + value_width])
    gain_grad = None
    for b in range(blocks):
        part = total[b * rows : (b + 1) * rows, :]
        sums[b][...] = part.astype(sums[b].dtype)
        new = jnp.sum(part * x_refs[b][...].astype(F32), axis=0, keepdims=True)
        gain_grad = new if gain_grad is None else gain_grad + new
    d_weights[:, : rope_width + value_width] = dot_tn(a1[...], d_lin[...]).astype(BF16)
    line = lax.broadcasted_iota(jnp.int32, extra.shape, 0)
    tail = jnp.where(line == gain_row, gain_grad, extra[...])
    d_weights[:, rope_width + value_width :] = tail.T.astype(BF16)


def attend_back(
    dh_stack, x_blocks, weights, out_weights, kept, bias, cosine, sine, extra, kv_heads, gain_row
):
    blocks, rows, model = dh_stack.shape
    seq = rows * blocks
    q_width = out_weights.shape[0]
    rope_width, value_width = kept[1].shape[1], kept[2].shape[1]
    outs = [shape_of(weights.shape, BF16), shape_of(out_weights.shape, BF16)] + [
        shape_of((rows, model), F32 if b == 0 else BF16) for b in range(blocks)
    ]
    out = pl.pallas_call(
        functools.partial(attend_back_kernel, blocks, kv_heads, gain_row),
        in_specs=[VMEM] * (blocks + 13),
        out_specs=[VMEM] * len(outs),
        out_shape=outs,
        scratch_shapes=[
            pltpu.VMEM((seq, model), BF16),
            pltpu.VMEM((seq, q_width), BF16),
            pltpu.VMEM((q_width, seq), F32),
            pltpu.VMEM((seq, rope_width), F32),
            pltpu.VMEM((seq, rope_width + value_width), BF16),
        ],
        compiler_params=params(),
        name="attend_back",
    )(dh_stack, *x_blocks, weights, out_weights, *kept, bias, cosine, sine, extra)
    return out[0], out[1], out[2:]


class Spot:
    def __init__(self, ranks, plane_size):
        self.ranks, self.chips = ranks, plane_size // 2
        self.rank = lax.axis_index("expert")
        self.index = lax.axis_index("fsdp")
        self.chip = self.index // 2
        self.core = self.index % 2

    def behind(self, s):
        return {"expert": lax.rem(self.rank - s + self.ranks, self.ranks)}

    def ahead(self, s):
        return {"expert": lax.rem(self.rank + s, self.ranks)}

    def partner(self):
        return {"fsdp": self.chip * 2 + (1 - self.core)}

    def chip_ahead(self, k):
        return lax.rem(self.chip + k, self.chips)

    def chip_behind(self, k):
        return lax.rem(self.chip - k + self.chips, self.chips)

    def on_chip(self, chip):
        return {"fsdp": chip * 2 + self.core}


def meet(peers):
    barrier = pltpu.get_barrier_semaphore()
    for peer in peers:
        pl.semaphore_signal(barrier, inc=1, device_id=peer, device_id_type=MESH)
    pl.semaphore_wait(barrier, len(peers))


def send(src, dst, send_sem, recv_sem, peer):
    copy = pltpu.make_async_remote_copy(
        src_ref=src,
        dst_ref=dst,
        send_sem=send_sem,
        recv_sem=recv_sem,
        device_id=peer,
        device_id_type=MESH,
    )
    copy.start()
    return copy


def remote(collective_id):
    return params(collective_id=collective_id, has_side_effects=True)


def gather_weights_kernel(ranks, plane_size, by_rank, rows_in, weights, out_rows, *sems):
    z_send, z_recv, p_send, p_recv, c_send, c_recv, local = sems
    spot = Spot(ranks, plane_size)
    f, me, chips = spot.index, spot.rank, spot.chips
    others = range(1, ranks)
    meet(
        [spot.ahead(s) for s in others]
        + [spot.on_chip(spot.chip_ahead(k)) for k in range(1, chips)]
        + [spot.partner()]
    )
    waits = []
    z_copies = [
        send(
            by_rank.at[lax.rem(me + s, ranks)],
            weights.at[f, me],
            z_send.at[s - 1],
            z_recv.at[s - 1],
            spot.ahead(s),
        )
        for s in others
    ]
    kept = [
        pltpu.make_async_copy(by_rank.at[me], weights.at[f, me], local.at[0]),
        pltpu.make_async_copy(rows_in, out_rows.at[f], local.at[1]),
    ]
    for copy in kept:
        copy.start()

    def spread(which, src, buf):
        return [
            send(
                src,
                buf.at[f],
                p_send.at[which, k - 1],
                p_recv.at[which, k - 1],
                spot.on_chip(spot.chip_ahead(k)),
            )
            for k in range(1, chips)
        ] + [send(src, buf.at[f], c_send.at[which, 0], c_recv.at[which, 0], spot.partner())]

    row_copies = spread(1, rows_in, out_rows)
    for copy in kept + z_copies:
        copy.wait()
    weight_copies = spread(0, weights.at[f], weights)
    for k in range(1, chips):
        source = spot.chip_behind(k) * 2 + spot.core
        for which, copies, buf in ((1, row_copies, out_rows), (0, weight_copies, weights)):
            copies[k - 1].wait()
            waits.append(
                send(
                    buf.at[source],
                    buf.at[source],
                    c_send.at[which, k],
                    c_recv.at[which, k],
                    spot.partner(),
                )
            )
    row_copies[-1].wait()
    weight_copies[-1].wait()
    for copy in waits:
        copy.wait()


def gather_weights(by_rank, rows_in, plane_size):
    ranks, rows, columns = by_rank.shape
    chips = plane_size // 2
    dma = pltpu.SemaphoreType.DMA
    return pl.pallas_call(
        functools.partial(gather_weights_kernel, ranks, plane_size),
        in_specs=[VMEM] * 2,
        out_specs=[VMEM] * 2,
        out_shape=[
            shape_of((plane_size, ranks, rows, columns), BF16),
            shape_of((plane_size,) + rows_in.shape, BF16),
        ],
        scratch_shapes=[
            dma((ranks - 1,)),
            dma((ranks - 1,)),
            dma((2, chips - 1)),
            dma((2, chips - 1)),
            dma((2, chips)),
            dma((2, chips)),
            dma((2,)),
        ],
        compiler_params=remote(0),
        name="gather_weights",
    )(by_rank, rows_in)


def scatter_start(spot, refs, buf, send_sem, recv_sem):
    return [
        send(refs[s], buf.at[s - 1], send_sem.at[s - 1], recv_sem.at[s - 1], spot.behind(s))
        for s in range(1, spot.ranks)
    ]


def middle_kernel(ranks, plane_size, x, gain, *refs):
    sums = refs[:ranks]
    h, a2, gathered, other = refs[ranks : ranks + 4]
    got, r_send, r_recv, g_send, g_recv, c_send, c_recv = refs[ranks + 4 :]
    spot = Spot(ranks, plane_size)
    meet([spot.ahead(s) for s in range(1, ranks)] + [spot.partner()])
    copies = scatter_start(spot, sums, got, r_send, r_recv)
    total = x[...] + sums[0][...]
    for s in range(1, ranks):
        copies[s - 1].wait()
        total = total + got[s - 1].astype(F32)
    scale = lax.rsqrt(jnp.mean(total * total, axis=-1, keepdims=True) + EPSILON)
    low = (total * scale * gain[...]).astype(BF16)
    gathered[0] = low
    a2[...] = low
    h[...] = total
    copies = [
        send(
            gathered.at[0], gathered.at[s], g_send.at[s - 1], g_recv.at[s - 1], spot.ahead(s)
        )
        for s in range(1, ranks)
    ]
    across = [
        send(gathered.at[0], other.at[0], c_send.at[0], c_recv.at[0], spot.partner())
    ]
    for s in range(1, ranks):
        copies[s - 1].wait()
        across.append(
            send(gathered.at[s], other.at[s], c_send.at[s], c_recv.at[s], spot.partner())
        )
    for copy in across:
        copy.wait()


def middle(x, gain, sums, plane_size):
    ranks = len(sums)
    dma = pltpu.SemaphoreType.DMA
    stack = shape_of((ranks,) + x.shape, BF16)
    return pl.pallas_call(
        functools.partial(middle_kernel, ranks, plane_size),
        in_specs=[VMEM] * (2 + ranks),
        out_specs=[VMEM] * 4,
        out_shape=[shape_of(x.shape, F32), shape_of(x.shape, BF16), stack, stack],
        scratch_shapes=[
            pltpu.VMEM((ranks - 1,) + x.shape, BF16),
            dma((ranks - 1,)),
            dma((ranks - 1,)),
            dma((ranks - 1,)),
            dma((ranks - 1,)),
            dma((ranks,)),
            dma((ranks,)),
        ],
        compiler_params=remote(1),
        name="middle",
    )(x, gain, *sums)


def rejoin_kernel(ranks, plane_size, gain_row, gates, h, dz, router_t, a2, *refs):
    parts = refs[:ranks]
    dh, gathered, extra, g_send, g_recv = refs[ranks:]
    model = h.shape[1]
    spot = Spot(ranks, plane_size)
    meet([spot.ahead(s) for s in range(1, ranks)])
    total = parts[0][...]
    for i in range(1, ranks):
        total = total + parts[i][...].astype(F32)
    tail = total[:, model:]
    dgates = tail + pltpu.roll(tail, LANES // 2, 1)
    gate = gates[...]
    mean = jnp.sum(gate * dgates, axis=1, keepdims=True)
    d_logits = (gate * (dgates - mean)).astype(BF16)
    da2 = total[:, :model] + dot(d_logits, router_t[...])
    value = h[...]
    scale = lax.rsqrt(jnp.mean(value * value, axis=-1, keepdims=True) + EPSILON)
    normed = value * scale
    gain = router_t[gain_row : gain_row + 1, :].astype(F32)
    weighted = da2 * gain
    grad = dz[...] + scale * (
        weighted - normed * jnp.mean(weighted * normed, axis=-1, keepdims=True)
    )
    gathered[0] = grad.astype(BF16)
    dh[...] = grad
    copies = [
        send(
            gathered.at[0], gathered.at[s], g_send.at[s - 1], g_recv.at[s - 1], spot.ahead(s)
        )
        for s in range(1, ranks)
    ]
    gain_grad = jnp.sum(da2 * normed, axis=0, keepdims=True)
    line = lax.broadcasted_iota(jnp.int32, (LANES, model), 0)
    extra[...] = jnp.where(line == gain_row, gain_grad, dot_tn(d_logits, a2[...]))
    for copy in copies:
        copy.wait()


def rejoin(parts, gates, h, dz, router_t, a2, gain_row, plane_size):
    ranks = len(parts)
    dma = pltpu.SemaphoreType.DMA
    return pl.pallas_call(
        functools.partial(rejoin_kernel, ranks, plane_size, gain_row),
        in_specs=[VMEM] * (5 + ranks),
        out_specs=[VMEM] * 3,
        out_shape=[
            shape_of(h.shape, F32),
            shape_of((ranks,) + h.shape, BF16),
            shape_of((LANES, h.shape[1]), F32),
        ],
        scratch_shapes=[dma((ranks - 1,)), dma((ranks - 1,))],
        compiler_params=remote(2),
        name="rejoin",
    )(gates, h, dz, router_t, a2, *parts)


def last_kernel(ranks, plane_size, x, dh, gain, d_weights, d_rows, *refs):
    sums = refs[:ranks]
    out, columns_out, rows_out = refs[ranks : ranks + 3]
    (got, core_w, core_r, sum_w, sum_r, chip_w, chip_r, final) = refs[ranks + 3 : ranks + 11]
    r_send, r_recv, c_send, c_recv, p_send, p_recv, z_send, z_recv, local = refs[ranks + 11 :]
    spot = Spot(ranks, plane_size)
    chips, core, me = spot.chips, spot.core, spot.rank
    meet(
        [spot.ahead(s) for s in range(1, ranks)]
        + [spot.on_chip(spot.chip_ahead(k)) for k in range(1, chips)]
        + [spot.partner()]
    )
    z_copies = scatter_start(spot, sums, got, r_send, r_recv)
    pairs = ((0, d_weights, core_w, sum_w, chip_w), (1, d_rows, core_r, sum_r, chip_r))
    across = {}
    for k in range(chips):
        at = spot.chip_ahead(k)
        for which, src, buf, _, _ in pairs:
            across[k, which] = send(
                src.at[at, 1 - core],
                buf.at[k],
                c_send.at[which, k],
                c_recv.at[which, k],
                spot.partner(),
            )
    for k in list(range(1, chips)) + [0]:
        at = spot.chip_ahead(k)
        for which, src, buf, total, _ in pairs:
            across[k, which].wait()
            total[k] = (src[at, core].astype(F32) + buf[k].astype(F32)).astype(BF16)
    hops = {}
    for k in range(1, chips):
        for which, _, _, total, buf in pairs:
            hops[k, which] = send(
                total.at[k],
                buf.at[k - 1],
                p_send.at[which, k - 1],
                p_recv.at[which, k - 1],
                spot.on_chip(spot.chip_ahead(k)),
            )
    value = x[...]
    scale = lax.rsqrt(jnp.mean(value * value, axis=-1, keepdims=True) + EPSILON)
    normed = value * scale
    total = sums[0][...]
    for s in range(1, ranks):
        z_copies[s - 1].wait()
        total = total + got[s - 1].astype(F32)
    weighted = total * gain[...]
    grad = scale * (weighted - normed * jnp.mean(weighted * normed, axis=-1, keepdims=True))
    for k in range(1, chips):
        for which in range(2):
            hops[k, which].wait()
    value = sum_w[0].astype(F32)
    for k in range(1, chips):
        value = value + chip_w[k - 1].astype(F32)
    final[...] = value.astype(BF16)
    out[...] = dh[...] + grad
    value = sum_r[0].astype(F32)
    for k in range(1, chips):
        value = value + chip_r[k - 1].astype(F32)
    rows_out[...] = value
    kept = pltpu.make_async_copy(final.at[me], columns_out.at[me], local.at[0])
    kept.start()
    copies = [
        send(
            final.at[lax.rem(me + s, ranks)],
            columns_out.at[me],
            z_send.at[s - 1],
            z_recv.at[s - 1],
            spot.ahead(s),
        )
        for s in range(1, ranks)
    ]
    for copy in copies:
        copy.wait()
    kept.wait()


def last(x, dh, gain, d_weights, d_rows, sums):
    ranks = len(sums)
    chips, _, _, rows, columns = d_weights.shape
    dma = pltpu.SemaphoreType.DMA
    w_shape, r_shape = d_weights.shape[2:], d_rows.shape[2:]
    return pl.pallas_call(
        functools.partial(last_kernel, ranks, 2 * chips),
        in_specs=[VMEM] * (5 + ranks),
        out_specs=[VMEM] * 3,
        out_shape=[shape_of(x.shape, F32), shape_of(w_shape, BF16), shape_of(r_shape, F32)],
        scratch_shapes=[
            pltpu.VMEM((ranks - 1,) + x.shape, BF16),
            pltpu.VMEM((chips,) + w_shape, BF16),
            pltpu.VMEM((chips,) + r_shape, BF16),
            pltpu.VMEM((chips,) + w_shape, BF16),
            pltpu.VMEM((chips,) + r_shape, BF16),
            pltpu.VMEM((chips - 1,) + w_shape, BF16),
            pltpu.VMEM((chips - 1,) + r_shape, BF16),
            pltpu.VMEM(w_shape, BF16),
            dma((ranks - 1,)),
            dma((ranks - 1,)),
            dma((2, chips)),
            dma((2, chips)),
            dma((2, chips - 1)),
            dma((2, chips - 1)),
            dma((ranks - 1,)),
            dma((ranks - 1,)),
            dma((1,)),
        ],
        compiler_params=remote(3),
        name="last",
    )(x, dh, gain, d_weights, d_rows, *sums)


def piece_ids(position_index, starts):
    inside = (position_index[:, None] >= starts[None, :]) & (
        position_index[:, None] < starts[None, :] + PIECE
    )
    labels = jnp.arange(1, starts.shape[0] + 1, dtype=jnp.int32)[None, :]
    return jnp.sum(jnp.where(inside, labels, 0), axis=1, dtype=jnp.int32)


def on_device(
    inputs,
    cotangent,
    norm1_gain,
    w_query,
    key_projection,
    value_projection,
    w_output,
    norm2_gain,
    w_router,
    w_gate,
    w_up,
    w_down,
    routes,
    piece_starts,
):
    plane = Plane()
    ranks = lax.axis_size("expert")
    me = lax.axis_index("expert")
    rows, model = inputs.shape
    seq = rows * ranks
    weight_rows = w_query.shape[0]
    n_experts = w_router.shape[1]
    ff = w_gate.shape[2]
    kv_heads = KEY_VALUE_HEADS // ranks
    q_cols, kv_cols = kv_heads * GROUP * HEAD_WIDTH, kv_heads * HEAD_WIDTH
    rope_width = q_cols + kv_cols
    value_width = -(-kv_cols // LANES) * LANES
    columns = rope_width + value_width + LANES
    gain_one_row, gain_two_row = n_experts, n_experts + 1

    scale_one = lax.rsqrt(jnp.mean(inputs * inputs, axis=-1, keepdims=True) + EPSILON)
    x_blocks = expert_gather((inputs * scale_one).astype(BF16))

    extra_cols = jnp.concatenate(
        [
            w_router,
            norm1_gain[:, None],
            norm2_gain[:, None],
            jnp.zeros((weight_rows, LANES - n_experts - 2), F32),
        ],
        axis=1,
    )
    by_rank = jnp.concatenate(
        [
            w_query.reshape(weight_rows, ranks, q_cols),
            key_projection.reshape(weight_rows, ranks, kv_cols),
            jnp.pad(
                value_projection.reshape(weight_rows, ranks, kv_cols),
                ((0, 0), (0, 0), (0, value_width - kv_cols)),
            ),
            jnp.broadcast_to(extra_cols[:, None, :], (weight_rows, ranks, LANES)),
        ],
        axis=2,
    ).astype(BF16)
    by_rank = jnp.transpose(by_rank, (1, 0, 2))

    axes = ("fsdp", "expert")
    total = plane.size * ranks
    move = [
        (j, (j % plane.size) * ranks + j // plane.size) for j in range(total)
    ]
    out_shard = lax.ppermute(w_output.astype(BF16), axes, move)

    lane_ids = jnp.arange(LANES, dtype=jnp.int32)
    routed = jnp.sum((routes[:, :, None] == lane_ids[None, None, :]).astype(F32), axis=1)
    grads = jnp.concatenate(
        expert_gather(jnp.concatenate([cotangent, routed], axis=1).astype(BF16)), axis=0
    )

    core = plane.core.astype(jnp.int32)[None]
    keep, send, halves = pack_experts(core, w_gate, w_up, w_down, plane.size)
    got = plane.other_core(send)
    parts = [
        jnp.concatenate([jnp.where(plane.core == part, keep, got), halves[part][None]], axis=0)
        for part in range(2)
    ]
    found = {(0, 0, 0): parts[0], (0, 0, 1): parts[1]}
    found[0, 1, 0] = plane.other_mid(parts[0])
    for s in range(1, plane.rows):
        found[s, 0, 1] = plane.next_row(parts[1], s)
        for mid in range(2):
            found[s, mid, 0] = plane.next_row(found[0, mid, 0], s)
    for s in range(plane.rows):
        found[s, 1, 1] = plane.other_mid(found[s, 0, 1])
    place, pieces = tuple(found.keys()), list(found.values())
    sources = [
        ((plane.row - s) % plane.rows) * 2 + (plane.mid + mid) % 2
        for s in range(plane.rows)
        for mid in range(2)
    ]
    where = jnp.stack([me] + sources).astype(jnp.int32)

    by_rank, parts, out_shard = lax.optimization_barrier((by_rank, parts, out_shard))
    weights, out_weights = gather_weights(by_rank, out_shard, plane.size)
    weights = weights.reshape(model, columns)
    out_weights = out_weights.reshape(q_cols, model)

    block_ids = jnp.arange(seq, dtype=jnp.int32) // rows
    places = ((me - block_ids) % ranks) * rows + jnp.arange(seq, dtype=jnp.int32) % rows
    ids = piece_ids(places, piece_starts[0])
    visible = (places[:, None] <= places[None, :]) | (
        (ids[:, None] == ids[None, :]) & (ids[None, :] > 0)
    )
    bias = jnp.where(visible, 0.0, NEG_FILL).astype(F32)
    half = HEAD_WIDTH // 2
    inverse = 10000.0 ** (-(jnp.arange(half, dtype=F32) * 2.0 / HEAD_WIDTH))
    angles = places.astype(F32)[:, None] * inverse[None, :]
    cosine = jnp.tile(jnp.cos(angles), (1, LANES // half))
    sine = jnp.tile(jnp.sin(angles), (1, LANES // half)) * jnp.where(
        lane_ids % HEAD_WIDTH < half, -1.0, 1.0
    )
    extra_t = weights[:, columns - LANES :].T
    gain_one = extra_t[gain_one_row : gain_one_row + 1].astype(F32)
    gain_two = extra_t[gain_two_row : gain_two_row + 1].astype(F32)
    kept, sums = attend(
        x_blocks, gain_one, weights, out_weights, bias, cosine, sine, kv_heads, rope_width
    )
    grads, sums = lax.optimization_barrier((grads, sums))
    mid_rows, a2, own_a2, other_a2 = middle(inputs, gain_two, sums, plane.size)

    other_grads = plane.other_core(grads)
    other_out, other_dx, _, *other_kept = experts(
        [other_a2.reshape(seq, model)], other_grads, extra_t, where, pieces, place, BF16
    )
    out_all, dx_all, gates, *own_kept = experts(
        [own_a2.reshape(seq, model)], grads, extra_t, where, pieces, place, F32
    )
    dx_all = dx_all + plane.other_core(other_dx).astype(F32)
    dxs = [
        dx_all[b * rows : (b + 1) * rows].astype(F32 if b == 0 else BF16) for b in range(ranks)
    ]
    dx_got = expert_scatter(dxs)
    order = [(s, mid) for s in reversed(range(plane.rows)) for mid in (1, 0)]
    chips = [
        ((plane.row + s) % plane.rows) * 2 + (plane.mid + mid) % 2 for s, mid in order
    ]
    own_kept.insert(2, grads[:, :model])
    other_kept.insert(2, other_grads[:, :model])
    flat = expert_grads(
        jnp.stack(chips).astype(jnp.int32), own_kept, other_kept, plane.size
    )
    dx_got, flat = lax.optimization_barrier((dx_got, flat))
    summed = {
        (s, mid, part): flat[2 * i + part]
        for i, (s, mid) in enumerate(order)
        for part in range(2)
    }

    def add(first, *others):
        value = first.astype(F32)
        for v in others:
            value = value + v.astype(F32)
        return value.astype(BF16)

    steps = range(1, plane.rows)
    a_sums = [
        add(summed[0, mid, 0], *[plane.next_row(summed[s, mid, 0], s) for s in steps])
        for mid in range(2)
    ]
    b_sums = [
        add(summed[s, 0, 1], plane.other_mid(summed[s, 1, 1])) for s in range(plane.rows)
    ]
    a_got = plane.other_mid(a_sums[1])
    b_got = [plane.next_row(b_sums[s], s) for s in steps]
    b_kept = b_sums[0]
    if len(b_got) > 1:
        b_kept = add(b_kept, *b_got[:-1])
    b_got = b_got[-1]
    other = plane.other_core(
        jnp.where(
            plane.core == 0,
            b_kept[:2].astype(F32) + b_got[:2].astype(F32),
            a_sums[0][:2].astype(F32) + a_got[:2].astype(F32),
        ).astype(BF16)
    )
    gate_grad, up_grad, down_grad = finish(
        core, a_sums[0], a_got, b_kept, b_got, other, w_down.shape[1], model, plane.size
    )

    dh, dh_stack, extra = rejoin(
        [dxs[0]] + dx_got, gates, mid_rows, cotangent, extra_t, a2, gain_two_row, plane.size
    )

    d_weights, d_out_weights, da1 = attend_back(
        dh_stack,
        x_blocks,
        weights,
        out_weights,
        kept,
        bias,
        cosine,
        sine,
        extra,
        kv_heads,
        gain_one_row,
    )
    chip_count = plane.size // 2
    input_grad, by_rank, out_part = last(
        inputs,
        dh,
        gain_one,
        d_weights.reshape(chip_count, 2, ranks, weight_rows, columns),
        d_out_weights.reshape(chip_count, 2, weight_rows, model),
        da1,
    )
    out_all = out_all + plane.other_core(other_out).astype(F32)
    outs = [out_all[b * rows : (b + 1) * rows] for b in range(ranks)]
    output = mid_rows + outs[0]
    for v in expert_scatter([v.astype(BF16) for v in outs]):
        output = output + v.astype(F32)

    w_output_grad = lax.ppermute(
        out_part.astype(BF16), axes, [(b, a) for a, b in move]
    ).astype(F32)
    by_rank = by_rank.astype(F32)

    def columns_of(start, width):
        piece = by_rank[:, :, start : start + width]
        return jnp.transpose(piece, (1, 0, 2)).reshape(weight_rows, ranks * width)

    extra_grad = jnp.sum(by_rank[:, :, columns - LANES :], axis=0)
    return (
        output,
        input_grad,
        extra_grad[:, gain_one_row],
        columns_of(0, q_cols),
        columns_of(q_cols, kv_cols),
        columns_of(rope_width, kv_cols),
        w_output_grad,
        extra_grad[:, gain_two_row],
        extra_grad[:, :n_experts],
        gate_grad,
        up_grad,
        down_grad,
    )


def solution(mesh):
    both = ("fsdp", "expert")
    rows, flat, stack = P(both, None), P(both), P("expert", "fsdp", None)
    weights = (flat, rows, rows, rows, rows, flat, rows, stack, stack, stack)
    return jax.shard_map(
        on_device,
        mesh=mesh,
        in_specs=(rows, rows) + weights + (rows, P("fsdp", None)),
        out_specs=(rows, rows) + weights,
        check_vma=False,
    )
```

```python
import functools

import jax
import jax.numpy as jnp
from jax import lax
from jax.experimental import pallas as pl
from jax.experimental.pallas import tpu as pltpu
from jax.sharding import PartitionSpec as P

QUERY_HEADS = 24
KEY_VALUE_HEADS = 8
GROUP = QUERY_HEADS // KEY_VALUE_HEADS
HEAD_WIDTH = 64
PIECE = 256
LANES = 128
DEVICE_ROWS = 128
EPSILON = 1e-05
NEG_FILL = -1e30
SCORE_SCALE = HEAD_WIDTH ** (-0.5)
F32 = jnp.float32
BF16 = jnp.bfloat16

VMEM = pl.BlockSpec(memory_space=pltpu.VMEM)
SMEM = pl.BlockSpec(memory_space=pltpu.SMEM)
ANY = pl.BlockSpec(memory_space=pl.ANY)
MESH = pl.DeviceIdType.MESH


def dot(a, b):
    return lax.dot_general(a, b, (((1,), (0,)), ((), ())), preferred_element_type=F32)


def dot_nt(a, b):
    return lax.dot_general(a, b, (((1,), (1,)), ((), ())), preferred_element_type=F32)


def dot_tn(a, b):
    return lax.dot_general(a, b, (((0,), (0,)), ((), ())), preferred_element_type=F32)


def shape_of(dims, dtype):
    return jax.ShapeDtypeStruct(tuple(dims), dtype)


def params(**kw):
    return pltpu.CompilerParams(vmem_limit_bytes=60 * 1024 * 1024, **kw)


class Plane:
    def __init__(self):
        self.size = lax.axis_size("fsdp")
        self.rows = self.size // 4
        index = lax.axis_index("fsdp")
        self.index = index
        self.core = index % 2
        self.mid = (index // 2) % 2
        self.row = index // 4

    def other_core(self, x):
        return lax.ppermute(x, "fsdp", [(i, i ^ 1) for i in range(self.size)])

    def other_mid(self, x):
        return lax.ppermute(x, "fsdp", [(i, i ^ 2) for i in range(self.size)])

    def next_row(self, x, step):
        return lax.ppermute(
            x, "fsdp", [(i, (i // 4 + step) % self.rows * 4 + i % 4) for i in range(self.size)]
        )


def expert_shift(x, step):
    count = lax.axis_size("expert")
    return lax.ppermute(x, "expert", [(i, (i + step) % count) for i in range(count)])


def expert_scatter(blocks):
    count = lax.axis_size("expert")
    return [expert_shift(blocks[s], count - s) for s in range(1, count)]


def chooser(width, blocks, part, dtype=BF16):
    n = width // blocks
    line = lax.broadcasted_iota(jnp.int32, (width // 2, width), 0)
    column = lax.broadcasted_iota(jnp.int32, (width // 2, width), 1)
    want = (2 * (line // n) + part) * n + line % n
    return jnp.where(column == want, 1.0, 0.0).astype(dtype)


def pack_kernel(blocks, core, gate, up, down, keep, send, halves):
    width = gate.shape[2]
    mine = chooser(width, blocks, core[0])
    theirs = chooser(width, blocks, 1 - core[0])
    for place, ref in ((0, gate), (1, up)):
        value = ref[0].astype(BF16)
        keep[place, 0] = dot_nt(value, mine).astype(BF16)
        send[place, 0] = dot_nt(value, theirs).astype(BF16)
    value = down[0].astype(BF16)
    rows, wide = value.shape[0] // 2, width // 2
    for part in range(2):
        for j in range(value.shape[1] // wide):
            halves[part, 0, j * rows : (j + 1) * rows] = value[
                part * rows : (part + 1) * rows, j * wide : (j + 1) * wide
            ]


def pack_experts(core, w_gate, w_up, w_down, blocks):
    local, depth, width = w_gate.shape
    out = shape_of((2, local, depth, width // 2), BF16)
    block = pl.BlockSpec((2, 1, depth, width // 2), lambda e: (0, e, 0, 0))
    return pl.pallas_call(
        functools.partial(pack_kernel, blocks),
        grid=(local,),
        in_specs=[SMEM]
        + [pl.BlockSpec((1,) + w.shape[1:], lambda e: (e, 0, 0)) for w in (w_gate, w_up, w_down)],
        out_specs=[block] * 3,
        out_shape=[out] * 3,
        name="pack_experts",
    )(core, w_gate, w_up, w_down)


def swap_halves(x):
    lane = lax.broadcasted_iota(jnp.int32, x.shape, 1)
    return jnp.where(
        lane % HEAD_WIDTH < HEAD_WIDTH // 2, pltpu.roll(x, LANES - 32, 1), pltpu.roll(x, 32, 1)
    )


def head_slice(ref, start):
    return ref[:, start : start + HEAD_WIDTH]


def experts_kernel(blocks, pieces, place, row_block, *refs):
    a2_in = refs[:blocks]
    grads_in, router_t, where_ref = refs[blocks : blocks + 3]
    piece_refs = refs[blocks + 3 : blocks + 3 + pieces]
    (out_all, dx_all, gates_out, a2_t, hidden_t, d_gate, d_up) = refs[
        blocks + 3 + pieces : blocks + 10 + pieces
    ]
    (a2, gate_w, up_w, down_w, out_sum, dx_sum, gates, dgates, in_sem, w_sem) = refs[
        blocks + 10 + pieces :
    ]
    step, steps = pl.program_id(0), pl.num_programs(0)
    rows = a2_in[0].shape[0]
    seq, model = a2.shape
    depth, width = piece_refs[0].shape[2], gate_w.shape[2]
    down_rows = depth * width // model
    slot = lax.rem(step, 2)

    def fetch(e, to):
        for i, (row_step, mid, part) in enumerate(place):
            source = where_ref[1 + row_step * 2 + mid] * 2 + part
            at = pl.multiple_of(source * depth, 32)
            for which, buf in ((0, gate_w), (1, up_w)):
                pltpu.make_async_copy(
                    piece_refs[i].at[which, e], buf.at[to, pl.ds(at, depth)], w_sem.at[which, to]
                ).start()
            at = pl.multiple_of(source * down_rows, 16)
            for j in range(model // width):
                pltpu.make_async_copy(
                    piece_refs[i].at[2, e, pl.ds(j * down_rows, down_rows)],
                    down_w.at[to, pl.ds(at, down_rows), pl.ds(j * width, width)],
                    w_sem.at[2, to],
                ).start()

    @pl.when(step == 0)
    def _():
        for b in range(blocks):
            pltpu.make_async_copy(
                a2_in[b], a2.at[pl.ds(b * rows, rows)], in_sem.at[0]
            ).start()
        fetch(0, 0)
        pltpu.make_async_copy(a2, a2, in_sem.at[0]).wait()
        logits = dot_nt(a2[...], router_t[...])
        routed = grads_in[:, model:].astype(F32) > 0.5
        top = jnp.max(jnp.where(routed, logits, NEG_FILL), axis=1, keepdims=True)
        weight = jnp.where(routed, jnp.exp(jnp.where(routed, logits, top) - top), 0.0)
        gates[...] = weight / jnp.sum(weight, axis=1, keepdims=True)
        gates_out[...] = gates[: gates_out.shape[0], :]
        dgates[...] = jnp.zeros_like(dgates)
        a2_t[...] = a2[...].T

    @pl.when(step + 1 < steps)
    def _():
        fetch(step + 1, 1 - slot)

    for which, buf in ((0, gate_w), (1, up_w), (2, down_w)):
        pltpu.make_async_copy(buf.at[slot], buf.at[slot], w_sem.at[which, slot]).wait()

    mine = where_ref[0] * steps + step

    def block(i, carry):
        at = pl.ds(pl.multiple_of(i * row_block, row_block), row_block)
        left = a2[at, :]
        gate_lin = dot(left, gate_w[slot])
        up_lin = dot(left, up_w[slot])
        back = dot_nt(grads_in[at, :model], down_w[slot])
        lane = lax.broadcasted_iota(jnp.int32, (row_block, LANES), 1)
        here = lane == mine
        gate = jnp.sum(jnp.where(here, gates[at, :], 0.0), axis=1, keepdims=True)
        sig = 1.0 / (1.0 + jnp.exp(-gate_lin))
        silu = gate_lin * sig
        hidden = silu * up_lin
        dgates[at, :] += jnp.where(here, jnp.sum(hidden * back, axis=1, keepdims=True), 0.0)
        hidden_low = (hidden * gate).astype(BF16)
        d_hidden = back * gate
        d_gate_low = (d_hidden * up_lin * (sig + silu * (1.0 - sig))).astype(BF16)
        d_up_low = (d_hidden * silu).astype(BF16)
        d_gate[at, :] = d_gate_low
        d_up[at, :] = d_up_low
        hidden_t[0, :, at] = hidden_low.T
        out_new = dot(hidden_low, down_w[slot])
        dx_new = dot_nt(d_gate_low, gate_w[slot]) + dot_nt(d_up_low, up_w[slot])

        @pl.when(step == 0)
        def _():
            out_sum[at, :] = out_new
            dx_sum[at, :] = dx_new

        @pl.when(step > 0)
        def _():
            out_sum[at, :] += out_new
            dx_sum[at, :] += dx_new

        return carry

    lax.fori_loop(0, seq // row_block, block, 0)

    @pl.when(step == steps - 1)
    def _():
        high = dgates[...].astype(BF16).astype(F32)
        low = dgates[...] - high
        lane = lax.broadcasted_iota(jnp.int32, high.shape, 1)
        tail = jnp.where(lane < LANES // 2, high, pltpu.roll(low, LANES // 2, 1))
        out_all[...] = out_sum[...].astype(out_all.dtype)
        dx_all[:, :model] = dx_sum[...].astype(dx_all.dtype)
        dx_all[:, model:] = tail.astype(dx_all.dtype)


def experts(a2_blocks, grads, router_t, where, pieces, place, dtype):
    blocks = len(a2_blocks)
    rows, model = a2_blocks[0].shape
    seq = rows * blocks
    local, depth, width = pieces[0].shape[1:]
    outs = [
        shape_of((seq, model), dtype),
        shape_of((seq, model + LANES), dtype),
        shape_of((DEVICE_ROWS, LANES), F32),
        shape_of((model, seq), BF16),
        shape_of((local, width, seq), BF16),
        shape_of((seq, local * width), BF16),
        shape_of((seq, local * width), BF16),
    ]
    whole = lambda dims: pl.BlockSpec(
        dims, lambda e: (0,) * len(dims), pipeline_mode=pl.Buffered(1)
    )
    out_specs = (
        [whole(o.shape) for o in outs[:4]]
        + [pl.BlockSpec((1, width, seq), lambda e: (e, 0, 0))]
        + [pl.BlockSpec((seq, width), lambda e: (0, e))] * 2
    )
    return pl.pallas_call(
        functools.partial(experts_kernel, blocks, len(pieces), place, 256),
        grid=(local,),
        in_specs=[ANY] * blocks
        + [whole(grads.shape), whole(router_t.shape), SMEM]
        + [ANY] * len(pieces),
        out_specs=out_specs,
        out_shape=outs,
        scratch_shapes=[
            pltpu.VMEM((seq, model), BF16),
            pltpu.VMEM((2, model, width), BF16),
            pltpu.VMEM((2, model, width), BF16),
            pltpu.VMEM((2, width, model), BF16),
            pltpu.VMEM((seq, model), F32),
            pltpu.VMEM((seq, model), F32),
            pltpu.VMEM((seq, LANES), F32),
            pltpu.VMEM((seq, LANES), F32),
            pltpu.SemaphoreType.DMA((1,)),
            pltpu.SemaphoreType.DMA((3, 2)),
        ],
        compiler_params=params(dimension_semantics=("arbitrary",)),
        name="experts",
    )(*a2_blocks, grads, router_t, where, *pieces)


def expert_grads_kernel(chips, depth, down_rows, where_ref, *refs):
    (a2_t0, a2_t1, hid0, hid1, grads0, grads1, dg0, dg1, du0, du1) = refs[:10]
    outs, down_sum = refs[10 : 10 + 2 * chips], refs[10 + 2 * chips]
    model, width = a2_t0.shape[0], dg0.shape[1]
    down_sum[...] = (dot(hid0[0], grads0[...]) + dot(hid1[0], grads1[...])).astype(BF16)
    for place in range(chips):
        source = where_ref[place]
        at = pl.ds(pl.multiple_of(source * 2 * depth, 32), 2 * depth)
        left0, left1 = a2_t0[at, :], a2_t1[at, :]
        gate = (dot(left0, dg0[...]) + dot(left1, dg1[...])).astype(BF16)
        up = (dot(left0, du0[...]) + dot(left1, du1[...])).astype(BF16)
        for part in range(2):
            out = outs[2 * place + part]
            out[0, 0] = gate[part * depth : (part + 1) * depth]
            out[1, 0] = up[part * depth : (part + 1) * depth]
            at = pl.ds(pl.multiple_of((source * 2 + part) * down_rows, 16), down_rows)
            down = down_sum[at, :]
            for j in range(model // width):
                out[2, 0, j * down_rows : (j + 1) * down_rows, :] = down[
                    :, j * width : (j + 1) * width
                ]


def expert_grads(where, first, second, plane_size):
    model, seq = first[0].shape
    local, width = first[1].shape[:2]
    chips = plane_size // 2
    depth, down_rows = model // plane_size, width // plane_size
    out = shape_of((3, local, depth, width), BF16)
    block = pl.BlockSpec((3, 1, depth, width), lambda e: (0, e, 0, 0))
    once = lambda dims: pl.BlockSpec(dims, lambda e: (0, 0), pipeline_mode=pl.Buffered(1))
    specs = [
        once((model, seq)),
        pl.BlockSpec((1, width, seq), lambda e: (e, 0, 0)),
        once((seq, model)),
        pl.BlockSpec((seq, width), lambda e: (0, e)),
        pl.BlockSpec((seq, width), lambda e: (0, e)),
    ]
    operands = [v for pair in zip(first, second) for v in pair]
    return pl.pallas_call(
        functools.partial(expert_grads_kernel, chips, depth, down_rows),
        grid=(local,),
        in_specs=[SMEM] + [spec for spec in specs for _ in range(2)],
        out_specs=[block] * (2 * chips),
        out_shape=[out] * (2 * chips),
        scratch_shapes=[pltpu.VMEM((width, model), BF16)],
        compiler_params=params(),
        name="expert_grads",
    )(where, *operands)


def finish_kernel(blocks, core, kept_a, got_a, kept_b, got_b, other, gate, up, down):
    width, wide = gate.shape[2], kept_a.shape[3]
    mine = chooser(width, blocks, core[0])
    theirs = chooser(width, blocks, 1 - core[0])
    first = core[0] == 0
    for place, out in ((0, gate), (1, up)):
        kept = jnp.where(first, kept_a[place, 0].astype(F32), kept_b[place, 0].astype(F32))
        got = jnp.where(first, got_a[place, 0].astype(F32), got_b[place, 0].astype(F32))
        out[0] = (
            dot(kept.astype(BF16), mine)
            + dot(got.astype(BF16), mine)
            + dot(other[place, 0], theirs)
        )
    rows = down.shape[1] // 2
    for part, kept, got in ((0, kept_a, got_a), (1, kept_b, got_b)):
        value = kept[2, 0].astype(F32) + got[2, 0].astype(F32)
        for j in range(value.shape[0] // rows):
            down[0, part * rows : (part + 1) * rows, j * wide : (j + 1) * wide] = value[
                j * rows : (j + 1) * rows
            ]


def finish(core, kept_a, got_a, kept_b, got_b, other, down_rows, model, blocks):
    local, depth, wide = kept_a.shape[1:]
    block = pl.BlockSpec((3, 1, depth, wide), lambda e: (0, e, 0, 0))
    outs = [
        shape_of((local, depth, 2 * wide), F32),
        shape_of((local, depth, 2 * wide), F32),
        shape_of((local, down_rows, model), F32),
    ]
    return pl.pallas_call(
        functools.partial(finish_kernel, blocks),
        grid=(local,),
        in_specs=[SMEM]
        + [block] * 4
        + [pl.BlockSpec((2, 1, depth, wide), lambda e: (0, e, 0, 0))],
        out_specs=[pl.BlockSpec((1,) + o.shape[1:], lambda e: (e, 0, 0)) for o in outs],
        out_shape=outs,
        name="finish",
    )(core, kept_a, got_a, kept_b, got_b, other)


def attend_back_kernel(blocks, kv_heads, gain_row, *refs):
    dh_ref, x_all = refs[:2]
    (weights, out_weights, a1, qk, val, mixed, maxes, inverse, bias, cosine, sine, extra) = refs[2:14]
    d_weights, d_out_weights = refs[14:16]
    sums = refs[16 : blocks + 16]
    grads, d_mixed, dq_t, d_qk, d_lin = refs[blocks + 16 :]
    rows = x_all.shape[1]
    rope_width, value_width = qk.shape[1], val.shape[1]
    q_width = kv_heads * GROUP * HEAD_WIDTH
    for b in range(blocks):
        grads[b * rows : (b + 1) * rows, :] = dh_ref[b]
    d_mixed[...] = dot_nt(grads[...], out_weights[...]).astype(BF16)
    d_out_weights[...] = dot_tn(mixed[...], grads[...]).astype(BF16)
    if value_width > kv_heads * HEAD_WIDTH:
        d_lin[:, rope_width:] = jnp.zeros((d_lin.shape[0], value_width), BF16)
    for g in range(kv_heads):
        key = head_slice(qk, q_width + g * HEAD_WIDTH)
        key_t = key.T
        value = head_slice(val, g * HEAD_WIDTH)
        d_key, d_value = None, None
        for j in range(GROUP):
            h = g * GROUP + j
            query = head_slice(qk, h * HEAD_WIDTH)
            grad = head_slice(d_mixed, h * HEAD_WIDTH)
            scores = dot_nt(key, query) * SCORE_SCALE + bias[...]
            prob = jnp.exp(scores - maxes[h : h + 1, :]) * inverse[h : h + 1, :]
            d_prob = dot_nt(value, grad)
            inner = jnp.sum(prob * d_prob, axis=0, keepdims=True)
            d_scores = (prob * (d_prob - inner)).astype(BF16)
            dk = dot(d_scores, query)
            dv = dot(prob.astype(BF16), grad)
            d_key = dk if d_key is None else d_key + dk
            d_value = dv if d_value is None else d_value + dv
            dq_t[h * HEAD_WIDTH : (h + 1) * HEAD_WIDTH, :] = dot(key_t, d_scores)
        start = q_width + g * HEAD_WIDTH
        d_qk[:, start : start + HEAD_WIDTH] = d_key * SCORE_SCALE
        start = rope_width + g * HEAD_WIDTH
        d_lin[:, start : start + HEAD_WIDTH] = d_value.astype(BF16)
    d_qk[:, :q_width] = dq_t[...].T * SCORE_SCALE
    for c in range(rope_width // LANES):
        at = slice(c * LANES, (c + 1) * LANES)
        x = d_qk[:, at]
        d_lin[:, at] = (x * cosine[...] - swap_halves(x) * sine[...]).astype(BF16)
    total = dot_nt(d_lin[...], weights[:, : rope_width + value_width])
    gain_grad = None
    for b in range(blocks):
        part = total[b * rows : (b + 1) * rows, :]
        sums[b][...] = part.astype(sums[b].dtype)
        new = jnp.sum(part * x_all[b].astype(F32), axis=0, keepdims=True)
        gain_grad = new if gain_grad is None else gain_grad + new
    d_weights[:, : rope_width + value_width] = dot_tn(a1[...], d_lin[...]).astype(BF16)
    line = lax.broadcasted_iota(jnp.int32, extra.shape, 0)
    tail = jnp.where(line == gain_row, gain_grad, extra[...])
    d_weights[:, rope_width + value_width :] = tail.T.astype(BF16)


def attend_back(
    dh_stack, x_all, weights, out_weights, kept, bias, cosine, sine, extra, kv_heads, gain_row
):
    blocks, rows, model = dh_stack.shape
    seq = rows * blocks
    q_width = out_weights.shape[0]
    rope_width, value_width = kept[1].shape[1], kept[2].shape[1]
    outs = [shape_of(weights.shape, BF16), shape_of(out_weights.shape, BF16)] + [
        shape_of((rows, model), F32 if b == 0 else BF16) for b in range(blocks)
    ]
    out = pl.pallas_call(
        functools.partial(attend_back_kernel, blocks, kv_heads, gain_row),
        in_specs=[VMEM] * 14,
        out_specs=[VMEM] * len(outs),
        out_shape=outs,
        scratch_shapes=[
            pltpu.VMEM((seq, model), BF16),
            pltpu.VMEM((seq, q_width), BF16),
            pltpu.VMEM((q_width, seq), F32),
            pltpu.VMEM((seq, rope_width), F32),
            pltpu.VMEM((seq, rope_width + value_width), BF16),
        ],
        compiler_params=params(),
        name="attend_back",
    )(dh_stack, x_all, weights, out_weights, *kept, bias, cosine, sine, extra)
    return out[0], out[1], out[2:]


class Spot:
    def __init__(self, ranks, plane_size):
        self.ranks, self.chips = ranks, plane_size // 2
        self.rank = lax.axis_index("expert")
        self.index = lax.axis_index("fsdp")
        self.chip = self.index // 2
        self.core = self.index % 2

    def behind(self, s):
        return {"expert": lax.rem(self.rank - s + self.ranks, self.ranks)}

    def ahead(self, s):
        return {"expert": lax.rem(self.rank + s, self.ranks)}

    def partner(self):
        return {"fsdp": self.chip * 2 + (1 - self.core)}

    def chip_ahead(self, k):
        return lax.rem(self.chip + k, self.chips)

    def chip_behind(self, k):
        return lax.rem(self.chip - k + self.chips, self.chips)

    def on_chip(self, chip):
        return {"fsdp": chip * 2 + self.core}


def greet(peers):
    barrier = pltpu.get_barrier_semaphore()
    for peer in peers:
        pl.semaphore_signal(barrier, inc=1, device_id=peer, device_id_type=MESH)


def await_peers(peers):
    pl.semaphore_wait(pltpu.get_barrier_semaphore(), len(peers))


def meet(peers):
    greet(peers)
    await_peers(peers)


def send(src, dst, send_sem, recv_sem, peer):
    copy = pltpu.make_async_remote_copy(
        src_ref=src,
        dst_ref=dst,
        send_sem=send_sem,
        recv_sem=recv_sem,
        device_id=peer,
        device_id_type=MESH,
    )
    copy.start()
    return copy


def remote(collective_id):
    return params(collective_id=collective_id, has_side_effects=True)


def gather_weights_kernel(
    ranks, plane_size, by_rank, rows_in, x_in, grads_in, weights, out_rows, x_all, grads_all, *sems
):
    z_send, z_recv, p_send, p_recv, c_send, c_recv, local = sems[:7]
    spot = Spot(ranks, plane_size)
    f, me, chips = spot.index, spot.rank, spot.chips
    others = range(1, ranks)
    meet(
        [spot.ahead(s) for s in others]
        + [spot.on_chip(spot.chip_ahead(k)) for k in range(1, chips)]
        + [spot.partner()]
    )
    waits = []
    z_copies = [
        send(
            by_rank.at[lax.rem(me + s, ranks)],
            weights.at[f, me],
            z_send.at[s - 1],
            z_recv.at[s - 1],
            spot.ahead(s),
        )
        for s in others
    ]
    kept = [
        pltpu.make_async_copy(by_rank.at[me], weights.at[f, me], local.at[0]),
        pltpu.make_async_copy(rows_in, out_rows.at[f], local.at[1]),
        pltpu.make_async_copy(x_in, x_all.at[0], local.at[2]),
        pltpu.make_async_copy(grads_in, grads_all.at[0], local.at[3]),
    ]
    for copy in kept:
        copy.start()
    lines = [
        LineGather(spot, x_all, sems[7], sems[8]),
        LineGather(spot, grads_all, sems[9], sems[10]),
    ]

    def spread(which, src, buf):
        return [
            send(
                src,
                buf.at[f],
                p_send.at[which, k - 1],
                p_recv.at[which, k - 1],
                spot.on_chip(spot.chip_ahead(k)),
            )
            for k in range(1, chips)
        ] + [send(src, buf.at[f], c_send.at[which, 0], c_recv.at[which, 0], spot.partner())]

    row_copies = spread(1, rows_in, out_rows)
    for copy in kept:
        copy.wait()
    lines[0].start(0)
    for copy in z_copies:
        copy.wait()
    weight_copies = spread(0, weights.at[f], weights)
    for hop in range(ranks - 1):
        lines[0].arrive(hop)
        if hop + 1 < ranks - 1:
            lines[0].start(hop + 1)
        else:
            lines[1].start(0)
    for k in range(1, chips):
        source = spot.chip_behind(k) * 2 + spot.core
        for which, copies, buf in ((1, row_copies, out_rows), (0, weight_copies, weights)):
            copies[k - 1].wait()
            waits.append(
                send(
                    buf.at[source],
                    buf.at[source],
                    c_send.at[which, k],
                    c_recv.at[which, k],
                    spot.partner(),
                )
            )
    for hop in range(ranks - 1):
        lines[1].arrive(hop)
        if hop + 1 < ranks - 1:
            lines[1].start(hop + 1)
    row_copies[-1].wait()
    weight_copies[-1].wait()
    for copy in waits:
        copy.wait()
    for line in lines:
        line.drain()


def gather_weights(by_rank, rows_in, x_in, grads_in, plane_size):
    ranks, rows, columns = by_rank.shape
    chips = plane_size // 2
    dma = pltpu.SemaphoreType.DMA
    return pl.pallas_call(
        functools.partial(gather_weights_kernel, ranks, plane_size),
        in_specs=[VMEM] * 4,
        out_specs=[VMEM] * 4,
        out_shape=[
            shape_of((plane_size, ranks, rows, columns), BF16),
            shape_of((plane_size,) + rows_in.shape, BF16),
            shape_of((ranks,) + x_in.shape, BF16),
            shape_of((ranks,) + grads_in.shape, BF16),
        ],
        scratch_shapes=[
            dma((ranks - 1,)),
            dma((ranks - 1,)),
            dma((2, chips - 1)),
            dma((2, chips - 1)),
            dma((2, chips)),
            dma((2, chips)),
            dma((4,)),
        ]
        + [dma((2, ranks - 1))] * 4,
        compiler_params=remote(0),
        name="gather_weights",
    )(by_rank, rows_in, x_in, grads_in)


def scatter_start(spot, refs, buf, send_sem, recv_sem):
    return [
        send(refs[s], buf.at[s - 1], send_sem.at[s - 1], recv_sem.at[s - 1], spot.behind(s))
        for s in range(1, spot.ranks)
    ]


class LineGather:
    def __init__(self, spot, buf, send_sem, recv_sem):
        self.spot, self.buf, self.sems = spot, buf, (send_sem, recv_sem)
        me, n = spot.rank, spot.ranks
        self.hops = n - 1
        self.sends = [(me - h >= 0) & (me + 1 < n) for h in range(n - 1)], [
            (me + h < n) & (me >= 1) for h in range(n - 1)
        ]
        self.gets = [me - 1 - h >= 0 for h in range(n - 1)], [
            me + 1 + h < n for h in range(n - 1)
        ]

    def slots(self, way, h):
        n = self.spot.ranks
        return (h, h + 1) if way == 0 else ((n - h) % n, n - h - 1)

    def copy(self, way, h):
        source, target = self.slots(way, h)
        return pltpu.make_async_remote_copy(
            src_ref=self.buf.at[source],
            dst_ref=self.buf.at[target],
            send_sem=self.sems[0].at[way, h],
            recv_sem=self.sems[1].at[way, h],
            device_id=self.spot.ahead(1) if way == 0 else self.spot.behind(1),
            device_id_type=MESH,
        )

    def start(self, h):
        for way in range(2):

            @pl.when(self.sends[way][h])
            def _():
                self.copy(way, h).start()

    def arrive(self, h):
        for way in range(2):

            @pl.when(self.gets[way][h])
            def _():
                self.copy(way, h).wait_recv()

    def passed(self, h, then):
        for way in range(2):

            @pl.when(self.gets[way][h])
            def _():
                then(self.slots(way, h)[1])

    def drain(self):
        for h in range(self.hops):
            for way in range(2):

                @pl.when(self.sends[way][h])
                def _():
                    self.copy(way, h).wait_send()


def attend_kernel(ranks, plane_size, kv_heads, *refs):
    x_all, gain, weights, out_weights, bias, cosine, sine, x, gain_two = refs[:9]
    (a1, qk, val, mixed, maxes, inverse, h_out, a2, gathered, other) = refs[9:19]
    mixed_t, sums, got, r_send, r_recv, g_send, g_recv, c_send, c_recv = refs[19:]
    spot = Spot(ranks, plane_size)
    peers = [spot.ahead(s) for s in range(1, ranks)] + [spot.partner()]
    greet(peers)
    rows = x_all.shape[1]
    rope_width = qk.shape[1]
    q_width = kv_heads * GROUP * HEAD_WIDTH
    for b in range(ranks):
        a1[b * rows : (b + 1) * rows, :] = (x_all[b].astype(F32) * gain[...]).astype(BF16)
    linear = dot(a1[...], weights[:, : rope_width + val.shape[1]])
    for c in range(rope_width // LANES):
        part = linear[:, c * LANES : (c + 1) * LANES]
        qk[:, c * LANES : (c + 1) * LANES] = (
            part * cosine[...] + swap_halves(part) * sine[...]
        ).astype(BF16)
    val[...] = linear[:, rope_width:].astype(BF16)
    for g in range(kv_heads):
        key = head_slice(qk, q_width + g * HEAD_WIDTH)
        value_t = head_slice(val, g * HEAD_WIDTH).T
        for j in range(GROUP):
            h = g * GROUP + j
            scores = dot_nt(key, head_slice(qk, h * HEAD_WIDTH)) * SCORE_SCALE + bias[...]
            top = jnp.max(scores, axis=0, keepdims=True)
            weight = jnp.exp(scores - top)
            inv = 1.0 / jnp.sum(weight, axis=0, keepdims=True)
            maxes[h : h + 1, :] = top
            inverse[h : h + 1, :] = inv
            mixed_t[h * HEAD_WIDTH : (h + 1) * HEAD_WIDTH, :] = dot(
                value_t, (weight * inv).astype(BF16)
            )
    mixed[...] = mixed_t[...].T.astype(BF16)
    await_peers(peers)
    total = dot(mixed[...], out_weights[...])
    for b in range(1, ranks):
        sums[b - 1] = total[b * rows : (b + 1) * rows, :].astype(BF16)
    copies = scatter_start(
        spot, [None] + [sums.at[s - 1] for s in range(1, ranks)], got, r_send, r_recv
    )
    total = x[...] + total[:rows, :]
    for s in range(1, ranks):
        copies[s - 1].wait()
        total = total + got[s - 1].astype(F32)
    scale = lax.rsqrt(jnp.mean(total * total, axis=-1, keepdims=True) + EPSILON)
    low = (total * scale * gain_two[...]).astype(BF16)
    gathered[0] = low
    line = LineGather(spot, gathered, g_send, g_recv)
    line.start(0)

    def across(s):
        return pltpu.make_async_remote_copy(
            src_ref=gathered.at[s],
            dst_ref=other.at[s],
            send_sem=c_send.at[s],
            recv_sem=c_recv.at[s],
            device_id=spot.partner(),
            device_id_type=MESH,
        )

    across(0).start()
    a2[...] = low
    h_out[...] = total
    for hop in range(line.hops):
        line.arrive(hop)
        if hop + 1 < line.hops:
            line.start(hop + 1)
        line.passed(hop, lambda s: across(s).start())
    line.drain()
    for s in range(ranks):
        across(s).wait()


def attend(
    x_all, gain, weights, out_weights, bias, cosine, sine, x, gain_two, kv_heads, rope_width,
    plane_size,
):
    ranks, rows, model = x_all.shape
    seq = rows * ranks
    q_width = kv_heads * GROUP * HEAD_WIDTH
    value_width = weights.shape[1] - LANES - rope_width
    heads = kv_heads * GROUP
    stack = shape_of((ranks, rows, model), BF16)
    outs = [
        shape_of((seq, model), BF16),
        shape_of((seq, rope_width), BF16),
        shape_of((seq, value_width), BF16),
        shape_of((seq, q_width), BF16),
        shape_of((heads, seq), F32),
        shape_of((heads, seq), F32),
        shape_of((rows, model), F32),
        shape_of((rows, model), BF16),
        stack,
        stack,
    ]
    dma = pltpu.SemaphoreType.DMA
    out = pl.pallas_call(
        functools.partial(attend_kernel, ranks, plane_size, kv_heads),
        in_specs=[VMEM] * 9,
        out_specs=[VMEM] * len(outs),
        out_shape=outs,
        scratch_shapes=[
            pltpu.VMEM((q_width, seq), F32),
            pltpu.VMEM((ranks - 1, rows, model), BF16),
            pltpu.VMEM((ranks - 1, rows, model), BF16),
            dma((ranks - 1,)),
            dma((ranks - 1,)),
            dma((2, ranks - 1)),
            dma((2, ranks - 1)),
            dma((ranks,)),
            dma((ranks,)),
        ],
        compiler_params=remote(1),
        name="attend",
    )(x_all, gain, weights, out_weights, bias, cosine, sine, x, gain_two)
    return out[:6], out[6:]


def rejoin_kernel(ranks, plane_size, gain_row, gates, h, dz, router_t, a2, *refs):
    parts = refs[:ranks]
    dh, gathered, extra, g_send, g_recv = refs[ranks:]
    model = h.shape[1]
    spot = Spot(ranks, plane_size)
    meet([spot.ahead(s) for s in range(1, ranks)])
    total = parts[0][...]
    for i in range(1, ranks):
        total = total + parts[i][...].astype(F32)
    tail = total[:, model:]
    dgates = tail + pltpu.roll(tail, LANES // 2, 1)
    gate = gates[...]
    mean = jnp.sum(gate * dgates, axis=1, keepdims=True)
    d_logits = (gate * (dgates - mean)).astype(BF16)
    da2 = total[:, :model] + dot(d_logits, router_t[...])
    value = h[...]
    scale = lax.rsqrt(jnp.mean(value * value, axis=-1, keepdims=True) + EPSILON)
    normed = value * scale
    gain = router_t[gain_row : gain_row + 1, :].astype(F32)
    weighted = da2 * gain
    grad = dz[...] + scale * (
        weighted - normed * jnp.mean(weighted * normed, axis=-1, keepdims=True)
    )
    gathered[0] = grad.astype(BF16)
    dh[...] = grad
    line_out = LineGather(spot, gathered, g_send, g_recv)
    line_out.start(0)
    gain_grad = jnp.sum(da2 * normed, axis=0, keepdims=True)
    line = lax.broadcasted_iota(jnp.int32, (LANES, model), 0)
    extra[...] = jnp.where(line == gain_row, gain_grad, dot_tn(d_logits, a2[...]))
    for hop in range(line_out.hops):
        line_out.arrive(hop)
        if hop + 1 < line_out.hops:
            line_out.start(hop + 1)
    line_out.drain()


def rejoin(parts, gates, h, dz, router_t, a2, gain_row, plane_size):
    ranks = len(parts)
    dma = pltpu.SemaphoreType.DMA
    return pl.pallas_call(
        functools.partial(rejoin_kernel, ranks, plane_size, gain_row),
        in_specs=[VMEM] * (5 + ranks),
        out_specs=[VMEM] * 3,
        out_shape=[
            shape_of(h.shape, F32),
            shape_of((ranks,) + h.shape, BF16),
            shape_of((LANES, h.shape[1]), F32),
        ],
        scratch_shapes=[dma((2, ranks - 1)), dma((2, ranks - 1))],
        compiler_params=remote(2),
        name="rejoin",
    )(gates, h, dz, router_t, a2, *parts)


def last_kernel(ranks, plane_size, x, dh, gain, d_weights, d_rows, *refs):
    sums = refs[:ranks]
    out, columns_out, rows_out = refs[ranks : ranks + 3]
    (got, core_w, core_r, sum_w, sum_r, chip_w, chip_r, final) = refs[ranks + 3 : ranks + 11]
    r_send, r_recv, c_send, c_recv, p_send, p_recv, z_send, z_recv, local = refs[ranks + 11 :]
    spot = Spot(ranks, plane_size)
    chips, core, me = spot.chips, spot.core, spot.rank
    meet(
        [spot.ahead(s) for s in range(1, ranks)]
        + [spot.on_chip(spot.chip_ahead(k)) for k in range(1, chips)]
        + [spot.partner()]
    )
    z_copies = scatter_start(spot, sums, got, r_send, r_recv)
    pairs = ((0, d_weights, core_w, sum_w, chip_w), (1, d_rows, core_r, sum_r, chip_r))
    across = {}
    for k in range(chips):
        at = spot.chip_ahead(k)
        for which, src, buf, _, _ in pairs:
            across[k, which] = send(
                src.at[at, 1 - core],
                buf.at[k],
                c_send.at[which, k],
                c_recv.at[which, k],
                spot.partner(),
            )
    for k in list(range(1, chips)) + [0]:
        at = spot.chip_ahead(k)
        for which, src, buf, total, _ in pairs:
            across[k, which].wait()
            total[k] = (src[at, core].astype(F32) + buf[k].astype(F32)).astype(BF16)
    hops = {}
    for k in range(1, chips):
        for which, _, _, total, buf in pairs:
            hops[k, which] = send(
                total.at[k],
                buf.at[k - 1],
                p_send.at[which, k - 1],
                p_recv.at[which, k - 1],
                spot.on_chip(spot.chip_ahead(k)),
            )
    value = x[...]
    scale = lax.rsqrt(jnp.mean(value * value, axis=-1, keepdims=True) + EPSILON)
    normed = value * scale
    total = sums[0][...]
    for s in range(1, ranks):
        z_copies[s - 1].wait()
        total = total + got[s - 1].astype(F32)
    weighted = total * gain[...]
    grad = scale * (weighted - normed * jnp.mean(weighted * normed, axis=-1, keepdims=True))
    for k in range(1, chips):
        for which in range(2):
            hops[k, which].wait()
    value = sum_w[0].astype(F32)
    for k in range(1, chips):
        value = value + chip_w[k - 1].astype(F32)
    final[...] = value.astype(BF16)
    out[...] = dh[...] + grad
    value = sum_r[0].astype(F32)
    for k in range(1, chips):
        value = value + chip_r[k - 1].astype(F32)
    rows_out[...] = value
    kept = pltpu.make_async_copy(final.at[me], columns_out.at[me], local.at[0])
    kept.start()
    copies = [
        send(
            final.at[lax.rem(me + s, ranks)],
            columns_out.at[me],
            z_send.at[s - 1],
            z_recv.at[s - 1],
            spot.ahead(s),
        )
        for s in range(1, ranks)
    ]
    for copy in copies:
        copy.wait()
    kept.wait()


def last(x, dh, gain, d_weights, d_rows, sums):
    ranks = len(sums)
    chips, _, _, rows, columns = d_weights.shape
    dma = pltpu.SemaphoreType.DMA
    w_shape, r_shape = d_weights.shape[2:], d_rows.shape[2:]
    return pl.pallas_call(
        functools.partial(last_kernel, ranks, 2 * chips),
        in_specs=[VMEM] * (5 + ranks),
        out_specs=[VMEM] * 3,
        out_shape=[shape_of(x.shape, F32), shape_of(w_shape, BF16), shape_of(r_shape, F32)],
        scratch_shapes=[
            pltpu.VMEM((ranks - 1,) + x.shape, BF16),
            pltpu.VMEM((chips,) + w_shape, BF16),
            pltpu.VMEM((chips,) + r_shape, BF16),
            pltpu.VMEM((chips,) + w_shape, BF16),
            pltpu.VMEM((chips,) + r_shape, BF16),
            pltpu.VMEM((chips - 1,) + w_shape, BF16),
            pltpu.VMEM((chips - 1,) + r_shape, BF16),
            pltpu.VMEM(w_shape, BF16),
            dma((ranks - 1,)),
            dma((ranks - 1,)),
            dma((2, chips)),
            dma((2, chips)),
            dma((2, chips - 1)),
            dma((2, chips - 1)),
            dma((ranks - 1,)),
            dma((ranks - 1,)),
            dma((1,)),
        ],
        compiler_params=remote(3),
        name="last",
    )(x, dh, gain, d_weights, d_rows, *sums)


def piece_ids(position_index, starts):
    inside = (position_index[:, None] >= starts[None, :]) & (
        position_index[:, None] < starts[None, :] + PIECE
    )
    labels = jnp.arange(1, starts.shape[0] + 1, dtype=jnp.int32)[None, :]
    return jnp.sum(jnp.where(inside, labels, 0), axis=1, dtype=jnp.int32)


def on_device(
    inputs,
    cotangent,
    norm1_gain,
    w_query,
    key_projection,
    value_projection,
    w_output,
    norm2_gain,
    w_router,
    w_gate,
    w_up,
    w_down,
    routes,
    piece_starts,
):
    plane = Plane()
    ranks = lax.axis_size("expert")
    me = lax.axis_index("expert")
    rows, model = inputs.shape
    seq = rows * ranks
    weight_rows = w_query.shape[0]
    n_experts = w_router.shape[1]
    ff = w_gate.shape[2]
    kv_heads = KEY_VALUE_HEADS // ranks
    q_cols, kv_cols = kv_heads * GROUP * HEAD_WIDTH, kv_heads * HEAD_WIDTH
    rope_width = q_cols + kv_cols
    value_width = -(-kv_cols // LANES) * LANES
    columns = rope_width + value_width + LANES
    gain_one_row, gain_two_row = n_experts, n_experts + 1

    scale_one = lax.rsqrt(jnp.mean(inputs * inputs, axis=-1, keepdims=True) + EPSILON)
    x_own = (inputs * scale_one).astype(BF16)

    extra_cols = jnp.concatenate(
        [
            w_router,
            norm1_gain[:, None],
            norm2_gain[:, None],
            jnp.zeros((weight_rows, LANES - n_experts - 2), F32),
        ],
        axis=1,
    )
    by_rank = jnp.concatenate(
        [
            w_query.reshape(weight_rows, ranks, q_cols),
            key_projection.reshape(weight_rows, ranks, kv_cols),
            jnp.pad(
                value_projection.reshape(weight_rows, ranks, kv_cols),
                ((0, 0), (0, 0), (0, value_width - kv_cols)),
            ),
            jnp.broadcast_to(extra_cols[:, None, :], (weight_rows, ranks, LANES)),
        ],
        axis=2,
    ).astype(BF16)
    by_rank = jnp.transpose(by_rank, (1, 0, 2))

    axes = ("fsdp", "expert")
    total = plane.size * ranks
    move = [
        (j, (j % plane.size) * ranks + j // plane.size) for j in range(total)
    ]
    out_shard = lax.ppermute(w_output.astype(BF16), axes, move)

    lane_ids = jnp.arange(LANES, dtype=jnp.int32)
    routed = jnp.sum((routes[:, :, None] == lane_ids[None, None, :]).astype(F32), axis=1)
    grads_own = jnp.concatenate([cotangent, routed], axis=1).astype(BF16)

    core = plane.core.astype(jnp.int32)[None]
    keep, send, halves = pack_experts(core, w_gate, w_up, w_down, plane.size)
    got = plane.other_core(send)
    parts = [
        jnp.concatenate([jnp.where(plane.core == part, keep, got), halves[part][None]], axis=0)
        for part in range(2)
    ]
    by_rank, parts, out_shard, x_own, grads_own = lax.optimization_barrier(
        (by_rank, parts, out_shard, x_own, grads_own)
    )
    first = [plane.other_mid(parts[0])] + [
        plane.next_row(parts[1], s) for s in range(1, plane.rows)
    ]
    weights, out_weights, x_all, grads = gather_weights(
        by_rank, out_shard, x_own, grads_own, plane.size
    )
    first, weights = lax.optimization_barrier((first, weights))
    grads = grads.reshape(seq, grads.shape[2])
    found = {(0, 0, 0): parts[0], (0, 0, 1): parts[1], (0, 1, 0): first[0]}
    for s in range(1, plane.rows):
        found[s, 0, 1] = first[s]
        for mid in range(2):
            found[s, mid, 0] = plane.next_row(found[0, mid, 0], s)
    for s in range(plane.rows):
        found[s, 1, 1] = plane.other_mid(found[s, 0, 1])
    place, pieces = tuple(found.keys()), list(found.values())
    sources = [
        ((plane.row - s) % plane.rows) * 2 + (plane.mid + mid) % 2
        for s in range(plane.rows)
        for mid in range(2)
    ]
    where = jnp.stack([me] + sources).astype(jnp.int32)

    weights = weights.reshape(model, columns)
    out_weights = out_weights.reshape(q_cols, model)

    block_ids = jnp.arange(seq, dtype=jnp.int32) // rows
    places = ((me - block_ids) % ranks) * rows + jnp.arange(seq, dtype=jnp.int32) % rows
    ids = piece_ids(places, piece_starts[0])
    visible = (places[:, None] <= places[None, :]) | (
        (ids[:, None] == ids[None, :]) & (ids[None, :] > 0)
    )
    bias = jnp.where(visible, 0.0, NEG_FILL).astype(F32)
    half = HEAD_WIDTH // 2
    inverse = 10000.0 ** (-(jnp.arange(half, dtype=F32) * 2.0 / HEAD_WIDTH))
    angles = places.astype(F32)[:, None] * inverse[None, :]
    cosine = jnp.tile(jnp.cos(angles), (1, LANES // half))
    sine = jnp.tile(jnp.sin(angles), (1, LANES // half)) * jnp.where(
        lane_ids % HEAD_WIDTH < half, -1.0, 1.0
    )
    extra_t = weights[:, columns - LANES :].T
    gain_one = extra_t[gain_one_row : gain_one_row + 1].astype(F32)
    gain_two = extra_t[gain_two_row : gain_two_row + 1].astype(F32)
    kept, (mid_rows, a2, own_a2, other_a2) = attend(
        x_all,
        gain_one,
        weights,
        out_weights,
        bias,
        cosine,
        sine,
        inputs,
        gain_two,
        kv_heads,
        rope_width,
        plane.size,
    )

    other_grads = plane.other_core(grads)
    other_out, other_dx, _, *other_kept = experts(
        [other_a2.reshape(seq, model)], other_grads, extra_t, where, pieces, place, BF16
    )
    out_all, dx_all, gates, *own_kept = experts(
        [own_a2.reshape(seq, model)], grads, extra_t, where, pieces, place, F32
    )
    dx_all = dx_all + plane.other_core(other_dx).astype(F32)
    dxs = [
        dx_all[b * rows : (b + 1) * rows].astype(F32 if b == 0 else BF16) for b in range(ranks)
    ]
    dx_got = expert_scatter(dxs)
    order = [(s, mid) for s in reversed(range(plane.rows)) for mid in (1, 0)]
    chips = [
        ((plane.row + s) % plane.rows) * 2 + (plane.mid + mid) % 2 for s, mid in order
    ]
    own_kept.insert(2, grads[:, :model])
    other_kept.insert(2, other_grads[:, :model])
    flat = expert_grads(
        jnp.stack(chips).astype(jnp.int32), own_kept, other_kept, plane.size
    )
    dx_got, flat = lax.optimization_barrier((dx_got, flat))
    summed = {
        (s, mid, part): flat[2 * i + part]
        for i, (s, mid) in enumerate(order)
        for part in range(2)
    }

    def add(first, *others):
        value = first.astype(F32)
        for v in others:
            value = value + v.astype(F32)
        return value.astype(BF16)

    steps = range(1, plane.rows)
    a_first = [[plane.next_row(summed[s, mid, 0], s) for s in steps] for mid in range(2)]
    b_first = [plane.other_mid(summed[s, 1, 1]) for s in range(plane.rows)]

    dh, dh_stack, extra = rejoin(
        [dxs[0]] + dx_got, gates, mid_rows, cotangent, extra_t, a2, gain_two_row, plane.size
    )

    d_weights, d_out_weights, da1 = attend_back(
        dh_stack,
        x_all,
        weights,
        out_weights,
        kept,
        bias,
        cosine,
        sine,
        extra,
        kv_heads,
        gain_one_row,
    )
    a_first, b_first, d_weights = lax.optimization_barrier((a_first, b_first, d_weights))
    a_sums = [add(summed[0, mid, 0], *a_first[mid]) for mid in range(2)]
    b_sums = [add(summed[s, 0, 1], b_first[s]) for s in range(plane.rows)]
    a_sums, b_sums, d_weights = lax.optimization_barrier((a_sums, b_sums, d_weights))
    a_got = plane.other_mid(a_sums[1])
    b_got = [plane.next_row(b_sums[s], s) for s in steps]
    chip_count = plane.size // 2
    input_grad, by_rank, out_part = last(
        inputs,
        dh,
        gain_one,
        d_weights.reshape(chip_count, 2, ranks, weight_rows, columns),
        d_out_weights.reshape(chip_count, 2, weight_rows, model),
        da1,
    )
    a_got, b_got, out_part = lax.optimization_barrier((a_got, b_got, out_part))
    b_kept = b_sums[0]
    if len(b_got) > 1:
        b_kept = add(b_kept, *b_got[:-1])
    b_got = b_got[-1]
    other = plane.other_core(
        jnp.where(
            plane.core == 0,
            b_kept[:2].astype(F32) + b_got[:2].astype(F32),
            a_sums[0][:2].astype(F32) + a_got[:2].astype(F32),
        ).astype(BF16)
    )
    gate_grad, up_grad, down_grad = finish(
        core, a_sums[0], a_got, b_kept, b_got, other, w_down.shape[1], model, plane.size
    )
    out_all = out_all + plane.other_core(other_out).astype(F32)
    outs = [out_all[b * rows : (b + 1) * rows] for b in range(ranks)]
    output = mid_rows + outs[0]
    for v in expert_scatter([v.astype(BF16) for v in outs]):
        output = output + v.astype(F32)

    w_output_grad = lax.ppermute(
        out_part.astype(BF16), axes, [(b, a) for a, b in move]
    ).astype(F32)
    by_rank = by_rank.astype(F32)

    def columns_of(start, width):
        piece = by_rank[:, :, start : start + width]
        return jnp.transpose(piece, (1, 0, 2)).reshape(weight_rows, ranks * width)

    extra_grad = jnp.sum(by_rank[:, :, columns - LANES :], axis=0)
    return (
        output,
        input_grad,
        extra_grad[:, gain_one_row],
        columns_of(0, q_cols),
        columns_of(q_cols, kv_cols),
        columns_of(rope_width, kv_cols),
        w_output_grad,
        extra_grad[:, gain_two_row],
        extra_grad[:, :n_experts],
        gate_grad,
        up_grad,
        down_grad,
    )


def solution(mesh):
    both = ("fsdp", "expert")
    rows, flat, stack = P(both, None), P(both), P("expert", "fsdp", None)
    weights = (flat, rows, rows, rows, rows, flat, rows, stack, stack, stack)
    return jax.shard_map(
        on_device,
        mesh=mesh,
        in_specs=(rows, rows) + weights + (rows, P("fsdp", None)),
        out_specs=(rows, rows) + weights,
        check_vma=False,
    )
```

```python
import functools

import jax
import jax.numpy as jnp
from jax import lax
from jax.experimental import pallas as pl
from jax.experimental.pallas import tpu as pltpu
from jax.sharding import PartitionSpec as P

QUERY_HEADS = 24
KEY_VALUE_HEADS = 8
GROUP = QUERY_HEADS // KEY_VALUE_HEADS
HEAD_WIDTH = 64
PIECE = 256
LANES = 128
DEVICE_ROWS = 128
EPSILON = 1e-05
NEG_FILL = -1e30
SCORE_SCALE = HEAD_WIDTH ** (-0.5)
F32 = jnp.float32
BF16 = jnp.bfloat16

VMEM = pl.BlockSpec(memory_space=pltpu.VMEM)
SMEM = pl.BlockSpec(memory_space=pltpu.SMEM)
ANY = pl.BlockSpec(memory_space=pl.ANY)
MESH = pl.DeviceIdType.MESH


def dot(a, b):
    return lax.dot_general(a, b, (((1,), (0,)), ((), ())), preferred_element_type=F32)


def dot_nt(a, b):
    return lax.dot_general(a, b, (((1,), (1,)), ((), ())), preferred_element_type=F32)


def dot_tn(a, b):
    return lax.dot_general(a, b, (((0,), (0,)), ((), ())), preferred_element_type=F32)


def shape_of(dims, dtype):
    return jax.ShapeDtypeStruct(tuple(dims), dtype)


def params(**kw):
    return pltpu.CompilerParams(vmem_limit_bytes=60 * 1024 * 1024, **kw)


class Plane:
    def __init__(self):
        self.size = lax.axis_size("fsdp")
        self.rows = self.size // 4
        index = lax.axis_index("fsdp")
        self.index = index
        self.core = index % 2
        self.mid = (index // 2) % 2
        self.row = index // 4

    def other_core(self, x):
        return lax.ppermute(x, "fsdp", [(i, i ^ 1) for i in range(self.size)])

    def other_mid(self, x):
        return lax.ppermute(x, "fsdp", [(i, i ^ 2) for i in range(self.size)])

    def next_row(self, x, step):
        return lax.ppermute(
            x, "fsdp", [(i, (i // 4 + step) % self.rows * 4 + i % 4) for i in range(self.size)]
        )


def expert_shift(x, step):
    count = lax.axis_size("expert")
    return lax.ppermute(x, "expert", [(i, (i + step) % count) for i in range(count)])


def expert_scatter(blocks):
    count = lax.axis_size("expert")
    return [expert_shift(blocks[s], count - s) for s in range(1, count)]


def chooser(width, blocks, part, dtype=BF16):
    n = width // blocks
    line = lax.broadcasted_iota(jnp.int32, (width // 2, width), 0)
    column = lax.broadcasted_iota(jnp.int32, (width // 2, width), 1)
    want = (2 * (line // n) + part) * n + line % n
    return jnp.where(column == want, 1.0, 0.0).astype(dtype)


def pack_kernel(blocks, core, gate, up, down, keep, send, halves):
    width = gate.shape[2]
    mine = chooser(width, blocks, core[0])
    theirs = chooser(width, blocks, 1 - core[0])
    for place, ref in ((0, gate), (1, up)):
        value = ref[0].astype(BF16)
        keep[place, 0] = dot_nt(value, mine).astype(BF16)
        send[place, 0] = dot_nt(value, theirs).astype(BF16)
    value = down[0].astype(BF16)
    rows, wide = value.shape[0] // 2, width // 2
    for part in range(2):
        for j in range(value.shape[1] // wide):
            halves[part, 0, j * rows : (j + 1) * rows] = value[
                part * rows : (part + 1) * rows, j * wide : (j + 1) * wide
            ]


def pack_experts(core, w_gate, w_up, w_down, blocks):
    local, depth, width = w_gate.shape
    out = shape_of((2, local, depth, width // 2), BF16)
    block = pl.BlockSpec((2, 1, depth, width // 2), lambda e: (0, e, 0, 0))
    return pl.pallas_call(
        functools.partial(pack_kernel, blocks),
        grid=(local,),
        in_specs=[SMEM]
        + [pl.BlockSpec((1,) + w.shape[1:], lambda e: (e, 0, 0)) for w in (w_gate, w_up, w_down)],
        out_specs=[block] * 3,
        out_shape=[out] * 3,
        name="pack_experts",
    )(core, w_gate, w_up, w_down)


def swap_halves(x):
    lane = lax.broadcasted_iota(jnp.int32, x.shape, 1)
    return jnp.where(
        lane % HEAD_WIDTH < HEAD_WIDTH // 2, pltpu.roll(x, LANES - 32, 1), pltpu.roll(x, 32, 1)
    )


def head_slice(ref, start):
    return ref[:, start : start + HEAD_WIDTH]


def experts_kernel(blocks, pieces, place, row_block, *refs):
    a2_in = refs[:blocks]
    grads_in, router_t, where_ref = refs[blocks : blocks + 3]
    piece_refs = refs[blocks + 3 : blocks + 3 + pieces]
    (out_all, dx_all, gates_out, a2_t, hidden_t, d_gate, d_up) = refs[
        blocks + 3 + pieces : blocks + 10 + pieces
    ]
    (a2, gate_w, up_w, down_w, out_sum, dx_sum, gates, dgates, in_sem, w_sem) = refs[
        blocks + 10 + pieces :
    ]
    step, steps = pl.program_id(0), pl.num_programs(0)
    rows = a2_in[0].shape[0]
    seq, model = a2.shape
    depth, width = piece_refs[0].shape[2], gate_w.shape[2]
    down_rows = depth * width // model
    slot = lax.rem(step, 2)

    def fetch(e, to):
        for i, (row_step, mid, part) in enumerate(place):
            source = where_ref[1 + row_step * 2 + mid] * 2 + part
            at = pl.multiple_of(source * depth, 32)
            for which, buf in ((0, gate_w), (1, up_w)):
                pltpu.make_async_copy(
                    piece_refs[i].at[which, e], buf.at[to, pl.ds(at, depth)], w_sem.at[which, to]
                ).start()
            at = pl.multiple_of(source * down_rows, 16)
            for j in range(model // width):
                pltpu.make_async_copy(
                    piece_refs[i].at[2, e, pl.ds(j * down_rows, down_rows)],
                    down_w.at[to, pl.ds(at, down_rows), pl.ds(j * width, width)],
                    w_sem.at[2, to],
                ).start()

    @pl.when(step == 0)
    def _():
        for b in range(blocks):
            pltpu.make_async_copy(
                a2_in[b], a2.at[pl.ds(b * rows, rows)], in_sem.at[0]
            ).start()
        fetch(0, 0)
        pltpu.make_async_copy(a2, a2, in_sem.at[0]).wait()
        logits = dot_nt(a2[...], router_t[...])
        routed = grads_in[:, model:].astype(F32) > 0.5
        top = jnp.max(jnp.where(routed, logits, NEG_FILL), axis=1, keepdims=True)
        weight = jnp.where(routed, jnp.exp(jnp.where(routed, logits, top) - top), 0.0)
        gates[...] = weight / jnp.sum(weight, axis=1, keepdims=True)
        gates_out[...] = gates[: gates_out.shape[0], :]
        dgates[...] = jnp.zeros_like(dgates)
        a2_t[...] = a2[...].T

    @pl.when(step + 1 < steps)
    def _():
        fetch(step + 1, 1 - slot)

    for which, buf in ((0, gate_w), (1, up_w), (2, down_w)):
        pltpu.make_async_copy(buf.at[slot], buf.at[slot], w_sem.at[which, slot]).wait()

    mine = where_ref[0] * steps + step

    def block(i, carry):
        at = pl.ds(pl.multiple_of(i * row_block, row_block), row_block)
        left = a2[at, :]
        gate_lin = dot(left, gate_w[slot])
        up_lin = dot(left, up_w[slot])
        back = dot_nt(grads_in[at, :model], down_w[slot])
        lane = lax.broadcasted_iota(jnp.int32, (row_block, LANES), 1)
        here = lane == mine
        gate = jnp.sum(jnp.where(here, gates[at, :], 0.0), axis=1, keepdims=True)
        sig = 1.0 / (1.0 + jnp.exp(-gate_lin))
        silu = gate_lin * sig
        hidden = silu * up_lin
        dgates[at, :] += jnp.where(here, jnp.sum(hidden * back, axis=1, keepdims=True), 0.0)
        hidden_low = (hidden * gate).astype(BF16)
        d_hidden = back * gate
        d_gate_low = (d_hidden * up_lin * (sig + silu * (1.0 - sig))).astype(BF16)
        d_up_low = (d_hidden * silu).astype(BF16)
        d_gate[at, :] = d_gate_low
        d_up[at, :] = d_up_low
        hidden_t[0, :, at] = hidden_low.T
        out_new = dot(hidden_low, down_w[slot])
        dx_new = dot_nt(d_gate_low, gate_w[slot]) + dot_nt(d_up_low, up_w[slot])

        @pl.when(step == 0)
        def _():
            out_sum[at, :] = out_new
            dx_sum[at, :] = dx_new

        @pl.when(step > 0)
        def _():
            out_sum[at, :] += out_new
            dx_sum[at, :] += dx_new

        return carry

    lax.fori_loop(0, seq // row_block, block, 0)

    @pl.when(step == steps - 1)
    def _():
        high = dgates[...].astype(BF16).astype(F32)
        low = dgates[...] - high
        lane = lax.broadcasted_iota(jnp.int32, high.shape, 1)
        tail = jnp.where(lane < LANES // 2, high, pltpu.roll(low, LANES // 2, 1))
        out_all[...] = out_sum[...].astype(out_all.dtype)
        dx_all[:, :model] = dx_sum[...].astype(dx_all.dtype)
        dx_all[:, model:] = tail.astype(dx_all.dtype)


def experts(a2_blocks, grads, router_t, where, pieces, place, dtype):
    blocks = len(a2_blocks)
    rows, model = a2_blocks[0].shape
    seq = rows * blocks
    local, depth, width = pieces[0].shape[1:]
    outs = [
        shape_of((seq, model), dtype),
        shape_of((seq, model + LANES), dtype),
        shape_of((DEVICE_ROWS, LANES), F32),
        shape_of((model, seq), BF16),
        shape_of((local, width, seq), BF16),
        shape_of((seq, local * width), BF16),
        shape_of((seq, local * width), BF16),
    ]
    whole = lambda dims: pl.BlockSpec(
        dims, lambda e: (0,) * len(dims), pipeline_mode=pl.Buffered(1)
    )
    out_specs = (
        [whole(o.shape) for o in outs[:4]]
        + [pl.BlockSpec((1, width, seq), lambda e: (e, 0, 0))]
        + [pl.BlockSpec((seq, width), lambda e: (0, e))] * 2
    )
    return pl.pallas_call(
        functools.partial(experts_kernel, blocks, len(pieces), place, 256),
        grid=(local,),
        in_specs=[ANY] * blocks
        + [whole(grads.shape), whole(router_t.shape), SMEM]
        + [ANY] * len(pieces),
        out_specs=out_specs,
        out_shape=outs,
        scratch_shapes=[
            pltpu.VMEM((seq, model), BF16),
            pltpu.VMEM((2, model, width), BF16),
            pltpu.VMEM((2, model, width), BF16),
            pltpu.VMEM((2, width, model), BF16),
            pltpu.VMEM((seq, model), F32),
            pltpu.VMEM((seq, model), F32),
            pltpu.VMEM((seq, LANES), F32),
            pltpu.VMEM((seq, LANES), F32),
            pltpu.SemaphoreType.DMA((1,)),
            pltpu.SemaphoreType.DMA((3, 2)),
        ],
        compiler_params=params(dimension_semantics=("arbitrary",)),
        name="experts",
    )(*a2_blocks, grads, router_t, where, *pieces)


def expert_grads_kernel(plane_rows, depth, down_rows, where_ref, *refs):
    (a2_t0, a2_t1, hid0, hid1, grads0, grads1, dg0, dg1, du0, du1) = refs[:10]
    row_outs, mid_outs = refs[10 : 10 + plane_rows], refs[10 + plane_rows : 12 + plane_rows]
    down_sum = refs[12 + plane_rows]
    model, width = a2_t0.shape[0], dg0.shape[1]
    down_sum[...] = (dot(hid0[0], grads0[...]) + dot(hid1[0], grads1[...])).astype(BF16)
    for s in range(plane_rows):
        for mid in range(2):
            source = where_ref[2 * s + mid]
            at = pl.ds(pl.multiple_of(source * 2 * depth, 32), 2 * depth)
            left0, left1 = a2_t0[at, :], a2_t1[at, :]
            gate = (dot(left0, dg0[...]) + dot(left1, dg1[...])).astype(BF16)
            up = (dot(left0, du0[...]) + dot(left1, du1[...])).astype(BF16)
            for part, out in ((0, row_outs[s].at[mid]), (1, mid_outs[mid].at[s])):
                out[0, 0] = gate[part * depth : (part + 1) * depth]
                out[1, 0] = up[part * depth : (part + 1) * depth]
                at = pl.ds(pl.multiple_of((source * 2 + part) * down_rows, 16), down_rows)
                down = down_sum[at, :]
                for j in range(model // width):
                    out[2, 0, j * down_rows : (j + 1) * down_rows, :] = down[
                        :, j * width : (j + 1) * width
                    ]


def expert_grads(where, first, second, plane_size, plane_rows):
    model, seq = first[0].shape
    local, width = first[1].shape[:2]
    depth, down_rows = model // plane_size, width // plane_size
    counts = [2] * plane_rows + [plane_rows] * 2
    once = lambda dims: pl.BlockSpec(dims, lambda e: (0, 0), pipeline_mode=pl.Buffered(1))
    specs = [
        once((model, seq)),
        pl.BlockSpec((1, width, seq), lambda e: (e, 0, 0)),
        once((seq, model)),
        pl.BlockSpec((seq, width), lambda e: (0, e)),
        pl.BlockSpec((seq, width), lambda e: (0, e)),
    ]
    operands = [v for pair in zip(first, second) for v in pair]
    return pl.pallas_call(
        functools.partial(expert_grads_kernel, plane_rows, depth, down_rows),
        grid=(local,),
        in_specs=[SMEM] + [spec for spec in specs for _ in range(2)],
        out_specs=[
            pl.BlockSpec((n, 3, 1, depth, width), lambda e: (0, 0, e, 0, 0)) for n in counts
        ],
        out_shape=[shape_of((n, 3, local, depth, width), BF16) for n in counts],
        scratch_shapes=[pltpu.VMEM((width, model), BF16)],
        compiler_params=params(),
        name="expert_grads",
    )(where, *operands)


def finish_kernel(blocks, core, kept_a, got_a, kept_b, got_b, other, gate, up, down):
    width, wide = gate.shape[2], kept_a.shape[3]
    mine = chooser(width, blocks, core[0])
    theirs = chooser(width, blocks, 1 - core[0])
    first = core[0] == 0
    for place, out in ((0, gate), (1, up)):
        kept = jnp.where(first, kept_a[place, 0].astype(F32), kept_b[place, 0].astype(F32))
        got = jnp.where(first, got_a[place, 0].astype(F32), got_b[place, 0].astype(F32))
        out[0] = (
            dot(kept.astype(BF16), mine)
            + dot(got.astype(BF16), mine)
            + dot(other[place, 0], theirs)
        )
    rows = down.shape[1] // 2
    for part, kept, got in ((0, kept_a, got_a), (1, kept_b, got_b)):
        value = kept[2, 0].astype(F32) + got[2, 0].astype(F32)
        for j in range(value.shape[0] // rows):
            down[0, part * rows : (part + 1) * rows, j * wide : (j + 1) * wide] = value[
                j * rows : (j + 1) * rows
            ]


def finish(core, kept_a, got_a, kept_b, got_b, other, down_rows, model, blocks):
    local, depth, wide = kept_a.shape[1:]
    block = pl.BlockSpec((3, 1, depth, wide), lambda e: (0, e, 0, 0))
    outs = [
        shape_of((local, depth, 2 * wide), F32),
        shape_of((local, depth, 2 * wide), F32),
        shape_of((local, down_rows, model), F32),
    ]
    return pl.pallas_call(
        functools.partial(finish_kernel, blocks),
        grid=(local,),
        in_specs=[SMEM]
        + [block] * 4
        + [pl.BlockSpec((2, 1, depth, wide), lambda e: (0, e, 0, 0))],
        out_specs=[pl.BlockSpec((1,) + o.shape[1:], lambda e: (e, 0, 0)) for o in outs],
        out_shape=outs,
        name="finish",
    )(core, kept_a, got_a, kept_b, got_b, other)


def attend_back_kernel(blocks, kv_heads, gain_row, *refs):
    dh_ref, x_all = refs[:2]
    (weights, out_weights, a1, qk, val, mixed, maxes, inverse, bias, cosine, sine, extra) = refs[2:14]
    d_weights, d_out_weights = refs[14:16]
    sums = refs[16 : blocks + 16]
    grads, d_mixed, dq_t, d_qk, d_lin = refs[blocks + 16 :]
    rows = x_all.shape[1]
    rope_width, value_width = qk.shape[1], val.shape[1]
    q_width = kv_heads * GROUP * HEAD_WIDTH
    for b in range(blocks):
        grads[b * rows : (b + 1) * rows, :] = dh_ref[b]
    d_mixed[...] = dot_nt(grads[...], out_weights[...]).astype(BF16)
    d_out_weights[...] = dot_tn(mixed[...], grads[...]).astype(BF16)
    if value_width > kv_heads * HEAD_WIDTH:
        d_lin[:, rope_width:] = jnp.zeros((d_lin.shape[0], value_width), BF16)
    for g in range(kv_heads):
        key = head_slice(qk, q_width + g * HEAD_WIDTH)
        key_t = key.T
        value = head_slice(val, g * HEAD_WIDTH)
        d_key, d_value = None, None
        for j in range(GROUP):
            h = g * GROUP + j
            query = head_slice(qk, h * HEAD_WIDTH)
            grad = head_slice(d_mixed, h * HEAD_WIDTH)
            scores = dot_nt(key, query) * SCORE_SCALE + bias[...]
            prob = jnp.exp(scores - maxes[h : h + 1, :]) * inverse[h : h + 1, :]
            d_prob = dot_nt(value, grad)
            inner = jnp.sum(prob * d_prob, axis=0, keepdims=True)
            d_scores = (prob * (d_prob - inner)).astype(BF16)
            dk = dot(d_scores, query)
            dv = dot(prob.astype(BF16), grad)
            d_key = dk if d_key is None else d_key + dk
            d_value = dv if d_value is None else d_value + dv
            dq_t[h * HEAD_WIDTH : (h + 1) * HEAD_WIDTH, :] = dot(key_t, d_scores)
        start = q_width + g * HEAD_WIDTH
        d_qk[:, start : start + HEAD_WIDTH] = d_key * SCORE_SCALE
        start = rope_width + g * HEAD_WIDTH
        d_lin[:, start : start + HEAD_WIDTH] = d_value.astype(BF16)
    d_qk[:, :q_width] = dq_t[...].T * SCORE_SCALE
    for c in range(rope_width // LANES):
        at = slice(c * LANES, (c + 1) * LANES)
        x = d_qk[:, at]
        d_lin[:, at] = (x * cosine[...] - swap_halves(x) * sine[...]).astype(BF16)
    total = dot_nt(d_lin[...], weights[:, : rope_width + value_width])
    gain_grad = None
    for b in range(blocks):
        part = total[b * rows : (b + 1) * rows, :]
        sums[b][...] = part.astype(sums[b].dtype)
        new = jnp.sum(part * x_all[b].astype(F32), axis=0, keepdims=True)
        gain_grad = new if gain_grad is None else gain_grad + new
    d_weights[:, : rope_width + value_width] = dot_tn(a1[...], d_lin[...]).astype(BF16)
    line = lax.broadcasted_iota(jnp.int32, extra.shape, 0)
    tail = jnp.where(line == gain_row, gain_grad, extra[...])
    d_weights[:, rope_width + value_width :] = tail.T.astype(BF16)


def attend_back(
    dh_stack, x_all, weights, out_weights, kept, bias, cosine, sine, extra, kv_heads, gain_row
):
    blocks, rows, model = dh_stack.shape
    seq = rows * blocks
    q_width = out_weights.shape[0]
    rope_width, value_width = kept[1].shape[1], kept[2].shape[1]
    outs = [shape_of(weights.shape, BF16), shape_of(out_weights.shape, BF16)] + [
        shape_of((rows, model), F32 if b == 0 else BF16) for b in range(blocks)
    ]
    out = pl.pallas_call(
        functools.partial(attend_back_kernel, blocks, kv_heads, gain_row),
        in_specs=[VMEM] * 14,
        out_specs=[VMEM] * len(outs),
        out_shape=outs,
        scratch_shapes=[
            pltpu.VMEM((seq, model), BF16),
            pltpu.VMEM((seq, q_width), BF16),
            pltpu.VMEM((q_width, seq), F32),
            pltpu.VMEM((seq, rope_width), F32),
            pltpu.VMEM((seq, rope_width + value_width), BF16),
        ],
        compiler_params=params(),
        name="attend_back",
    )(dh_stack, x_all, weights, out_weights, *kept, bias, cosine, sine, extra)
    return out[0], out[1], out[2:]


class Spot:
    def __init__(self, ranks, plane_size):
        self.ranks, self.chips = ranks, plane_size // 2
        self.rank = lax.axis_index("expert")
        self.index = lax.axis_index("fsdp")
        self.chip = self.index // 2
        self.core = self.index % 2

    def behind(self, s):
        return {"expert": lax.rem(self.rank - s + self.ranks, self.ranks)}

    def ahead(self, s):
        return {"expert": lax.rem(self.rank + s, self.ranks)}

    def partner(self):
        return {"fsdp": self.chip * 2 + (1 - self.core)}

    def chip_ahead(self, k):
        return lax.rem(self.chip + k, self.chips)

    def chip_behind(self, k):
        return lax.rem(self.chip - k + self.chips, self.chips)

    def on_chip(self, chip):
        return {"fsdp": chip * 2 + self.core}


def greet(peers):
    barrier = pltpu.get_barrier_semaphore()
    for peer in peers:
        pl.semaphore_signal(barrier, inc=1, device_id=peer, device_id_type=MESH)


def await_peers(peers):
    pl.semaphore_wait(pltpu.get_barrier_semaphore(), len(peers))


def meet(peers):
    greet(peers)
    await_peers(peers)


def send(src, dst, send_sem, recv_sem, peer):
    copy = pltpu.make_async_remote_copy(
        src_ref=src,
        dst_ref=dst,
        send_sem=send_sem,
        recv_sem=recv_sem,
        device_id=peer,
        device_id_type=MESH,
    )
    copy.start()
    return copy


def remote(collective_id):
    return params(collective_id=collective_id, has_side_effects=True)


def gather_weights_kernel(
    ranks, plane_size, by_rank, rows_in, x_in, grads_in, weights, out_rows, x_all, grads_all, *sems
):
    z_send, z_recv, p_send, p_recv, c_send, c_recv, local = sems[:7]
    spot = Spot(ranks, plane_size)
    f, me, chips = spot.index, spot.rank, spot.chips
    others = range(1, ranks)
    meet(
        [spot.ahead(s) for s in others]
        + [spot.on_chip(spot.chip_ahead(k)) for k in range(1, chips)]
        + [spot.partner()]
    )
    waits = []
    z_copies = [
        send(
            by_rank.at[lax.rem(me + s, ranks)],
            weights.at[f, me],
            z_send.at[s - 1],
            z_recv.at[s - 1],
            spot.ahead(s),
        )
        for s in others
    ]
    kept = [
        pltpu.make_async_copy(by_rank.at[me], weights.at[f, me], local.at[0]),
        pltpu.make_async_copy(rows_in, out_rows.at[f], local.at[1]),
        pltpu.make_async_copy(x_in, x_all.at[0], local.at[2]),
        pltpu.make_async_copy(grads_in, grads_all.at[0], local.at[3]),
    ]
    for copy in kept:
        copy.start()
    lines = [
        LineGather(spot, x_all, sems[7], sems[8]),
        LineGather(spot, grads_all, sems[9], sems[10]),
    ]

    def spread(which, src, buf):
        return [
            send(
                src,
                buf.at[f],
                p_send.at[which, k - 1],
                p_recv.at[which, k - 1],
                spot.on_chip(spot.chip_ahead(k)),
            )
            for k in range(1, chips)
        ] + [send(src, buf.at[f], c_send.at[which, 0], c_recv.at[which, 0], spot.partner())]

    row_copies = spread(1, rows_in, out_rows)
    for copy in kept:
        copy.wait()
    lines[0].start(0)
    for copy in z_copies:
        copy.wait()
    weight_copies = spread(0, weights.at[f], weights)
    for hop in range(ranks - 1):
        lines[0].arrive(hop)
        if hop + 1 < ranks - 1:
            lines[0].start(hop + 1)
        else:
            lines[1].start(0)
    for k in range(1, chips):
        source = spot.chip_behind(k) * 2 + spot.core
        for which, copies, buf in ((1, row_copies, out_rows), (0, weight_copies, weights)):
            copies[k - 1].wait()
            waits.append(
                send(
                    buf.at[source],
                    buf.at[source],
                    c_send.at[which, k],
                    c_recv.at[which, k],
                    spot.partner(),
                )
            )
    for hop in range(ranks - 1):
        lines[1].arrive(hop)
        if hop + 1 < ranks - 1:
            lines[1].start(hop + 1)
    row_copies[-1].wait()
    weight_copies[-1].wait()
    for copy in waits:
        copy.wait()
    for line in lines:
        line.drain()


def gather_weights(by_rank, rows_in, x_in, grads_in, plane_size):
    ranks, rows, columns = by_rank.shape
    chips = plane_size // 2
    dma = pltpu.SemaphoreType.DMA
    return pl.pallas_call(
        functools.partial(gather_weights_kernel, ranks, plane_size),
        in_specs=[VMEM] * 4,
        out_specs=[VMEM] * 4,
        out_shape=[
            shape_of((plane_size, ranks, rows, columns), BF16),
            shape_of((plane_size,) + rows_in.shape, BF16),
            shape_of((ranks,) + x_in.shape, BF16),
            shape_of((ranks,) + grads_in.shape, BF16),
        ],
        scratch_shapes=[
            dma((ranks - 1,)),
            dma((ranks - 1,)),
            dma((2, chips - 1)),
            dma((2, chips - 1)),
            dma((2, chips)),
            dma((2, chips)),
            dma((4,)),
        ]
        + [dma((2, ranks - 1))] * 4,
        compiler_params=remote(0),
        name="gather_weights",
    )(by_rank, rows_in, x_in, grads_in)


def scatter_start(spot, refs, buf, send_sem, recv_sem):
    return [
        send(refs[s], buf.at[s - 1], send_sem.at[s - 1], recv_sem.at[s - 1], spot.behind(s))
        for s in range(1, spot.ranks)
    ]


class LineGather:
    def __init__(self, spot, buf, send_sem, recv_sem):
        self.spot, self.buf, self.sems = spot, buf, (send_sem, recv_sem)
        me, n = spot.rank, spot.ranks
        self.hops = n - 1
        self.sends = [(me - h >= 0) & (me + 1 < n) for h in range(n - 1)], [
            (me + h < n) & (me >= 1) for h in range(n - 1)
        ]
        self.gets = [me - 1 - h >= 0 for h in range(n - 1)], [
            me + 1 + h < n for h in range(n - 1)
        ]

    def slots(self, way, h):
        n = self.spot.ranks
        return (h, h + 1) if way == 0 else ((n - h) % n, n - h - 1)

    def copy(self, way, h):
        source, target = self.slots(way, h)
        return pltpu.make_async_remote_copy(
            src_ref=self.buf.at[source],
            dst_ref=self.buf.at[target],
            send_sem=self.sems[0].at[way, h],
            recv_sem=self.sems[1].at[way, h],
            device_id=self.spot.ahead(1) if way == 0 else self.spot.behind(1),
            device_id_type=MESH,
        )

    def start(self, h):
        for way in range(2):

            @pl.when(self.sends[way][h])
            def _():
                self.copy(way, h).start()

    def arrive(self, h):
        for way in range(2):

            @pl.when(self.gets[way][h])
            def _():
                self.copy(way, h).wait_recv()

    def passed(self, h, then):
        for way in range(2):

            @pl.when(self.gets[way][h])
            def _():
                then(self.slots(way, h)[1])

    def drain(self):
        for h in range(self.hops):
            for way in range(2):

                @pl.when(self.sends[way][h])
                def _():
                    self.copy(way, h).wait_send()


def attend_kernel(ranks, plane_size, kv_heads, *refs):
    x_all, gain, weights, out_weights, bias, cosine, sine, x, gain_two = refs[:9]
    (a1, qk, val, mixed, maxes, inverse, h_out, a2, gathered, other) = refs[9:19]
    mixed_t, sums, got, r_send, r_recv, g_send, g_recv, c_send, c_recv = refs[19:]
    spot = Spot(ranks, plane_size)
    peers = [spot.ahead(s) for s in range(1, ranks)] + [spot.partner()]
    greet(peers)
    rows = x_all.shape[1]
    rope_width = qk.shape[1]
    q_width = kv_heads * GROUP * HEAD_WIDTH
    for b in range(ranks):
        a1[b * rows : (b + 1) * rows, :] = (x_all[b].astype(F32) * gain[...]).astype(BF16)
    linear = dot(a1[...], weights[:, : rope_width + val.shape[1]])
    for c in range(rope_width // LANES):
        part = linear[:, c * LANES : (c + 1) * LANES]
        qk[:, c * LANES : (c + 1) * LANES] = (
            part * cosine[...] + swap_halves(part) * sine[...]
        ).astype(BF16)
    val[...] = linear[:, rope_width:].astype(BF16)
    for g in range(kv_heads):
        key = head_slice(qk, q_width + g * HEAD_WIDTH)
        value_t = head_slice(val, g * HEAD_WIDTH).T
        for j in range(GROUP):
            h = g * GROUP + j
            scores = dot_nt(key, head_slice(qk, h * HEAD_WIDTH)) * SCORE_SCALE + bias[...]
            top = jnp.max(scores, axis=0, keepdims=True)
            weight = jnp.exp(scores - top)
            inv = 1.0 / jnp.sum(weight, axis=0, keepdims=True)
            maxes[h : h + 1, :] = top
            inverse[h : h + 1, :] = inv
            mixed_t[h * HEAD_WIDTH : (h + 1) * HEAD_WIDTH, :] = dot(
                value_t, (weight * inv).astype(BF16)
            )
    mixed[...] = mixed_t[...].T.astype(BF16)
    await_peers(peers)
    total = dot(mixed[...], out_weights[...])
    for b in range(1, ranks):
        sums[b - 1] = total[b * rows : (b + 1) * rows, :].astype(BF16)
    copies = scatter_start(
        spot, [None] + [sums.at[s - 1] for s in range(1, ranks)], got, r_send, r_recv
    )
    total = x[...] + total[:rows, :]
    for s in range(1, ranks):
        copies[s - 1].wait()
        total = total + got[s - 1].astype(F32)
    scale = lax.rsqrt(jnp.mean(total * total, axis=-1, keepdims=True) + EPSILON)
    low = (total * scale * gain_two[...]).astype(BF16)
    gathered[0] = low
    line = LineGather(spot, gathered, g_send, g_recv)
    line.start(0)

    def across(s):
        return pltpu.make_async_remote_copy(
            src_ref=gathered.at[s],
            dst_ref=other.at[s],
            send_sem=c_send.at[s],
            recv_sem=c_recv.at[s],
            device_id=spot.partner(),
            device_id_type=MESH,
        )

    across(0).start()
    a2[...] = low
    h_out[...] = total
    for hop in range(line.hops):
        line.arrive(hop)
        if hop + 1 < line.hops:
            line.start(hop + 1)
        line.passed(hop, lambda s: across(s).start())
    line.drain()
    for s in range(ranks):
        across(s).wait()


def attend(
    x_all, gain, weights, out_weights, bias, cosine, sine, x, gain_two, kv_heads, rope_width,
    plane_size,
):
    ranks, rows, model = x_all.shape
    seq = rows * ranks
    q_width = kv_heads * GROUP * HEAD_WIDTH
    value_width = weights.shape[1] - LANES - rope_width
    heads = kv_heads * GROUP
    stack = shape_of((ranks, rows, model), BF16)
    outs = [
        shape_of((seq, model), BF16),
        shape_of((seq, rope_width), BF16),
        shape_of((seq, value_width), BF16),
        shape_of((seq, q_width), BF16),
        shape_of((heads, seq), F32),
        shape_of((heads, seq), F32),
        shape_of((rows, model), F32),
        shape_of((rows, model), BF16),
        stack,
        stack,
    ]
    dma = pltpu.SemaphoreType.DMA
    out = pl.pallas_call(
        functools.partial(attend_kernel, ranks, plane_size, kv_heads),
        in_specs=[VMEM] * 9,
        out_specs=[VMEM] * len(outs),
        out_shape=outs,
        scratch_shapes=[
            pltpu.VMEM((q_width, seq), F32),
            pltpu.VMEM((ranks - 1, rows, model), BF16),
            pltpu.VMEM((ranks - 1, rows, model), BF16),
            dma((ranks - 1,)),
            dma((ranks - 1,)),
            dma((2, ranks - 1)),
            dma((2, ranks - 1)),
            dma((ranks,)),
            dma((ranks,)),
        ],
        compiler_params=remote(1),
        name="attend",
    )(x_all, gain, weights, out_weights, bias, cosine, sine, x, gain_two)
    return out[:6], out[6:]


def rejoin_kernel(ranks, plane_size, gain_row, gates, h, dz, router_t, a2, *refs):
    parts = refs[:ranks]
    dh, gathered, extra, g_send, g_recv = refs[ranks:]
    model = h.shape[1]
    spot = Spot(ranks, plane_size)
    meet([spot.ahead(s) for s in range(1, ranks)])
    total = parts[0][...]
    for i in range(1, ranks):
        total = total + parts[i][...].astype(F32)
    tail = total[:, model:]
    dgates = tail + pltpu.roll(tail, LANES // 2, 1)
    gate = gates[...]
    mean = jnp.sum(gate * dgates, axis=1, keepdims=True)
    d_logits = (gate * (dgates - mean)).astype(BF16)
    da2 = total[:, :model] + dot(d_logits, router_t[...])
    value = h[...]
    scale = lax.rsqrt(jnp.mean(value * value, axis=-1, keepdims=True) + EPSILON)
    normed = value * scale
    gain = router_t[gain_row : gain_row + 1, :].astype(F32)
    weighted = da2 * gain
    grad = dz[...] + scale * (
        weighted - normed * jnp.mean(weighted * normed, axis=-1, keepdims=True)
    )
    gathered[0] = grad.astype(BF16)
    dh[...] = grad
    line_out = LineGather(spot, gathered, g_send, g_recv)
    line_out.start(0)
    gain_grad = jnp.sum(da2 * normed, axis=0, keepdims=True)
    line = lax.broadcasted_iota(jnp.int32, (LANES, model), 0)
    extra[...] = jnp.where(line == gain_row, gain_grad, dot_tn(d_logits, a2[...]))
    for hop in range(line_out.hops):
        line_out.arrive(hop)
        if hop + 1 < line_out.hops:
            line_out.start(hop + 1)
    line_out.drain()


def rejoin(parts, gates, h, dz, router_t, a2, gain_row, plane_size):
    ranks = len(parts)
    dma = pltpu.SemaphoreType.DMA
    return pl.pallas_call(
        functools.partial(rejoin_kernel, ranks, plane_size, gain_row),
        in_specs=[VMEM] * (5 + ranks),
        out_specs=[VMEM] * 3,
        out_shape=[
            shape_of(h.shape, F32),
            shape_of((ranks,) + h.shape, BF16),
            shape_of((LANES, h.shape[1]), F32),
        ],
        scratch_shapes=[dma((2, ranks - 1)), dma((2, ranks - 1))],
        compiler_params=remote(2),
        name="rejoin",
    )(gates, h, dz, router_t, a2, *parts)


def last_kernel(ranks, plane_size, x, dh, gain, d_weights, d_rows, *refs):
    sums = refs[:ranks]
    out, columns_out, rows_out = refs[ranks : ranks + 3]
    (got, core_w, core_r, sum_w, sum_r, chip_w, chip_r, final) = refs[ranks + 3 : ranks + 11]
    r_send, r_recv, c_send, c_recv, p_send, p_recv, z_send, z_recv, local = refs[ranks + 11 :]
    spot = Spot(ranks, plane_size)
    chips, core, me = spot.chips, spot.core, spot.rank
    meet(
        [spot.ahead(s) for s in range(1, ranks)]
        + [spot.on_chip(spot.chip_ahead(k)) for k in range(1, chips)]
        + [spot.partner()]
    )
    z_copies = scatter_start(spot, sums, got, r_send, r_recv)
    pairs = ((0, d_weights, core_w, sum_w, chip_w), (1, d_rows, core_r, sum_r, chip_r))
    across = {}
    for k in range(chips):
        at = spot.chip_ahead(k)
        for which, src, buf, _, _ in pairs:
            across[k, which] = send(
                src.at[at, 1 - core],
                buf.at[k],
                c_send.at[which, k],
                c_recv.at[which, k],
                spot.partner(),
            )
    for k in list(range(1, chips)) + [0]:
        at = spot.chip_ahead(k)
        for which, src, buf, total, _ in pairs:
            across[k, which].wait()
            total[k] = (src[at, core].astype(F32) + buf[k].astype(F32)).astype(BF16)
    hops = {}
    for k in range(1, chips):
        for which, _, _, total, buf in pairs:
            hops[k, which] = send(
                total.at[k],
                buf.at[k - 1],
                p_send.at[which, k - 1],
                p_recv.at[which, k - 1],
                spot.on_chip(spot.chip_ahead(k)),
            )
    value = x[...]
    scale = lax.rsqrt(jnp.mean(value * value, axis=-1, keepdims=True) + EPSILON)
    normed = value * scale
    total = sums[0][...]
    for s in range(1, ranks):
        z_copies[s - 1].wait()
        total = total + got[s - 1].astype(F32)
    weighted = total * gain[...]
    grad = scale * (weighted - normed * jnp.mean(weighted * normed, axis=-1, keepdims=True))
    for k in range(1, chips):
        for which in range(2):
            hops[k, which].wait()
    value = sum_w[0].astype(F32)
    for k in range(1, chips):
        value = value + chip_w[k - 1].astype(F32)
    final[...] = value.astype(BF16)
    out[...] = dh[...] + grad
    value = sum_r[0].astype(F32)
    for k in range(1, chips):
        value = value + chip_r[k - 1].astype(F32)
    rows_out[...] = value
    kept = pltpu.make_async_copy(final.at[me], columns_out.at[me], local.at[0])
    kept.start()
    copies = [
        send(
            final.at[lax.rem(me + s, ranks)],
            columns_out.at[me],
            z_send.at[s - 1],
            z_recv.at[s - 1],
            spot.ahead(s),
        )
        for s in range(1, ranks)
    ]
    for copy in copies:
        copy.wait()
    kept.wait()


def last(x, dh, gain, d_weights, d_rows, sums):
    ranks = len(sums)
    chips, _, _, rows, columns = d_weights.shape
    dma = pltpu.SemaphoreType.DMA
    w_shape, r_shape = d_weights.shape[2:], d_rows.shape[2:]
    return pl.pallas_call(
        functools.partial(last_kernel, ranks, 2 * chips),
        in_specs=[VMEM] * (5 + ranks),
        out_specs=[VMEM] * 3,
        out_shape=[shape_of(x.shape, F32), shape_of(w_shape, BF16), shape_of(r_shape, F32)],
        scratch_shapes=[
            pltpu.VMEM((ranks - 1,) + x.shape, BF16),
            pltpu.VMEM((chips,) + w_shape, BF16),
            pltpu.VMEM((chips,) + r_shape, BF16),
            pltpu.VMEM((chips,) + w_shape, BF16),
            pltpu.VMEM((chips,) + r_shape, BF16),
            pltpu.VMEM((chips - 1,) + w_shape, BF16),
            pltpu.VMEM((chips - 1,) + r_shape, BF16),
            pltpu.VMEM(w_shape, BF16),
            dma((ranks - 1,)),
            dma((ranks - 1,)),
            dma((2, chips)),
            dma((2, chips)),
            dma((2, chips - 1)),
            dma((2, chips - 1)),
            dma((ranks - 1,)),
            dma((ranks - 1,)),
            dma((1,)),
        ],
        compiler_params=remote(3),
        name="last",
    )(x, dh, gain, d_weights, d_rows, *sums)


def piece_ids(position_index, starts):
    inside = (position_index[:, None] >= starts[None, :]) & (
        position_index[:, None] < starts[None, :] + PIECE
    )
    labels = jnp.arange(1, starts.shape[0] + 1, dtype=jnp.int32)[None, :]
    return jnp.sum(jnp.where(inside, labels, 0), axis=1, dtype=jnp.int32)


def on_device(
    inputs,
    cotangent,
    norm1_gain,
    w_query,
    key_projection,
    value_projection,
    w_output,
    norm2_gain,
    w_router,
    w_gate,
    w_up,
    w_down,
    routes,
    piece_starts,
):
    plane = Plane()
    ranks = lax.axis_size("expert")
    me = lax.axis_index("expert")
    rows, model = inputs.shape
    seq = rows * ranks
    weight_rows = w_query.shape[0]
    n_experts = w_router.shape[1]
    ff = w_gate.shape[2]
    kv_heads = KEY_VALUE_HEADS // ranks
    q_cols, kv_cols = kv_heads * GROUP * HEAD_WIDTH, kv_heads * HEAD_WIDTH
    rope_width = q_cols + kv_cols
    value_width = -(-kv_cols // LANES) * LANES
    columns = rope_width + value_width + LANES
    gain_one_row, gain_two_row = n_experts, n_experts + 1

    scale_one = lax.rsqrt(jnp.mean(inputs * inputs, axis=-1, keepdims=True) + EPSILON)
    x_own = (inputs * scale_one).astype(BF16)

    extra_cols = jnp.concatenate(
        [
            w_router,
            norm1_gain[:, None],
            norm2_gain[:, None],
            jnp.zeros((weight_rows, LANES - n_experts - 2), F32),
        ],
        axis=1,
    )
    by_rank = jnp.concatenate(
        [
            w_query.reshape(weight_rows, ranks, q_cols),
            key_projection.reshape(weight_rows, ranks, kv_cols),
            jnp.pad(
                value_projection.reshape(weight_rows, ranks, kv_cols),
                ((0, 0), (0, 0), (0, value_width - kv_cols)),
            ),
            jnp.broadcast_to(extra_cols[:, None, :], (weight_rows, ranks, LANES)),
        ],
        axis=2,
    ).astype(BF16)
    by_rank = jnp.transpose(by_rank, (1, 0, 2))

    axes = ("fsdp", "expert")
    total = plane.size * ranks
    move = [
        (j, (j % plane.size) * ranks + j // plane.size) for j in range(total)
    ]
    out_shard = lax.ppermute(w_output.astype(BF16), axes, move)

    lane_ids = jnp.arange(LANES, dtype=jnp.int32)
    routed = jnp.sum((routes[:, :, None] == lane_ids[None, None, :]).astype(F32), axis=1)
    grads_own = jnp.concatenate([cotangent, routed], axis=1).astype(BF16)

    core = plane.core.astype(jnp.int32)[None]
    keep, send, halves = pack_experts(core, w_gate, w_up, w_down, plane.size)
    got = plane.other_core(send)
    parts = [
        jnp.concatenate([jnp.where(plane.core == part, keep, got), halves[part][None]], axis=0)
        for part in range(2)
    ]
    by_rank, parts, out_shard, x_own, grads_own = lax.optimization_barrier(
        (by_rank, parts, out_shard, x_own, grads_own)
    )
    first = [plane.other_mid(parts[0])] + [
        plane.next_row(parts[1], s) for s in range(1, plane.rows)
    ]
    weights, out_weights, x_all, grads = gather_weights(
        by_rank, out_shard, x_own, grads_own, plane.size
    )
    first, weights = lax.optimization_barrier((first, weights))
    grads = grads.reshape(seq, grads.shape[2])
    found = {(0, 0, 0): parts[0], (0, 0, 1): parts[1], (0, 1, 0): first[0]}
    for s in range(1, plane.rows):
        found[s, 0, 1] = first[s]
        for mid in range(2):
            found[s, mid, 0] = plane.next_row(found[0, mid, 0], s)
    for s in range(plane.rows):
        found[s, 1, 1] = plane.other_mid(found[s, 0, 1])
    place, pieces = tuple(found.keys()), list(found.values())
    sources = [
        ((plane.row - s) % plane.rows) * 2 + (plane.mid + mid) % 2
        for s in range(plane.rows)
        for mid in range(2)
    ]
    where = jnp.stack([me] + sources).astype(jnp.int32)

    weights = weights.reshape(model, columns)
    out_weights = out_weights.reshape(q_cols, model)

    block_ids = jnp.arange(seq, dtype=jnp.int32) // rows
    places = ((me - block_ids) % ranks) * rows + jnp.arange(seq, dtype=jnp.int32) % rows
    ids = piece_ids(places, piece_starts[0])
    visible = (places[:, None] <= places[None, :]) | (
        (ids[:, None] == ids[None, :]) & (ids[None, :] > 0)
    )
    bias = jnp.where(visible, 0.0, NEG_FILL).astype(F32)
    half = HEAD_WIDTH // 2
    inverse = 10000.0 ** (-(jnp.arange(half, dtype=F32) * 2.0 / HEAD_WIDTH))
    angles = places.astype(F32)[:, None] * inverse[None, :]
    cosine = jnp.tile(jnp.cos(angles), (1, LANES // half))
    sine = jnp.tile(jnp.sin(angles), (1, LANES // half)) * jnp.where(
        lane_ids % HEAD_WIDTH < half, -1.0, 1.0
    )
    extra_t = weights[:, columns - LANES :].T
    gain_one = extra_t[gain_one_row : gain_one_row + 1].astype(F32)
    gain_two = extra_t[gain_two_row : gain_two_row + 1].astype(F32)
    kept, (mid_rows, a2, own_a2, other_a2) = attend(
        x_all,
        gain_one,
        weights,
        out_weights,
        bias,
        cosine,
        sine,
        inputs,
        gain_two,
        kv_heads,
        rope_width,
        plane.size,
    )

    other_grads = plane.other_core(grads)
    other_out, other_dx, _, *other_kept = experts(
        [other_a2.reshape(seq, model)], other_grads, extra_t, where, pieces, place, BF16
    )
    out_all, dx_all, gates, *own_kept = experts(
        [own_a2.reshape(seq, model)], grads, extra_t, where, pieces, place, F32
    )
    dx_all = dx_all + plane.other_core(other_dx).astype(F32)
    dxs = [
        dx_all[b * rows : (b + 1) * rows].astype(F32 if b == 0 else BF16) for b in range(ranks)
    ]
    dx_got = expert_scatter(dxs)
    chips = [
        ((plane.row + s) % plane.rows) * 2 + (plane.mid + mid) % 2
        for s in range(plane.rows)
        for mid in range(2)
    ]
    own_kept.insert(2, grads[:, :model])
    other_kept.insert(2, other_grads[:, :model])
    flat = expert_grads(
        jnp.stack(chips).astype(jnp.int32), own_kept, other_kept, plane.size, plane.rows
    )
    dx_got, flat = lax.optimization_barrier((dx_got, flat))
    by_row, by_mid = flat[: plane.rows], flat[plane.rows :]

    def add(first, *others):
        value = first.astype(F32)
        for v in others:
            value = value + v.astype(F32)
        return value.astype(BF16)

    steps = range(1, plane.rows)
    a_first = [plane.next_row(by_row[s], s) for s in steps]
    b_first = plane.other_mid(by_mid[1])

    dh, dh_stack, extra = rejoin(
        [dxs[0]] + dx_got, gates, mid_rows, cotangent, extra_t, a2, gain_two_row, plane.size
    )
    other_out = plane.other_core(other_out)
    dh_stack, other_out, out_all = lax.optimization_barrier((dh_stack, other_out, out_all))
    out_all = out_all + other_out.astype(F32)
    outs = [out_all[b * rows : (b + 1) * rows] for b in range(ranks)]
    outs = [outs[0]] + [v.astype(BF16) for v in outs[1:]]
    dh_stack, outs = lax.optimization_barrier((dh_stack, outs))
    out_got = expert_scatter(outs)

    d_weights, d_out_weights, da1 = attend_back(
        dh_stack,
        x_all,
        weights,
        out_weights,
        kept,
        bias,
        cosine,
        sine,
        extra,
        kv_heads,
        gain_one_row,
    )
    a_first, b_first, d_weights, out_got = lax.optimization_barrier(
        (a_first, b_first, d_weights, out_got)
    )
    a_sums = [add(by_row[0][mid], *[v[mid] for v in a_first]) for mid in range(2)]
    b_sums = [add(by_mid[0][s], b_first[s]) for s in range(plane.rows)]
    a_sums, b_sums, d_weights = lax.optimization_barrier((a_sums, b_sums, d_weights))
    a_got = plane.other_mid(a_sums[1])
    b_got = [plane.next_row(b_sums[s], s) for s in steps]
    chip_count = plane.size // 2
    input_grad, by_rank, out_part = last(
        inputs,
        dh,
        gain_one,
        d_weights.reshape(chip_count, 2, ranks, weight_rows, columns),
        d_out_weights.reshape(chip_count, 2, weight_rows, model),
        da1,
    )
    a_got, b_got, out_part = lax.optimization_barrier((a_got, b_got, out_part))
    b_kept = b_sums[0]
    if len(b_got) > 1:
        b_kept = add(b_kept, *b_got[:-1])
    b_got = b_got[-1]
    other = plane.other_core(
        jnp.where(
            plane.core == 0,
            b_kept[:2].astype(F32) + b_got[:2].astype(F32),
            a_sums[0][:2].astype(F32) + a_got[:2].astype(F32),
        ).astype(BF16)
    )
    gate_grad, up_grad, down_grad = finish(
        core, a_sums[0], a_got, b_kept, b_got, other, w_down.shape[1], model, plane.size
    )
    output = mid_rows + outs[0]
    for v in out_got:
        output = output + v.astype(F32)

    w_output_grad = lax.ppermute(
        out_part.astype(BF16), axes, [(b, a) for a, b in move]
    ).astype(F32)
    by_rank = by_rank.astype(F32)

    def columns_of(start, width):
        piece = by_rank[:, :, start : start + width]
        return jnp.transpose(piece, (1, 0, 2)).reshape(weight_rows, ranks * width)

    extra_grad = jnp.sum(by_rank[:, :, columns - LANES :], axis=0)
    return (
        output,
        input_grad,
        extra_grad[:, gain_one_row],
        columns_of(0, q_cols),
        columns_of(q_cols, kv_cols),
        columns_of(rope_width, kv_cols),
        w_output_grad,
        extra_grad[:, gain_two_row],
        extra_grad[:, :n_experts],
        gate_grad,
        up_grad,
        down_grad,
    )


def solution(mesh):
    both = ("fsdp", "expert")
    rows, flat, stack = P(both, None), P(both), P("expert", "fsdp", None)
    weights = (flat, rows, rows, rows, rows, flat, rows, stack, stack, stack)
    return jax.shard_map(
        on_device,
        mesh=mesh,
        in_specs=(rows, rows) + weights + (rows, P("fsdp", None)),
        out_specs=(rows, rows) + weights,
        check_vma=False,
    )
```

```python
import functools

import jax
import jax.numpy as jnp
from jax import lax
from jax.experimental import pallas as pl
from jax.experimental.pallas import tpu as pltpu
from jax.sharding import PartitionSpec as P

QUERY_HEADS = 24
KEY_VALUE_HEADS = 8
GROUP = QUERY_HEADS // KEY_VALUE_HEADS
HEAD_WIDTH = 64
PIECE = 256
LANES = 128
DEVICE_ROWS = 128
EPSILON = 1e-05
NEG_FILL = -1e30
SCORE_SCALE = HEAD_WIDTH ** (-0.5)
F32 = jnp.float32
BF16 = jnp.bfloat16

VMEM = pl.BlockSpec(memory_space=pltpu.VMEM)
SMEM = pl.BlockSpec(memory_space=pltpu.SMEM)
ANY = pl.BlockSpec(memory_space=pl.ANY)
MESH = pl.DeviceIdType.MESH


def dot(a, b):
    return lax.dot_general(a, b, (((1,), (0,)), ((), ())), preferred_element_type=F32)


def dot_nt(a, b):
    return lax.dot_general(a, b, (((1,), (1,)), ((), ())), preferred_element_type=F32)


def dot_tn(a, b):
    return lax.dot_general(a, b, (((0,), (0,)), ((), ())), preferred_element_type=F32)


def shape_of(dims, dtype):
    return jax.ShapeDtypeStruct(tuple(dims), dtype)


def lasting(us):
    return pl.CostEstimate(flops=us * 10**9, bytes_accessed=us * 10**6, transcendentals=0)


def params(**kw):
    return pltpu.CompilerParams(vmem_limit_bytes=60 * 1024 * 1024, **kw)


class Plane:
    def __init__(self):
        self.size = lax.axis_size("fsdp")
        self.rows = self.size // 4
        index = lax.axis_index("fsdp")
        self.index = index
        self.core = index % 2
        self.mid = (index // 2) % 2
        self.row = index // 4

    def other_core(self, x):
        return lax.ppermute(x, "fsdp", [(i, i ^ 1) for i in range(self.size)])

    def other_mid(self, x):
        return lax.ppermute(x, "fsdp", [(i, i ^ 2) for i in range(self.size)])

    def next_row(self, x, step):
        return lax.ppermute(
            x, "fsdp", [(i, (i // 4 + step) % self.rows * 4 + i % 4) for i in range(self.size)]
        )


def expert_shift(x, step):
    count = lax.axis_size("expert")
    return lax.ppermute(x, "expert", [(i, (i + step) % count) for i in range(count)])


def expert_scatter(blocks):
    count = lax.axis_size("expert")
    return [expert_shift(blocks[s], count - s) for s in range(1, count)]


def chooser(width, blocks, part, dtype=BF16):
    n = width // blocks
    line = lax.broadcasted_iota(jnp.int32, (width // 2, width), 0)
    column = lax.broadcasted_iota(jnp.int32, (width // 2, width), 1)
    want = (2 * (line // n) + part) * n + line % n
    return jnp.where(column == want, 1.0, 0.0).astype(dtype)


def swap_halves(x):
    lane = lax.broadcasted_iota(jnp.int32, x.shape, 1)
    return jnp.where(
        lane % HEAD_WIDTH < HEAD_WIDTH // 2, pltpu.roll(x, LANES - 32, 1), pltpu.roll(x, 32, 1)
    )


def head_slice(ref, start):
    return ref[:, start : start + HEAD_WIDTH]


def experts_kernel(blocks, pieces, place, row_block, *refs):
    a2_in = refs[:blocks]
    grads_in, router_t, where_ref = refs[blocks : blocks + 3]
    piece_refs = refs[blocks + 3 : blocks + 3 + pieces]
    (out_all, dx_all, gates_out, a2_t, hidden_t, d_gate, d_up) = refs[
        blocks + 3 + pieces : blocks + 10 + pieces
    ]
    (a2, gate_w, up_w, down_w, out_sum, dx_sum, gates, dgates, in_sem, w_sem) = refs[
        blocks + 10 + pieces :
    ]
    step, steps = pl.program_id(0), pl.num_programs(0)
    rows = a2_in[0].shape[0]
    seq, model = a2.shape
    depth, width = piece_refs[0].shape[2], gate_w.shape[2]
    down_rows = depth * width // model
    slot = lax.rem(step, 2)

    def fetch(e, to):
        for i, (row_step, mid, part) in enumerate(place):
            source = where_ref[1 + row_step * 2 + mid] * 2 + part
            at = pl.multiple_of(source * depth, 32)
            for which, buf in ((0, gate_w), (1, up_w)):
                pltpu.make_async_copy(
                    piece_refs[i].at[which, e], buf.at[to, pl.ds(at, depth)], w_sem.at[which, to]
                ).start()
            at = pl.multiple_of(source * down_rows, 16)
            for j in range(model // width):
                pltpu.make_async_copy(
                    piece_refs[i].at[2, e, pl.ds(j * down_rows, down_rows)],
                    down_w.at[to, pl.ds(at, down_rows), pl.ds(j * width, width)],
                    w_sem.at[2, to],
                ).start()

    @pl.when(step == 0)
    def _():
        for b in range(blocks):
            pltpu.make_async_copy(
                a2_in[b], a2.at[pl.ds(b * rows, rows)], in_sem.at[0]
            ).start()
        fetch(0, 0)
        pltpu.make_async_copy(a2, a2, in_sem.at[0]).wait()
        logits = dot_nt(a2[...], router_t[...])
        routed = grads_in[:, model:].astype(F32) > 0.5
        top = jnp.max(jnp.where(routed, logits, NEG_FILL), axis=1, keepdims=True)
        weight = jnp.where(routed, jnp.exp(jnp.where(routed, logits, top) - top), 0.0)
        gates[...] = weight / jnp.sum(weight, axis=1, keepdims=True)
        gates_out[...] = gates[: gates_out.shape[0], :]
        dgates[...] = jnp.zeros_like(dgates)
        a2_t[...] = a2[...].T

    @pl.when(step + 1 < steps)
    def _():
        fetch(step + 1, 1 - slot)

    for which, buf in ((0, gate_w), (1, up_w), (2, down_w)):
        pltpu.make_async_copy(buf.at[slot], buf.at[slot], w_sem.at[which, slot]).wait()

    mine = where_ref[0] * steps + step

    def block(i, carry):
        at = pl.ds(pl.multiple_of(i * row_block, row_block), row_block)
        left = a2[at, :]
        gate_lin = dot(left, gate_w[slot])
        up_lin = dot(left, up_w[slot])
        back = dot_nt(grads_in[at, :model], down_w[slot])
        lane = lax.broadcasted_iota(jnp.int32, (row_block, LANES), 1)
        here = lane == mine
        gate = jnp.sum(jnp.where(here, gates[at, :], 0.0), axis=1, keepdims=True)
        sig = 1.0 / (1.0 + jnp.exp(-gate_lin))
        silu = gate_lin * sig
        hidden = silu * up_lin
        dgates[at, :] += jnp.where(here, jnp.sum(hidden * back, axis=1, keepdims=True), 0.0)
        hidden_low = (hidden * gate).astype(BF16)
        d_hidden = back * gate
        d_gate_low = (d_hidden * up_lin * (sig + silu * (1.0 - sig))).astype(BF16)
        d_up_low = (d_hidden * silu).astype(BF16)
        d_gate[at, :] = d_gate_low
        d_up[at, :] = d_up_low
        hidden_t[0, :, at] = hidden_low.T
        out_new = dot(hidden_low, down_w[slot])
        dx_new = dot_nt(d_gate_low, gate_w[slot]) + dot_nt(d_up_low, up_w[slot])

        @pl.when(step == 0)
        def _():
            out_sum[at, :] = out_new
            dx_sum[at, :] = dx_new

        @pl.when(step > 0)
        def _():
            out_sum[at, :] += out_new
            dx_sum[at, :] += dx_new

        return carry

    lax.fori_loop(0, seq // row_block, block, 0)

    @pl.when(step == steps - 1)
    def _():
        high = dgates[...].astype(BF16).astype(F32)
        low = dgates[...] - high
        lane = lax.broadcasted_iota(jnp.int32, high.shape, 1)
        tail = jnp.where(lane < LANES // 2, high, pltpu.roll(low, LANES // 2, 1))
        out_all[...] = out_sum[...].astype(out_all.dtype)
        dx_all[:, :model] = dx_sum[...].astype(dx_all.dtype)
        dx_all[:, model:] = tail.astype(dx_all.dtype)


def experts(a2_blocks, grads, router_t, where, pieces, place, dtype):
    blocks = len(a2_blocks)
    rows, model = a2_blocks[0].shape
    seq = rows * blocks
    local, depth, width = pieces[0].shape[1:]
    outs = [
        shape_of((seq, model), dtype),
        shape_of((seq, model + LANES), dtype),
        shape_of((DEVICE_ROWS, LANES), F32),
        shape_of((model, seq), BF16),
        shape_of((local, width, seq), BF16),
        shape_of((seq, local * width), BF16),
        shape_of((seq, local * width), BF16),
    ]
    whole = lambda dims: pl.BlockSpec(
        dims, lambda e: (0,) * len(dims), pipeline_mode=pl.Buffered(1)
    )
    out_specs = (
        [whole(o.shape) for o in outs[:4]]
        + [pl.BlockSpec((1, width, seq), lambda e: (e, 0, 0))]
        + [pl.BlockSpec((seq, width), lambda e: (0, e))] * 2
    )
    return pl.pallas_call(
        functools.partial(experts_kernel, blocks, len(pieces), place, 256),
        grid=(local,),
        in_specs=[ANY] * blocks
        + [whole(grads.shape), whole(router_t.shape), SMEM]
        + [ANY] * len(pieces),
        out_specs=out_specs,
        out_shape=outs,
        scratch_shapes=[
            pltpu.VMEM((seq, model), BF16),
            pltpu.VMEM((2, model, width), BF16),
            pltpu.VMEM((2, model, width), BF16),
            pltpu.VMEM((2, width, model), BF16),
            pltpu.VMEM((seq, model), F32),
            pltpu.VMEM((seq, model), F32),
            pltpu.VMEM((seq, LANES), F32),
            pltpu.VMEM((seq, LANES), F32),
            pltpu.SemaphoreType.DMA((1,)),
            pltpu.SemaphoreType.DMA((3, 2)),
        ],
        compiler_params=params(dimension_semantics=("arbitrary",)),
        name="experts",
    )(*a2_blocks, grads, router_t, where, *pieces)


def expert_grads_kernel(plane_rows, depth, down_rows, where_ref, *refs):
    (a2_t0, a2_t1, hid0, hid1, grads0, grads1, dg0, dg1, du0, du1) = refs[:10]
    row_outs, mid_outs = refs[10 : 10 + plane_rows], refs[10 + plane_rows : 12 + plane_rows]
    down_sum = refs[12 + plane_rows]
    model, width = a2_t0.shape[0], dg0.shape[1]
    down_sum[...] = (dot(hid0[0], grads0[...]) + dot(hid1[0], grads1[...])).astype(BF16)
    for s in range(plane_rows):
        for mid in range(2):
            source = where_ref[2 * s + mid]
            at = pl.ds(pl.multiple_of(source * 2 * depth, 32), 2 * depth)
            left0, left1 = a2_t0[at, :], a2_t1[at, :]
            gate = (dot(left0, dg0[...]) + dot(left1, dg1[...])).astype(BF16)
            up = (dot(left0, du0[...]) + dot(left1, du1[...])).astype(BF16)
            for part, out in ((0, row_outs[s].at[mid]), (1, mid_outs[mid].at[s])):
                out[0, 0] = gate[part * depth : (part + 1) * depth]
                out[1, 0] = up[part * depth : (part + 1) * depth]
                at = pl.ds(pl.multiple_of((source * 2 + part) * down_rows, 16), down_rows)
                down = down_sum[at, :]
                for j in range(model // width):
                    out[2, 0, j * down_rows : (j + 1) * down_rows, :] = down[
                        :, j * width : (j + 1) * width
                    ]


def expert_grads(where, first, second, plane_size, plane_rows):
    model, seq = first[0].shape
    local, width = first[1].shape[:2]
    depth, down_rows = model // plane_size, width // plane_size
    counts = [2] * plane_rows + [plane_rows] * 2
    once = lambda dims: pl.BlockSpec(dims, lambda e: (0, 0), pipeline_mode=pl.Buffered(1))
    specs = [
        once((model, seq)),
        pl.BlockSpec((1, width, seq), lambda e: (e, 0, 0)),
        once((seq, model)),
        pl.BlockSpec((seq, width), lambda e: (0, e)),
        pl.BlockSpec((seq, width), lambda e: (0, e)),
    ]
    operands = [v for pair in zip(first, second) for v in pair]
    return pl.pallas_call(
        functools.partial(expert_grads_kernel, plane_rows, depth, down_rows),
        grid=(local,),
        in_specs=[SMEM] + [spec for spec in specs for _ in range(2)],
        out_specs=[
            pl.BlockSpec((n, 3, 1, depth, width), lambda e: (0, 0, e, 0, 0)) for n in counts
        ],
        out_shape=[shape_of((n, 3, local, depth, width), BF16) for n in counts],
        scratch_shapes=[pltpu.VMEM((width, model), BF16)],
        compiler_params=params(),
        cost_estimate=lasting(18),
        name="expert_grads",
    )(where, *operands)


def finish_kernel(blocks, count_a, count_b, core, *refs):
    parts_a, parts_b = refs[:count_a], refs[count_a : count_a + count_b]
    other, gate, up, down, choose = refs[count_a + count_b :]
    width, wide = gate.shape[2], other.shape[3]

    @pl.when(pl.program_id(0) == 0)
    def _():
        choose[0] = chooser(width, blocks, core[0])
        choose[1] = chooser(width, blocks, 1 - core[0])

    mine, theirs = choose[0], choose[1]
    first = core[0] == 0

    def total(parts, place):
        value = parts[0][place, 0].astype(F32)
        for part in parts[1:]:
            value = value + part[place, 0].astype(F32)
        return value

    for place, out in ((0, gate), (1, up)):
        kept = jnp.where(first, total(parts_a[:-1], place), total(parts_b[:-1], place))
        got = jnp.where(
            first, parts_a[-1][place, 0].astype(F32), parts_b[-1][place, 0].astype(F32)
        )
        out[0] = (
            dot(kept.astype(BF16), mine)
            + dot(got.astype(BF16), mine)
            + dot(other[place, 0], theirs)
        )
    rows = down.shape[1] // 2
    for part, parts in ((0, parts_a), (1, parts_b)):
        value = total(parts, 2)
        for j in range(value.shape[0] // rows):
            down[0, part * rows : (part + 1) * rows, j * wide : (j + 1) * wide] = value[
                j * rows : (j + 1) * rows
            ]


def finish(core, parts_a, parts_b, other, down_rows, model, blocks):
    local, depth, wide = other.shape[1:]
    block = pl.BlockSpec((3, 1, depth, wide), lambda e: (0, e, 0, 0))
    front = pl.BlockSpec((None, 3, 1, depth, wide), lambda e: (0, 0, e, 0, 0))
    outs = [
        shape_of((local, depth, 2 * wide), F32),
        shape_of((local, depth, 2 * wide), F32),
        shape_of((local, down_rows, model), F32),
    ]
    parts = list(parts_a) + list(parts_b)
    return pl.pallas_call(
        functools.partial(finish_kernel, blocks, len(parts_a), len(parts_b)),
        grid=(local,),
        in_specs=[SMEM]
        + [front if v.ndim == 5 else block for v in parts]
        + [pl.BlockSpec((2, 1, depth, wide), lambda e: (0, e, 0, 0))],
        out_specs=[pl.BlockSpec((1,) + o.shape[1:], lambda e: (e, 0, 0)) for o in outs],
        out_shape=outs,
        scratch_shapes=[pltpu.VMEM((2, wide, 2 * wide), BF16)],
        name="finish",
    )(core, *parts, other)


def attend_back_kernel(blocks, kv_heads, gain_row, *refs):
    dh_ref, x_all = refs[:2]
    (weights, out_weights, a1, qk, val, mixed, maxes, inverse, bias, cosine, sine, extra) = refs[2:14]
    d_weights, d_out_weights = refs[14:16]
    sums = refs[16 : blocks + 16]
    grads, d_mixed, dq_t, d_qk, d_lin = refs[blocks + 16 :]
    rows = x_all.shape[1]
    rope_width, value_width = qk.shape[1], val.shape[1]
    q_width = kv_heads * GROUP * HEAD_WIDTH
    for b in range(blocks):
        grads[b * rows : (b + 1) * rows, :] = dh_ref[b]
    d_mixed[...] = dot_nt(grads[...], out_weights[...]).astype(BF16)
    d_out_weights[...] = dot_tn(mixed[...], grads[...]).astype(BF16)
    if value_width > kv_heads * HEAD_WIDTH:
        d_lin[:, rope_width:] = jnp.zeros((d_lin.shape[0], value_width), BF16)
    for g in range(kv_heads):
        key = head_slice(qk, q_width + g * HEAD_WIDTH)
        key_t = key.T
        value = head_slice(val, g * HEAD_WIDTH)
        d_key, d_value = None, None
        for j in range(GROUP):
            h = g * GROUP + j
            query = head_slice(qk, h * HEAD_WIDTH)
            grad = head_slice(d_mixed, h * HEAD_WIDTH)
            scores = dot_nt(key, query) * SCORE_SCALE + bias[...]
            prob = jnp.exp(scores - maxes[h : h + 1, :]) * inverse[h : h + 1, :]
            d_prob = dot_nt(value, grad)
            inner = jnp.sum(prob * d_prob, axis=0, keepdims=True)
            d_scores = (prob * (d_prob - inner)).astype(BF16)
            dk = dot(d_scores, query)
            dv = dot(prob.astype(BF16), grad)
            d_key = dk if d_key is None else d_key + dk
            d_value = dv if d_value is None else d_value + dv
            dq_t[h * HEAD_WIDTH : (h + 1) * HEAD_WIDTH, :] = dot(key_t, d_scores)
        start = q_width + g * HEAD_WIDTH
        d_qk[:, start : start + HEAD_WIDTH] = d_key * SCORE_SCALE
        start = rope_width + g * HEAD_WIDTH
        d_lin[:, start : start + HEAD_WIDTH] = d_value.astype(BF16)
    d_qk[:, :q_width] = dq_t[...].T * SCORE_SCALE
    for c in range(rope_width // LANES):
        at = slice(c * LANES, (c + 1) * LANES)
        x = d_qk[:, at]
        d_lin[:, at] = (x * cosine[...] - swap_halves(x) * sine[...]).astype(BF16)
    total = dot_nt(d_lin[...], weights[:, : rope_width + value_width])
    gain_grad = None
    for b in range(blocks):
        part = total[b * rows : (b + 1) * rows, :]
        sums[b][...] = part.astype(sums[b].dtype)
        new = jnp.sum(part * x_all[b].astype(F32), axis=0, keepdims=True)
        gain_grad = new if gain_grad is None else gain_grad + new
    d_weights[:, : rope_width + value_width] = dot_tn(a1[...], d_lin[...]).astype(BF16)
    line = lax.broadcasted_iota(jnp.int32, extra.shape, 0)
    tail = jnp.where(line == gain_row, gain_grad, extra[...])
    d_weights[:, rope_width + value_width :] = tail.T.astype(BF16)


def attend_back(
    dh_stack, x_all, weights, out_weights, kept, bias, cosine, sine, extra, kv_heads, gain_row
):
    blocks, rows, model = dh_stack.shape
    seq = rows * blocks
    q_width = out_weights.shape[0]
    rope_width, value_width = kept[1].shape[1], kept[2].shape[1]
    outs = [shape_of(weights.shape, BF16), shape_of(out_weights.shape, BF16)] + [
        shape_of((rows, model), F32 if b == 0 else BF16) for b in range(blocks)
    ]
    out = pl.pallas_call(
        functools.partial(attend_back_kernel, blocks, kv_heads, gain_row),
        in_specs=[VMEM] * 14,
        out_specs=[VMEM] * len(outs),
        out_shape=outs,
        scratch_shapes=[
            pltpu.VMEM((seq, model), BF16),
            pltpu.VMEM((seq, q_width), BF16),
            pltpu.VMEM((q_width, seq), F32),
            pltpu.VMEM((seq, rope_width), F32),
            pltpu.VMEM((seq, rope_width + value_width), BF16),
        ],
        compiler_params=params(),
        cost_estimate=lasting(16),
        name="attend_back",
    )(dh_stack, x_all, weights, out_weights, *kept, bias, cosine, sine, extra)
    return out[0], out[1], out[2:]


class Spot:
    def __init__(self, ranks, plane_size):
        self.ranks, self.chips = ranks, plane_size // 2
        self.rank = lax.axis_index("expert")
        self.index = lax.axis_index("fsdp")
        self.chip = self.index // 2
        self.core = self.index % 2

    def behind(self, s):
        return {"expert": lax.rem(self.rank - s + self.ranks, self.ranks)}

    def ahead(self, s):
        return {"expert": lax.rem(self.rank + s, self.ranks)}

    def partner(self):
        return {"fsdp": self.chip * 2 + (1 - self.core)}

    def chip_ahead(self, k):
        return lax.rem(self.chip + k, self.chips)

    def chip_behind(self, k):
        return lax.rem(self.chip - k + self.chips, self.chips)

    def on_chip(self, chip):
        return {"fsdp": chip * 2 + self.core}


def greet(peers):
    barrier = pltpu.get_barrier_semaphore()
    for peer in peers:
        pl.semaphore_signal(barrier, inc=1, device_id=peer, device_id_type=MESH)


def await_peers(peers):
    pl.semaphore_wait(pltpu.get_barrier_semaphore(), len(peers))


def meet(peers):
    greet(peers)
    await_peers(peers)


def send(src, dst, send_sem, recv_sem, peer):
    copy = pltpu.make_async_remote_copy(
        src_ref=src,
        dst_ref=dst,
        send_sem=send_sem,
        recv_sem=recv_sem,
        device_id=peer,
        device_id_type=MESH,
    )
    copy.start()
    return copy


def remote(collective_id):
    return params(collective_id=collective_id, has_side_effects=True)


def pack_experts(spot, w_gate, w_up, w_down, held, outgoing):
    local, width = w_gate.shape[0], w_gate.shape[2]
    mine = chooser(width, 2 * spot.chips, spot.core)
    theirs = chooser(width, 2 * spot.chips, 1 - spot.core)
    rows, wide = w_down.shape[1] // 2, width // 2

    def one(e, carry):
        for place, ref in ((0, w_gate), (1, w_up)):
            value = ref[e].astype(BF16)
            kept = dot_nt(value, mine).astype(BF16)
            for part in range(2):

                @pl.when(spot.core == part)
                def _():
                    held[part][place, e] = kept

            outgoing[place, e] = dot_nt(value, theirs).astype(BF16)
        value = w_down[e].astype(BF16)
        for part in range(2):
            for j in range(value.shape[1] // wide):
                held[part][2, e, j * rows : (j + 1) * rows] = value[
                    part * rows : (part + 1) * rows, j * wide : (j + 1) * wide
                ]
        return carry

    lax.fori_loop(0, local, one, 0)


def gather_weights_kernel(ranks, plane_size, *refs):
    by_rank, rows_in, x_in, grads_in, w_gate, w_up, w_down = refs[:7]
    weights, out_rows, x_all, grads_all, parts_a, parts_b, got_a, got_b = refs[7:15]
    held_a, held_b, outgoing = refs[15:18]
    z_send, z_recv, p_send, p_recv, c_send, c_recv, local, e_send, e_recv = refs[18:27]
    x_send, x_recv, grads_send, grads_recv = refs[27:]
    spot = Spot(ranks, plane_size)
    f, me, chips, core = spot.index, spot.rank, spot.chips, spot.core
    others = range(1, ranks)
    kept = [
        pltpu.make_async_copy(by_rank.at[me], weights.at[f, me], local.at[0]),
        pltpu.make_async_copy(rows_in, out_rows.at[f], local.at[1]),
        pltpu.make_async_copy(x_in, x_all.at[0], local.at[2]),
        pltpu.make_async_copy(grads_in, grads_all.at[0], local.at[3]),
    ]
    for copy in kept:
        copy.start()
    meet(
        [spot.ahead(s) for s in others]
        + [spot.on_chip(spot.chip_ahead(k)) for k in range(1, chips)]
        + [spot.partner()]
    )
    z_copies = [
        send(
            by_rank.at[lax.rem(me + s, ranks)],
            weights.at[f, me],
            z_send.at[s - 1],
            z_recv.at[s - 1],
            spot.ahead(s),
        )
        for s in others
    ]
    lines = [
        LineGather(spot, x_all, x_send, x_recv),
        LineGather(spot, grads_all, grads_send, grads_recv),
    ]

    def spread(which, src, buf):
        return [
            send(
                src,
                buf.at[f],
                p_send.at[which, k - 1],
                p_recv.at[which, k - 1],
                spot.on_chip(spot.chip_ahead(k)),
            )
            for k in range(1, chips)
        ] + [send(src, buf.at[f], c_send.at[which, 0], c_recv.at[which, 0], spot.partner())]

    row_copies = spread(1, rows_in, out_rows)
    for copy in kept:
        copy.wait()
    for line in lines:
        line.start(0)

    pack_experts(spot, w_gate, w_up, w_down, (held_a, held_b), outgoing)

    def swap(part, held):
        return pltpu.make_async_remote_copy(
            src_ref=outgoing,
            dst_ref=held.at[pl.ds(0, 2)],
            send_sem=e_send.at[0],
            recv_sem=e_recv.at[0],
            device_id=spot.partner(),
            device_id_type=MESH,
        )

    for part, held in ((0, held_a), (1, held_b)):

        @pl.when(core == part)
        def _():
            swap(part, held).start()

    for copy in z_copies:
        copy.wait()
    weight_copies = spread(0, weights.at[f], weights)
    for part, held in ((0, held_a), (1, held_b)):

        @pl.when(core == part)
        def _():
            swap(part, held).wait_send()

        @pl.when(core == 1 - part)
        def _():
            swap(part, held).wait_recv()

    row, mid = spot.chip // 2, lax.rem(spot.chip, 2)
    expert_copies = [
        send(held_a, got_a, e_send.at[1], e_recv.at[1], spot.on_chip(row * 2 + (1 - mid)))
    ] + [
        send(
            held_b,
            got_b.at[s - 1],
            e_send.at[1 + s],
            e_recv.at[1 + s],
            spot.on_chip(lax.rem(row + s, chips // 2) * 2 + mid),
        )
        for s in range(1, chips // 2)
    ]
    stores = [
        pltpu.make_async_copy(held_a, parts_a, local.at[4]),
        pltpu.make_async_copy(held_b, parts_b, local.at[5]),
    ]
    for copy in stores:
        copy.start()
    waits = []
    for hop in range(ranks - 1):
        for line in lines:
            line.arrive(hop)
            if hop + 1 < line.hops:
                line.start(hop + 1)
    for k in range(1, chips):
        source = spot.chip_behind(k) * 2 + core
        for which, copies, buf in ((1, row_copies, out_rows), (0, weight_copies, weights)):
            copies[k - 1].wait()
            waits.append(
                send(
                    buf.at[source],
                    buf.at[source],
                    c_send.at[which, k],
                    c_recv.at[which, k],
                    spot.partner(),
                )
            )
    row_copies[-1].wait()
    weight_copies[-1].wait()
    for copy in waits + stores + expert_copies:
        copy.wait()
    for line in lines:
        line.drain()


def gather_weights(by_rank, rows_in, x_in, grads_in, w_gate, w_up, w_down, plane_size):
    ranks, rows, columns = by_rank.shape
    chips = plane_size // 2
    local, depth, width = w_gate.shape
    dma = pltpu.SemaphoreType.DMA
    half = (local, depth, width // 2)
    return pl.pallas_call(
        functools.partial(gather_weights_kernel, ranks, plane_size),
        in_specs=[VMEM] * 7,
        out_specs=[VMEM] * 4 + [ANY] * 4,
        out_shape=[
            shape_of((plane_size, ranks, rows, columns), BF16),
            shape_of((plane_size,) + rows_in.shape, BF16),
            shape_of((ranks,) + x_in.shape, BF16),
            shape_of((ranks,) + grads_in.shape, BF16),
            shape_of((3,) + half, BF16),
            shape_of((3,) + half, BF16),
            shape_of((3,) + half, BF16),
            shape_of((chips // 2 - 1, 3) + half, BF16),
        ],
        scratch_shapes=[
            pltpu.VMEM((3,) + half, BF16),
            pltpu.VMEM((3,) + half, BF16),
            pltpu.VMEM((2,) + half, BF16),
            dma((ranks - 1,)),
            dma((ranks - 1,)),
            dma((2, chips - 1)),
            dma((2, chips - 1)),
            dma((2, chips)),
            dma((2, chips)),
            dma((6,)),
            dma((1 + chips // 2,)),
            dma((1 + chips // 2,)),
        ]
        + [dma((2, ranks - 1))] * 4,
        compiler_params=remote(0),
        name="gather_weights",
    )(by_rank, rows_in, x_in, grads_in, w_gate, w_up, w_down)


def scatter_start(spot, refs, buf, send_sem, recv_sem):
    return [
        send(refs[s], buf.at[s - 1], send_sem.at[s - 1], recv_sem.at[s - 1], spot.behind(s))
        for s in range(1, spot.ranks)
    ]


class LineGather:
    def __init__(self, spot, buf, send_sem, recv_sem, part=0, parts=1):
        self.spot, self.buf, self.sems = spot, buf, (send_sem, recv_sem)
        count = buf.shape[1] // parts
        self.rows = pl.ds(part * count, count)
        me, n = spot.rank, spot.ranks
        self.hops = n - 1
        self.sends = [(me - h >= 0) & (me + 1 < n) for h in range(n - 1)], [
            (me + h < n) & (me >= 1) for h in range(n - 1)
        ]
        self.gets = [me - 1 - h >= 0 for h in range(n - 1)], [
            me + 1 + h < n for h in range(n - 1)
        ]

    def slots(self, way, h):
        n = self.spot.ranks
        return (h, h + 1) if way == 0 else ((n - h) % n, n - h - 1)

    def copy(self, way, h):
        source, target = self.slots(way, h)
        return pltpu.make_async_remote_copy(
            src_ref=self.buf.at[source, self.rows],
            dst_ref=self.buf.at[target, self.rows],
            send_sem=self.sems[0].at[way, h],
            recv_sem=self.sems[1].at[way, h],
            device_id=self.spot.ahead(1) if way == 0 else self.spot.behind(1),
            device_id_type=MESH,
        )

    def start(self, h):
        for way in range(2):

            @pl.when(self.sends[way][h])
            def _():
                self.copy(way, h).start()

    def arrive(self, h):
        for way in range(2):

            @pl.when(self.gets[way][h])
            def _():
                self.copy(way, h).wait_recv()

    def passed(self, h, then):
        for way in range(2):

            @pl.when(self.gets[way][h])
            def _():
                then(self.slots(way, h)[1])

    def drain(self):
        for h in range(self.hops):
            for way in range(2):

                @pl.when(self.sends[way][h])
                def _():
                    self.copy(way, h).wait_send()


def half_lines(spot, buf, send_sem, recv_sem):
    return [LineGather(spot, buf, send_sem.at[k], recv_sem.at[k], k, 2) for k in range(2)]


def attend_kernel(ranks, plane_size, kv_heads, gain_row, *refs):
    x_all, weights, out_weights, bias, cosine, sine, x = refs[:7]
    (extra_t, a1, qk, val, mixed, maxes, inverse, h_out, a2, gathered, other) = refs[7:18]
    mixed_t, sums, got, r_send, r_recv, g_send, g_recv, c_send, c_recv = refs[18:]
    extra_t[...] = weights[:, weights.shape[1] - LANES :].T
    gain = extra_t[gain_row : gain_row + 1, :].astype(F32)
    gain_two = extra_t[gain_row + 1 : gain_row + 2, :].astype(F32)
    spot = Spot(ranks, plane_size)
    peers = [spot.ahead(s) for s in range(1, ranks)] + [spot.partner()]
    greet(peers)
    rows = x_all.shape[1]
    rope_width = qk.shape[1]
    q_width = kv_heads * GROUP * HEAD_WIDTH
    for b in range(ranks):
        a1[b * rows : (b + 1) * rows, :] = (x_all[b].astype(F32) * gain).astype(BF16)
    linear = dot(a1[...], weights[:, : rope_width + val.shape[1]])
    for c in range(rope_width // LANES):
        part = linear[:, c * LANES : (c + 1) * LANES]
        qk[:, c * LANES : (c + 1) * LANES] = (
            part * cosine[...] + swap_halves(part) * sine[...]
        ).astype(BF16)
    val[...] = linear[:, rope_width:].astype(BF16)
    for g in range(kv_heads):
        key = head_slice(qk, q_width + g * HEAD_WIDTH)
        value_t = head_slice(val, g * HEAD_WIDTH).T
        for j in range(GROUP):
            h = g * GROUP + j
            scores = dot_nt(key, head_slice(qk, h * HEAD_WIDTH)) * SCORE_SCALE + bias[...]
            top = jnp.max(scores, axis=0, keepdims=True)
            weight = jnp.exp(scores - top)
            inv = 1.0 / jnp.sum(weight, axis=0, keepdims=True)
            maxes[h : h + 1, :] = top
            inverse[h : h + 1, :] = inv
            mixed_t[h * HEAD_WIDTH : (h + 1) * HEAD_WIDTH, :] = dot(
                value_t, (weight * inv).astype(BF16)
            )
    mixed[...] = mixed_t[...].T.astype(BF16)
    await_peers(peers)
    total = dot(mixed[...], out_weights[...])
    for b in range(1, ranks):
        sums[b - 1] = total[b * rows : (b + 1) * rows, :].astype(BF16)
    copies = scatter_start(
        spot, [None] + [sums.at[s - 1] for s in range(1, ranks)], got, r_send, r_recv
    )
    total = x[...] + total[:rows, :]
    for s in range(1, ranks):
        copies[s - 1].wait()
        total = total + got[s - 1].astype(F32)
    scale = lax.rsqrt(jnp.mean(total * total, axis=-1, keepdims=True) + EPSILON)
    low = (total * scale * gain_two).astype(BF16)
    gathered[0] = low
    lines = half_lines(spot, gathered, g_send, g_recv)
    for line in lines:
        line.start(0)

    def across(s, part):
        return pltpu.make_async_remote_copy(
            src_ref=gathered.at[s, lines[part].rows],
            dst_ref=other.at[s, lines[part].rows],
            send_sem=c_send.at[part, s],
            recv_sem=c_recv.at[part, s],
            device_id=spot.partner(),
            device_id_type=MESH,
        )

    for part in range(2):
        across(0, part).start()
    a2[...] = low
    h_out[...] = total
    for hop in range(ranks - 1):
        for part, line in enumerate(lines):
            line.arrive(hop)
            if hop + 1 < line.hops:
                line.start(hop + 1)
            line.passed(hop, lambda s: across(s, part).start())
    for part, line in enumerate(lines):
        line.drain()
        for s in range(ranks):
            across(s, part).wait()


def attend(
    x_all, weights, out_weights, bias, cosine, sine, x, gain_row, kv_heads, rope_width, plane_size
):
    ranks, rows, model = x_all.shape
    seq = rows * ranks
    q_width = kv_heads * GROUP * HEAD_WIDTH
    value_width = weights.shape[1] - LANES - rope_width
    heads = kv_heads * GROUP
    stack = shape_of((ranks, rows, model), BF16)
    outs = [
        shape_of((LANES, model), BF16),
        shape_of((seq, model), BF16),
        shape_of((seq, rope_width), BF16),
        shape_of((seq, value_width), BF16),
        shape_of((seq, q_width), BF16),
        shape_of((heads, seq), F32),
        shape_of((heads, seq), F32),
        shape_of((rows, model), F32),
        shape_of((rows, model), BF16),
        stack,
        stack,
    ]
    dma = pltpu.SemaphoreType.DMA
    out = pl.pallas_call(
        functools.partial(attend_kernel, ranks, plane_size, kv_heads, gain_row),
        in_specs=[VMEM] * 7,
        out_specs=[VMEM] * len(outs),
        out_shape=outs,
        scratch_shapes=[
            pltpu.VMEM((q_width, seq), F32),
            pltpu.VMEM((ranks - 1, rows, model), BF16),
            pltpu.VMEM((ranks - 1, rows, model), BF16),
            dma((ranks - 1,)),
            dma((ranks - 1,)),
            dma((2, 2, ranks - 1)),
            dma((2, 2, ranks - 1)),
            dma((2, ranks)),
            dma((2, ranks)),
        ],
        compiler_params=remote(1),
        name="attend",
    )(x_all, weights, out_weights, bias, cosine, sine, x)
    return out[0], out[1:7], out[7:]


def rejoin_kernel(ranks, plane_size, gain_row, gates, h, dz, router_t, a2, *refs):
    parts = refs[:ranks]
    dh, gathered, extra, g_send, g_recv = refs[ranks:]
    model = h.shape[1]
    spot = Spot(ranks, plane_size)
    meet([spot.ahead(s) for s in range(1, ranks)])
    total = parts[0][...]
    for i in range(1, ranks):
        total = total + parts[i][...].astype(F32)
    tail = total[:, model:]
    dgates = tail + pltpu.roll(tail, LANES // 2, 1)
    gate = gates[...]
    mean = jnp.sum(gate * dgates, axis=1, keepdims=True)
    d_logits = (gate * (dgates - mean)).astype(BF16)
    da2 = total[:, :model] + dot(d_logits, router_t[...])
    value = h[...]
    scale = lax.rsqrt(jnp.mean(value * value, axis=-1, keepdims=True) + EPSILON)
    normed = value * scale
    gain = router_t[gain_row : gain_row + 1, :].astype(F32)
    weighted = da2 * gain
    grad = dz[...] + scale * (
        weighted - normed * jnp.mean(weighted * normed, axis=-1, keepdims=True)
    )
    gathered[0] = grad.astype(BF16)
    dh[...] = grad
    lines = half_lines(spot, gathered, g_send, g_recv)
    for line_out in lines:
        line_out.start(0)
    gain_grad = jnp.sum(da2 * normed, axis=0, keepdims=True)
    line = lax.broadcasted_iota(jnp.int32, (LANES, model), 0)
    extra[...] = jnp.where(line == gain_row, gain_grad, dot_tn(d_logits, a2[...]))
    for hop in range(ranks - 1):
        for line_out in lines:
            line_out.arrive(hop)
            if hop + 1 < line_out.hops:
                line_out.start(hop + 1)
    for line_out in lines:
        line_out.drain()


def rejoin(parts, gates, h, dz, router_t, a2, gain_row, plane_size):
    ranks = len(parts)
    dma = pltpu.SemaphoreType.DMA
    return pl.pallas_call(
        functools.partial(rejoin_kernel, ranks, plane_size, gain_row),
        in_specs=[VMEM] * (5 + ranks),
        out_specs=[VMEM] * 3,
        out_shape=[
            shape_of(h.shape, F32),
            shape_of((ranks,) + h.shape, BF16),
            shape_of((LANES, h.shape[1]), F32),
        ],
        scratch_shapes=[dma((2, 2, ranks - 1)), dma((2, 2, ranks - 1))],
        compiler_params=remote(2),
        cost_estimate=lasting(35),
        name="rejoin",
    )(gates, h, dz, router_t, a2, *parts)


def last_kernel(ranks, plane_size, gain_row, x, dh, extra_t, d_weights, d_rows, *refs):
    sums = refs[:ranks]
    out, columns_out, rows_out = refs[ranks : ranks + 3]
    (got, core_w, core_r, sum_w, sum_r, chip_w, chip_r, final) = refs[ranks + 3 : ranks + 11]
    r_send, r_recv, c_send, c_recv, p_send, p_recv, z_send, z_recv, local = refs[ranks + 11 :]
    spot = Spot(ranks, plane_size)
    chips, core, me = spot.chips, spot.core, spot.rank
    meet(
        [spot.ahead(s) for s in range(1, ranks)]
        + [spot.on_chip(spot.chip_ahead(k)) for k in range(1, chips)]
        + [spot.partner()]
    )
    z_copies = scatter_start(spot, sums, got, r_send, r_recv)
    pairs = ((0, d_weights, core_w, sum_w, chip_w), (1, d_rows, core_r, sum_r, chip_r))
    across = {}
    for k in range(chips):
        at = spot.chip_ahead(k)
        for which, src, buf, _, _ in pairs:
            across[k, which] = send(
                src.at[at, 1 - core],
                buf.at[k],
                c_send.at[which, k],
                c_recv.at[which, k],
                spot.partner(),
            )
    for k in list(range(1, chips)) + [0]:
        at = spot.chip_ahead(k)
        for which, src, buf, total, _ in pairs:
            across[k, which].wait()
            total[k] = (src[at, core].astype(F32) + buf[k].astype(F32)).astype(BF16)
    hops = {}
    for k in range(1, chips):
        for which, _, _, total, buf in pairs:
            hops[k, which] = send(
                total.at[k],
                buf.at[k - 1],
                p_send.at[which, k - 1],
                p_recv.at[which, k - 1],
                spot.on_chip(spot.chip_ahead(k)),
            )
    value = x[...]
    scale = lax.rsqrt(jnp.mean(value * value, axis=-1, keepdims=True) + EPSILON)
    normed = value * scale
    total = sums[0][...]
    for s in range(1, ranks):
        z_copies[s - 1].wait()
        total = total + got[s - 1].astype(F32)
    weighted = total * extra_t[gain_row : gain_row + 1, :].astype(F32)
    grad = scale * (weighted - normed * jnp.mean(weighted * normed, axis=-1, keepdims=True))
    for k in range(1, chips):
        for which in range(2):
            hops[k, which].wait()
    value = sum_w[0].astype(F32)
    for k in range(1, chips):
        value = value + chip_w[k - 1].astype(F32)
    final[...] = value.astype(BF16)
    out[...] = dh[...] + grad
    value = sum_r[0].astype(F32)
    for k in range(1, chips):
        value = value + chip_r[k - 1].astype(F32)
    rows_out[...] = value
    kept = pltpu.make_async_copy(final.at[me], columns_out.at[me], local.at[0])
    kept.start()
    copies = [
        send(
            final.at[lax.rem(me + s, ranks)],
            columns_out.at[me],
            z_send.at[s - 1],
            z_recv.at[s - 1],
            spot.ahead(s),
        )
        for s in range(1, ranks)
    ]
    for copy in copies:
        copy.wait()
    kept.wait()


def last(x, dh, extra_t, d_weights, d_rows, sums, gain_row):
    ranks = len(sums)
    chips, _, _, rows, columns = d_weights.shape
    dma = pltpu.SemaphoreType.DMA
    w_shape, r_shape = d_weights.shape[2:], d_rows.shape[2:]
    return pl.pallas_call(
        functools.partial(last_kernel, ranks, 2 * chips, gain_row),
        in_specs=[VMEM] * (5 + ranks),
        out_specs=[VMEM] * 3,
        out_shape=[shape_of(x.shape, F32), shape_of(w_shape, BF16), shape_of(r_shape, F32)],
        scratch_shapes=[
            pltpu.VMEM((ranks - 1,) + x.shape, BF16),
            pltpu.VMEM((chips,) + w_shape, BF16),
            pltpu.VMEM((chips,) + r_shape, BF16),
            pltpu.VMEM((chips,) + w_shape, BF16),
            pltpu.VMEM((chips,) + r_shape, BF16),
            pltpu.VMEM((chips - 1,) + w_shape, BF16),
            pltpu.VMEM((chips - 1,) + r_shape, BF16),
            pltpu.VMEM(w_shape, BF16),
            dma((ranks - 1,)),
            dma((ranks - 1,)),
            dma((2, chips)),
            dma((2, chips)),
            dma((2, chips - 1)),
            dma((2, chips - 1)),
            dma((ranks - 1,)),
            dma((ranks - 1,)),
            dma((1,)),
        ],
        compiler_params=remote(3),
        cost_estimate=lasting(60),
        name="last",
    )(x, dh, extra_t, d_weights, d_rows, *sums)


def piece_ids(position_index, starts):
    inside = (position_index[:, None] >= starts[None, :]) & (
        position_index[:, None] < starts[None, :] + PIECE
    )
    labels = jnp.arange(1, starts.shape[0] + 1, dtype=jnp.int32)[None, :]
    return jnp.sum(jnp.where(inside, labels, 0), axis=1, dtype=jnp.int32)


def on_device(
    inputs,
    cotangent,
    norm1_gain,
    w_query,
    key_projection,
    value_projection,
    w_output,
    norm2_gain,
    w_router,
    w_gate,
    w_up,
    w_down,
    routes,
    piece_starts,
):
    plane = Plane()
    ranks = lax.axis_size("expert")
    me = lax.axis_index("expert")
    rows, model = inputs.shape
    seq = rows * ranks
    weight_rows = w_query.shape[0]
    n_experts = w_router.shape[1]
    ff = w_gate.shape[2]
    kv_heads = KEY_VALUE_HEADS // ranks
    q_cols, kv_cols = kv_heads * GROUP * HEAD_WIDTH, kv_heads * HEAD_WIDTH
    rope_width = q_cols + kv_cols
    value_width = -(-kv_cols // LANES) * LANES
    columns = rope_width + value_width + LANES
    gain_one_row, gain_two_row = n_experts, n_experts + 1

    scale_one = lax.rsqrt(jnp.mean(inputs * inputs, axis=-1, keepdims=True) + EPSILON)
    x_own = (inputs * scale_one).astype(BF16)

    extra_cols = jnp.concatenate(
        [
            w_router,
            norm1_gain[:, None],
            norm2_gain[:, None],
            jnp.zeros((weight_rows, LANES - n_experts - 2), F32),
        ],
        axis=1,
    )
    by_rank = jnp.concatenate(
        [
            w_query.reshape(weight_rows, ranks, q_cols),
            key_projection.reshape(weight_rows, ranks, kv_cols),
            jnp.pad(
                value_projection.reshape(weight_rows, ranks, kv_cols),
                ((0, 0), (0, 0), (0, value_width - kv_cols)),
            ),
            jnp.broadcast_to(extra_cols[:, None, :], (weight_rows, ranks, LANES)),
        ],
        axis=2,
    ).astype(BF16)
    by_rank = jnp.transpose(by_rank, (1, 0, 2))

    axes = ("fsdp", "expert")
    total = plane.size * ranks
    move = [
        (j, (j % plane.size) * ranks + j // plane.size) for j in range(total)
    ]
    out_shard = lax.ppermute(w_output.astype(BF16), axes, move)

    lane_ids = jnp.arange(LANES, dtype=jnp.int32)
    routed = jnp.sum((routes[:, :, None] == lane_ids[None, None, :]).astype(F32), axis=1)
    grads_own = jnp.concatenate([cotangent, routed], axis=1).astype(BF16)

    core = plane.core.astype(jnp.int32)[None]
    weights, out_weights, x_all, grads, part_a, part_b, got_a, got_b = gather_weights(
        by_rank, out_shard, x_own, grads_own, w_gate, w_up, w_down, plane.size
    )
    grads = grads.reshape(seq, grads.shape[2])
    found = {(0, 0, 0): part_a, (0, 0, 1): part_b, (0, 1, 0): got_a}
    for s in range(1, plane.rows):
        found[s, 0, 1] = got_b[s - 1]
        for mid in range(2):
            found[s, mid, 0] = plane.next_row(found[0, mid, 0], s)
    for s in range(plane.rows):
        found[s, 1, 1] = plane.other_mid(found[s, 0, 1])
    place, pieces = tuple(found.keys()), list(found.values())
    sources = [
        ((plane.row - s) % plane.rows) * 2 + (plane.mid + mid) % 2
        for s in range(plane.rows)
        for mid in range(2)
    ]
    where = jnp.stack([me] + sources).astype(jnp.int32)

    weights = weights.reshape(model, columns)
    out_weights = out_weights.reshape(q_cols, model)

    block_ids = jnp.arange(seq, dtype=jnp.int32) // rows
    places = ((me - block_ids) % ranks) * rows + jnp.arange(seq, dtype=jnp.int32) % rows
    ids = piece_ids(places, piece_starts[0])
    visible = (places[:, None] <= places[None, :]) | (
        (ids[:, None] == ids[None, :]) & (ids[None, :] > 0)
    )
    bias = jnp.where(visible, 0.0, NEG_FILL).astype(F32)
    half = HEAD_WIDTH // 2
    inverse = 10000.0 ** (-(jnp.arange(half, dtype=F32) * 2.0 / HEAD_WIDTH))
    angles = places.astype(F32)[:, None] * inverse[None, :]
    cosine = jnp.tile(jnp.cos(angles), (1, LANES // half))
    sine = jnp.tile(jnp.sin(angles), (1, LANES // half)) * jnp.where(
        lane_ids % HEAD_WIDTH < half, -1.0, 1.0
    )
    extra_t, kept, (mid_rows, a2, own_a2, other_a2) = attend(
        x_all,
        weights,
        out_weights,
        bias,
        cosine,
        sine,
        inputs,
        gain_one_row,
        kv_heads,
        rope_width,
        plane.size,
    )

    other_grads = plane.other_core(grads)
    other_out, other_dx, _, *other_kept = experts(
        [other_a2.reshape(seq, model)], other_grads, extra_t, where, pieces, place, BF16
    )
    out_all, dx_all, gates, *own_kept = experts(
        [own_a2.reshape(seq, model)], grads, extra_t, where, pieces, place, F32
    )
    dx_all = dx_all + plane.other_core(other_dx).astype(F32)
    dxs = [
        dx_all[b * rows : (b + 1) * rows].astype(F32 if b == 0 else BF16) for b in range(ranks)
    ]
    dx_got = expert_scatter(dxs)
    chips = [
        ((plane.row + s) % plane.rows) * 2 + (plane.mid + mid) % 2
        for s in range(plane.rows)
        for mid in range(2)
    ]
    own_kept.insert(2, grads)
    other_kept.insert(2, other_grads)
    flat = expert_grads(
        jnp.stack(chips).astype(jnp.int32), own_kept, other_kept, plane.size, plane.rows
    )
    by_row, by_mid = flat[: plane.rows], flat[plane.rows :]

    def add(first, *others):
        value = first.astype(F32)
        for v in others:
            value = value + v.astype(F32)
        return value.astype(BF16)

    steps = range(1, plane.rows)
    a_first = [plane.next_row(by_row[s], s) for s in steps]
    b_first = plane.other_mid(by_mid[1])

    dh, dh_stack, extra = rejoin(
        [dxs[0]] + dx_got, gates, mid_rows, cotangent, extra_t, a2, gain_two_row, plane.size
    )
    other_out = plane.other_core(other_out)
    dh_stack, other_out, out_all = lax.optimization_barrier((dh_stack, other_out, out_all))
    out_all = out_all + other_out.astype(F32)
    outs = [out_all[b * rows : (b + 1) * rows] for b in range(ranks)]
    outs = [outs[0]] + [v.astype(BF16) for v in outs[1:]]
    dh_stack, outs = lax.optimization_barrier((dh_stack, outs))
    out_got = expert_scatter(outs)

    d_weights, d_out_weights, da1 = attend_back(
        dh_stack,
        x_all,
        weights,
        out_weights,
        kept,
        bias,
        cosine,
        sine,
        extra,
        kv_heads,
        gain_one_row,
    )
    a_first, b_first, d_weights = lax.optimization_barrier((a_first, b_first, d_weights))
    a_next = add(by_row[0][1], *[v[1] for v in a_first])
    b_next = [add(by_mid[0][s], b_first[s]) for s in steps]
    a_got = plane.other_mid(a_next)
    b_got = [plane.next_row(v, s) for s, v in zip(steps, b_next)]
    a_next, b_next, d_weights, out_got = lax.optimization_barrier(
        (a_next, b_next, d_weights, out_got)
    )
    chip_count = plane.size // 2
    input_grad, by_rank, out_part = last(
        inputs,
        dh,
        extra_t,
        d_weights.reshape(chip_count, 2, ranks, weight_rows, columns),
        d_out_weights.reshape(chip_count, 2, weight_rows, model),
        da1,
        gain_one_row,
    )
    a_got, b_got, out_part = lax.optimization_barrier((a_got, b_got, out_part))
    parts_a = [by_row[0], *a_first, a_got]
    parts_b = [by_mid[0], b_first, *b_got]

    def total(parts):
        value = 0.0
        for v in parts:
            value = value + (v[0] if v.ndim == 5 else v)[:2].astype(F32)
        return value

    other = plane.other_core(
        jnp.where(plane.core == 0, total(parts_b), total(parts_a)).astype(BF16)
    )
    gate_grad, up_grad, down_grad = finish(
        core, parts_a, parts_b, other, w_down.shape[1], model, plane.size
    )
    output = mid_rows + outs[0]
    for v in out_got:
        output = output + v.astype(F32)

    w_output_grad = lax.ppermute(
        out_part.astype(BF16), axes, [(b, a) for a, b in move]
    ).astype(F32)
    by_rank = by_rank.astype(F32)

    def columns_of(start, width):
        piece = by_rank[:, :, start : start + width]
        return jnp.transpose(piece, (1, 0, 2)).reshape(weight_rows, ranks * width)

    extra_grad = jnp.sum(by_rank[:, :, columns - LANES :], axis=0)
    return (
        output,
        input_grad,
        extra_grad[:, gain_one_row],
        columns_of(0, q_cols),
        columns_of(q_cols, kv_cols),
        columns_of(rope_width, kv_cols),
        w_output_grad,
        extra_grad[:, gain_two_row],
        extra_grad[:, :n_experts],
        gate_grad,
        up_grad,
        down_grad,
    )


def solution(mesh):
    both = ("fsdp", "expert")
    rows, flat, stack = P(both, None), P(both), P("expert", "fsdp", None)
    weights = (flat, rows, rows, rows, rows, flat, rows, stack, stack, stack)
    return jax.shard_map(
        on_device,
        mesh=mesh,
        in_specs=(rows, rows) + weights + (rows, P("fsdp", None)),
        out_specs=(rows, rows) + weights,
        check_vma=False,
    )
```

```python
import functools

import jax
import jax.numpy as jnp
from jax import lax
from jax.experimental import pallas as pl
from jax.experimental.pallas import tpu as pltpu
from jax.sharding import PartitionSpec as P

QUERY_HEADS = 24
KEY_VALUE_HEADS = 8
GROUP = QUERY_HEADS // KEY_VALUE_HEADS
HEAD_WIDTH = 64
PIECE = 256
LANES = 128
DEVICE_ROWS = 128
EPSILON = 1e-05
NEG_FILL = -1e30
SCORE_SCALE = HEAD_WIDTH ** (-0.5)
F32 = jnp.float32
BF16 = jnp.bfloat16

VMEM = pl.BlockSpec(memory_space=pltpu.VMEM)
SMEM = pl.BlockSpec(memory_space=pltpu.SMEM)
ANY = pl.BlockSpec(memory_space=pl.ANY)
MESH = pl.DeviceIdType.MESH


def dot(a, b):
    return lax.dot_general(a, b, (((1,), (0,)), ((), ())), preferred_element_type=F32)


def dot_nt(a, b):
    return lax.dot_general(a, b, (((1,), (1,)), ((), ())), preferred_element_type=F32)


def dot_tn(a, b):
    return lax.dot_general(a, b, (((0,), (0,)), ((), ())), preferred_element_type=F32)


def shape_of(dims, dtype):
    return jax.ShapeDtypeStruct(tuple(dims), dtype)


def lasting(us):
    return pl.CostEstimate(flops=us * 10**9, bytes_accessed=us * 10**6, transcendentals=0)


def params(**kw):
    return pltpu.CompilerParams(vmem_limit_bytes=60 * 1024 * 1024, **kw)


class Plane:
    def __init__(self):
        self.size = lax.axis_size("fsdp")
        self.rows = self.size // 4
        index = lax.axis_index("fsdp")
        self.index = index
        self.core = index % 2
        self.mid = (index // 2) % 2
        self.row = index // 4

    def other_core(self, x):
        return lax.ppermute(x, "fsdp", [(i, i ^ 1) for i in range(self.size)])

    def other_mid(self, x):
        return lax.ppermute(x, "fsdp", [(i, i ^ 2) for i in range(self.size)])

    def next_row(self, x, step):
        return lax.ppermute(
            x, "fsdp", [(i, (i // 4 + step) % self.rows * 4 + i % 4) for i in range(self.size)]
        )


def expert_shift(x, step):
    count = lax.axis_size("expert")
    return lax.ppermute(x, "expert", [(i, (i + step) % count) for i in range(count)])


def expert_scatter(blocks):
    count = lax.axis_size("expert")
    return [expert_shift(blocks[s], count - s) for s in range(1, count)]


def chooser(width, blocks, part, dtype=BF16):
    n = width // blocks
    line = lax.broadcasted_iota(jnp.int32, (width // 2, width), 0)
    column = lax.broadcasted_iota(jnp.int32, (width // 2, width), 1)
    want = (2 * (line // n) + part) * n + line % n
    return jnp.where(column == want, 1.0, 0.0).astype(dtype)


def swap_halves(x):
    lane = lax.broadcasted_iota(jnp.int32, x.shape, 1)
    return jnp.where(
        lane % HEAD_WIDTH < HEAD_WIDTH // 2, pltpu.roll(x, LANES - 32, 1), pltpu.roll(x, 32, 1)
    )


def head_slice(ref, start):
    return ref[:, start : start + HEAD_WIDTH]


def experts_kernel(blocks, pieces, place, row_block, *refs):
    a2_in = refs[:blocks]
    grads_in, router_t, where_ref = refs[blocks : blocks + 3]
    piece_refs = refs[blocks + 3 : blocks + 3 + pieces]
    (out_all, dx_all, gates_out, a2_t, hidden_t, d_gate, d_up) = refs[
        blocks + 3 + pieces : blocks + 10 + pieces
    ]
    (a2, gate_w, up_w, down_w, out_sum, dx_sum, gates, dgates, in_sem, w_sem) = refs[
        blocks + 10 + pieces :
    ]
    step, steps = pl.program_id(0), pl.num_programs(0)
    rows = a2_in[0].shape[0]
    seq, model = a2.shape
    depth, width = piece_refs[0].shape[2], gate_w.shape[2]
    down_rows = depth * width // model
    slot = lax.rem(step, 2)

    def fetch(e, to):
        for i, (row_step, mid, part) in enumerate(place):
            source = where_ref[1 + row_step * 2 + mid] * 2 + part
            at = pl.multiple_of(source * depth, 32)
            for which, buf in ((0, gate_w), (1, up_w)):
                pltpu.make_async_copy(
                    piece_refs[i].at[which, e], buf.at[to, pl.ds(at, depth)], w_sem.at[which, to]
                ).start()
            at = pl.multiple_of(source * down_rows, 16)
            for j in range(model // width):
                pltpu.make_async_copy(
                    piece_refs[i].at[2, e, pl.ds(j * down_rows, down_rows)],
                    down_w.at[to, pl.ds(at, down_rows), pl.ds(j * width, width)],
                    w_sem.at[2, to],
                ).start()

    @pl.when(step == 0)
    def _():
        for b in range(blocks):
            pltpu.make_async_copy(
                a2_in[b], a2.at[pl.ds(b * rows, rows)], in_sem.at[0]
            ).start()
        fetch(0, 0)
        pltpu.make_async_copy(a2, a2, in_sem.at[0]).wait()
        logits = dot_nt(a2[...], router_t[...])
        routed = grads_in[:, model:].astype(F32) > 0.5
        top = jnp.max(jnp.where(routed, logits, NEG_FILL), axis=1, keepdims=True)
        weight = jnp.where(routed, jnp.exp(jnp.where(routed, logits, top) - top), 0.0)
        gates[...] = weight / jnp.sum(weight, axis=1, keepdims=True)
        gates_out[...] = gates[: gates_out.shape[0], :]
        dgates[...] = jnp.zeros_like(dgates)
        a2_t[...] = a2[...].T

    @pl.when(step + 1 < steps)
    def _():
        fetch(step + 1, 1 - slot)

    for which, buf in ((0, gate_w), (1, up_w), (2, down_w)):
        pltpu.make_async_copy(buf.at[slot], buf.at[slot], w_sem.at[which, slot]).wait()

    mine = where_ref[0] * steps + step

    def block(i, carry):
        at = pl.ds(pl.multiple_of(i * row_block, row_block), row_block)
        left = a2[at, :]
        gate_lin = dot(left, gate_w[slot])
        up_lin = dot(left, up_w[slot])
        back = dot_nt(grads_in[at, :model], down_w[slot])
        lane = lax.broadcasted_iota(jnp.int32, (row_block, LANES), 1)
        here = lane == mine
        gate = jnp.sum(jnp.where(here, gates[at, :], 0.0), axis=1, keepdims=True)
        sig = 1.0 / (1.0 + jnp.exp(-gate_lin))
        silu = gate_lin * sig
        hidden = silu * up_lin
        dgates[at, :] += jnp.where(here, jnp.sum(hidden * back, axis=1, keepdims=True), 0.0)
        hidden_low = (hidden * gate).astype(BF16)
        d_hidden = back * gate
        d_gate_low = (d_hidden * up_lin * (sig + silu * (1.0 - sig))).astype(BF16)
        d_up_low = (d_hidden * silu).astype(BF16)
        d_gate[at, :] = d_gate_low
        d_up[at, :] = d_up_low
        hidden_t[0, :, at] = hidden_low.T
        out_new = dot(hidden_low, down_w[slot])
        dx_new = dot_nt(d_gate_low, gate_w[slot]) + dot_nt(d_up_low, up_w[slot])

        @pl.when(step == 0)
        def _():
            out_sum[at, :] = out_new
            dx_sum[at, :] = dx_new

        @pl.when(step > 0)
        def _():
            out_sum[at, :] += out_new
            dx_sum[at, :] += dx_new

        return carry

    lax.fori_loop(0, seq // row_block, block, 0)

    @pl.when(step == steps - 1)
    def _():
        high = dgates[...].astype(BF16).astype(F32)
        low = dgates[...] - high
        lane = lax.broadcasted_iota(jnp.int32, high.shape, 1)
        tail = jnp.where(lane < LANES // 2, high, pltpu.roll(low, LANES // 2, 1))
        out_all[...] = out_sum[...].astype(out_all.dtype)
        dx_all[:, :model] = dx_sum[...].astype(dx_all.dtype)
        dx_all[:, model:] = tail.astype(dx_all.dtype)


def experts(a2_blocks, grads, router_t, where, pieces, place, dtype):
    blocks = len(a2_blocks)
    rows, model = a2_blocks[0].shape
    seq = rows * blocks
    local, depth, width = pieces[0].shape[1:]
    outs = [
        shape_of((seq, model), dtype),
        shape_of((seq, model + LANES), dtype),
        shape_of((DEVICE_ROWS, LANES), F32),
        shape_of((model, seq), BF16),
        shape_of((local, width, seq), BF16),
        shape_of((seq, local * width), BF16),
        shape_of((seq, local * width), BF16),
    ]
    whole = lambda dims: pl.BlockSpec(
        dims, lambda e: (0,) * len(dims), pipeline_mode=pl.Buffered(1)
    )
    out_specs = (
        [whole(o.shape) for o in outs[:4]]
        + [pl.BlockSpec((1, width, seq), lambda e: (e, 0, 0))]
        + [pl.BlockSpec((seq, width), lambda e: (0, e))] * 2
    )
    return pl.pallas_call(
        functools.partial(experts_kernel, blocks, len(pieces), place, 256),
        grid=(local,),
        in_specs=[ANY] * blocks
        + [whole(grads.shape), whole(router_t.shape), SMEM]
        + [ANY] * len(pieces),
        out_specs=out_specs,
        out_shape=outs,
        scratch_shapes=[
            pltpu.VMEM((seq, model), BF16),
            pltpu.VMEM((2, model, width), BF16),
            pltpu.VMEM((2, model, width), BF16),
            pltpu.VMEM((2, width, model), BF16),
            pltpu.VMEM((seq, model), F32),
            pltpu.VMEM((seq, model), F32),
            pltpu.VMEM((seq, LANES), F32),
            pltpu.VMEM((seq, LANES), F32),
            pltpu.SemaphoreType.DMA((1,)),
            pltpu.SemaphoreType.DMA((3, 2)),
        ],
        compiler_params=params(dimension_semantics=("arbitrary",)),
        name="experts",
    )(*a2_blocks, grads, router_t, where, *pieces)


def expert_grads_kernel(plane_rows, depth, down_rows, where_ref, *refs):
    (a2_t0, a2_t1, hid0, hid1, grads0, grads1, dg0, dg1, du0, du1) = refs[:10]
    row_outs, mid_outs = refs[10 : 10 + plane_rows], refs[10 + plane_rows : 12 + plane_rows]
    down_sum = refs[12 + plane_rows]
    model, width = a2_t0.shape[0], dg0.shape[1]
    down_sum[...] = (dot(hid0[0], grads0[...]) + dot(hid1[0], grads1[...])).astype(BF16)
    for s in range(plane_rows):
        for mid in range(2):
            source = where_ref[2 * s + mid]
            at = pl.ds(pl.multiple_of(source * 2 * depth, 32), 2 * depth)
            left0, left1 = a2_t0[at, :], a2_t1[at, :]
            gate = (dot(left0, dg0[...]) + dot(left1, dg1[...])).astype(BF16)
            up = (dot(left0, du0[...]) + dot(left1, du1[...])).astype(BF16)
            for part, out in ((0, row_outs[s].at[mid]), (1, mid_outs[mid].at[s])):
                out[0, 0] = gate[part * depth : (part + 1) * depth]
                out[1, 0] = up[part * depth : (part + 1) * depth]
                at = pl.ds(pl.multiple_of((source * 2 + part) * down_rows, 16), down_rows)
                down = down_sum[at, :]
                for j in range(model // width):
                    out[2, 0, j * down_rows : (j + 1) * down_rows, :] = down[
                        :, j * width : (j + 1) * width
                    ]


def expert_grads(where, first, second, plane_size, plane_rows):
    model, seq = first[0].shape
    local, width = first[1].shape[:2]
    depth, down_rows = model // plane_size, width // plane_size
    counts = [2] * plane_rows + [plane_rows] * 2
    once = lambda dims: pl.BlockSpec(dims, lambda e: (0, 0), pipeline_mode=pl.Buffered(1))
    specs = [
        once((model, seq)),
        pl.BlockSpec((1, width, seq), lambda e: (e, 0, 0)),
        once((seq, model)),
        pl.BlockSpec((seq, width), lambda e: (0, e)),
        pl.BlockSpec((seq, width), lambda e: (0, e)),
    ]
    operands = [v for pair in zip(first, second) for v in pair]
    return pl.pallas_call(
        functools.partial(expert_grads_kernel, plane_rows, depth, down_rows),
        grid=(local,),
        in_specs=[SMEM] + [spec for spec in specs for _ in range(2)],
        out_specs=[
            pl.BlockSpec((n, 3, 1, depth, width), lambda e: (0, 0, e, 0, 0)) for n in counts
        ],
        out_shape=[shape_of((n, 3, local, depth, width), BF16) for n in counts],
        scratch_shapes=[pltpu.VMEM((width, model), BF16)],
        compiler_params=params(),
        cost_estimate=lasting(18),
        name="expert_grads",
    )(where, *operands)


def finish_kernel(blocks, count_a, count_b, core, *refs):
    parts_a, parts_b = refs[:count_a], refs[count_a : count_a + count_b]
    other, gate, up, down, choose = refs[count_a + count_b :]
    width, wide = gate.shape[2], other.shape[3]

    @pl.when(pl.program_id(0) == 0)
    def _():
        choose[0] = chooser(width, blocks, core[0])
        choose[1] = chooser(width, blocks, 1 - core[0])

    mine, theirs = choose[0], choose[1]
    first = core[0] == 0

    def total(parts, place):
        value = parts[0][place, 0].astype(F32)
        for part in parts[1:]:
            value = value + part[place, 0].astype(F32)
        return value

    for place, out in ((0, gate), (1, up)):
        kept = jnp.where(first, total(parts_a[:-1], place), total(parts_b[:-1], place))
        got = jnp.where(
            first, parts_a[-1][place, 0].astype(F32), parts_b[-1][place, 0].astype(F32)
        )
        out[0] = (
            dot(kept.astype(BF16), mine)
            + dot(got.astype(BF16), mine)
            + dot(other[place, 0], theirs)
        )
    rows = down.shape[1] // 2
    for part, parts in ((0, parts_a), (1, parts_b)):
        value = total(parts, 2)
        for j in range(value.shape[0] // rows):
            down[0, part * rows : (part + 1) * rows, j * wide : (j + 1) * wide] = value[
                j * rows : (j + 1) * rows
            ]


def finish(core, parts_a, parts_b, other, down_rows, model, blocks):
    local, depth, wide = other.shape[1:]
    block = pl.BlockSpec((3, 1, depth, wide), lambda e: (0, e, 0, 0))
    front = pl.BlockSpec((None, 3, 1, depth, wide), lambda e: (0, 0, e, 0, 0))
    outs = [
        shape_of((local, depth, 2 * wide), F32),
        shape_of((local, depth, 2 * wide), F32),
        shape_of((local, down_rows, model), F32),
    ]
    parts = list(parts_a) + list(parts_b)
    return pl.pallas_call(
        functools.partial(finish_kernel, blocks, len(parts_a), len(parts_b)),
        grid=(local,),
        in_specs=[SMEM]
        + [front if v.ndim == 5 else block for v in parts]
        + [pl.BlockSpec((2, 1, depth, wide), lambda e: (0, e, 0, 0))],
        out_specs=[pl.BlockSpec((1,) + o.shape[1:], lambda e: (e, 0, 0)) for o in outs],
        out_shape=outs,
        scratch_shapes=[pltpu.VMEM((2, wide, 2 * wide), BF16)],
        name="finish",
    )(core, *parts, other)


def attend_back_kernel(blocks, kv_heads, gain_row, *refs):
    dh_ref, x_all = refs[:2]
    (weights, out_weights, a1, qk, val, mixed, maxes, inverse, bias, cosine, sine, extra) = refs[2:14]
    d_weights, d_out_weights = refs[14:16]
    sums = refs[16 : blocks + 16]
    grads, d_mixed, dq_t, d_qk, d_lin = refs[blocks + 16 :]
    rows = x_all.shape[1]
    rope_width, value_width = qk.shape[1], val.shape[1]
    q_width = kv_heads * GROUP * HEAD_WIDTH
    for b in range(blocks):
        grads[b * rows : (b + 1) * rows, :] = dh_ref[b]
    d_mixed[...] = dot_nt(grads[...], out_weights[...]).astype(BF16)
    d_out_weights[...] = dot_tn(mixed[...], grads[...]).astype(BF16)
    if value_width > kv_heads * HEAD_WIDTH:
        d_lin[:, rope_width:] = jnp.zeros((d_lin.shape[0], value_width), BF16)
    for g in range(kv_heads):
        key = head_slice(qk, q_width + g * HEAD_WIDTH)
        key_t = key.T
        value = head_slice(val, g * HEAD_WIDTH)
        d_key, d_value = None, None
        for j in range(GROUP):
            h = g * GROUP + j
            query = head_slice(qk, h * HEAD_WIDTH)
            grad = head_slice(d_mixed, h * HEAD_WIDTH)
            scores = dot_nt(key, query) * SCORE_SCALE + bias[...]
            prob = jnp.exp(scores - maxes[h : h + 1, :]) * inverse[h : h + 1, :]
            d_prob = dot_nt(value, grad)
            inner = jnp.sum(prob * d_prob, axis=0, keepdims=True)
            d_scores = (prob * (d_prob - inner)).astype(BF16)
            dk = dot(d_scores, query)
            dv = dot(prob.astype(BF16), grad)
            d_key = dk if d_key is None else d_key + dk
            d_value = dv if d_value is None else d_value + dv
            dq_t[h * HEAD_WIDTH : (h + 1) * HEAD_WIDTH, :] = dot(key_t, d_scores)
        start = q_width + g * HEAD_WIDTH
        d_qk[:, start : start + HEAD_WIDTH] = d_key * SCORE_SCALE
        start = rope_width + g * HEAD_WIDTH
        d_lin[:, start : start + HEAD_WIDTH] = d_value.astype(BF16)
    d_qk[:, :q_width] = dq_t[...].T * SCORE_SCALE
    for c in range(rope_width // LANES):
        at = slice(c * LANES, (c + 1) * LANES)
        x = d_qk[:, at]
        d_lin[:, at] = (x * cosine[...] - swap_halves(x) * sine[...]).astype(BF16)
    total = dot_nt(d_lin[...], weights[:, : rope_width + value_width])
    gain_grad = None
    for b in range(blocks):
        part = total[b * rows : (b + 1) * rows, :]
        sums[b][...] = part.astype(sums[b].dtype)
        new = jnp.sum(part * x_all[b].astype(F32), axis=0, keepdims=True)
        gain_grad = new if gain_grad is None else gain_grad + new
    d_weights[:, : rope_width + value_width] = dot_tn(a1[...], d_lin[...]).astype(BF16)
    line = lax.broadcasted_iota(jnp.int32, extra.shape, 0)
    tail = jnp.where(line == gain_row, gain_grad, extra[...])
    d_weights[:, rope_width + value_width :] = tail.T.astype(BF16)


def attend_back(
    dh_stack, x_all, weights, out_weights, kept, bias, cosine, sine, extra, kv_heads, gain_row
):
    blocks, rows, model = dh_stack.shape
    seq = rows * blocks
    q_width = out_weights.shape[0]
    rope_width, value_width = kept[1].shape[1], kept[2].shape[1]
    outs = [shape_of(weights.shape, BF16), shape_of(out_weights.shape, BF16)] + [
        shape_of((rows, model), F32 if b == 0 else BF16) for b in range(blocks)
    ]
    out = pl.pallas_call(
        functools.partial(attend_back_kernel, blocks, kv_heads, gain_row),
        in_specs=[VMEM] * 14,
        out_specs=[VMEM] * len(outs),
        out_shape=outs,
        scratch_shapes=[
            pltpu.VMEM((seq, model), BF16),
            pltpu.VMEM((seq, q_width), BF16),
            pltpu.VMEM((q_width, seq), F32),
            pltpu.VMEM((seq, rope_width), F32),
            pltpu.VMEM((seq, rope_width + value_width), BF16),
        ],
        compiler_params=params(),
        cost_estimate=lasting(16),
        name="attend_back",
    )(dh_stack, x_all, weights, out_weights, *kept, bias, cosine, sine, extra)
    return out[0], out[1], out[2:]


class Spot:
    def __init__(self, ranks, plane_size):
        self.ranks, self.chips = ranks, plane_size // 2
        self.rank = lax.axis_index("expert")
        self.index = lax.axis_index("fsdp")
        self.chip = self.index // 2
        self.core = self.index % 2

    def behind(self, s):
        return {"expert": lax.rem(self.rank - s + self.ranks, self.ranks)}

    def ahead(self, s):
        return {"expert": lax.rem(self.rank + s, self.ranks)}

    def partner(self):
        return {"fsdp": self.chip * 2 + (1 - self.core)}

    def chip_ahead(self, k):
        return lax.rem(self.chip + k, self.chips)

    def chip_behind(self, k):
        return lax.rem(self.chip - k + self.chips, self.chips)

    def on_chip(self, chip):
        return {"fsdp": chip * 2 + self.core}


def greet(peers):
    barrier = pltpu.get_barrier_semaphore()
    for peer in peers:
        pl.semaphore_signal(barrier, inc=1, device_id=peer, device_id_type=MESH)


def await_peers(peers):
    pl.semaphore_wait(pltpu.get_barrier_semaphore(), len(peers))


def meet(peers):
    greet(peers)
    await_peers(peers)


def send(src, dst, send_sem, recv_sem, peer):
    copy = pltpu.make_async_remote_copy(
        src_ref=src,
        dst_ref=dst,
        send_sem=send_sem,
        recv_sem=recv_sem,
        device_id=peer,
        device_id_type=MESH,
    )
    copy.start()
    return copy


def remote(collective_id):
    return params(collective_id=collective_id, has_side_effects=True)


def pack_experts(spot, w_gate, w_up, w_down, held, outgoing):
    local, width = w_gate.shape[0], w_gate.shape[2]
    mine = chooser(width, 2 * spot.chips, spot.core)
    theirs = chooser(width, 2 * spot.chips, 1 - spot.core)
    rows, wide = w_down.shape[1] // 2, width // 2

    def one(e, carry):
        for place, ref in ((0, w_gate), (1, w_up)):
            value = ref[e].astype(BF16)
            kept = dot_nt(value, mine).astype(BF16)
            for part in range(2):

                @pl.when(spot.core == part)
                def _():
                    held[part][place, e] = kept

            outgoing[place, e] = dot_nt(value, theirs).astype(BF16)
        value = w_down[e].astype(BF16)
        for part in range(2):
            for j in range(value.shape[1] // wide):
                held[part][2, e, j * rows : (j + 1) * rows] = value[
                    part * rows : (part + 1) * rows, j * wide : (j + 1) * wide
                ]
        return carry

    lax.fori_loop(0, local, one, 0)


def gather_weights_kernel(ranks, plane_size, *refs):
    by_rank, rows_in, x_in, grads_in, w_gate, w_up, w_down = refs[:7]
    weights, out_rows, x_all, grads_all, parts_a, parts_b, got_a, got_b = refs[7:15]
    held_a, held_b, outgoing = refs[15:18]
    z_send, z_recv, p_send, p_recv, c_send, c_recv, local, e_send, e_recv = refs[18:27]
    x_send, x_recv, grads_send, grads_recv = refs[27:]
    spot = Spot(ranks, plane_size)
    f, me, chips, core = spot.index, spot.rank, spot.chips, spot.core
    others = range(1, ranks)
    kept = [
        pltpu.make_async_copy(by_rank.at[me], weights.at[f, me], local.at[0]),
        pltpu.make_async_copy(rows_in, out_rows.at[f], local.at[1]),
        pltpu.make_async_copy(x_in, x_all.at[0], local.at[2]),
        pltpu.make_async_copy(grads_in, grads_all.at[0], local.at[3]),
    ]
    for copy in kept:
        copy.start()
    meet(
        [spot.ahead(s) for s in others]
        + [spot.on_chip(spot.chip_ahead(k)) for k in range(1, chips)]
        + [spot.partner()]
    )
    z_copies = [
        send(
            by_rank.at[lax.rem(me + s, ranks)],
            weights.at[f, me],
            z_send.at[s - 1],
            z_recv.at[s - 1],
            spot.ahead(s),
        )
        for s in others
    ]
    lines = [
        LineGather(spot, x_all, x_send, x_recv),
        LineGather(spot, grads_all, grads_send, grads_recv),
    ]

    def spread(which, src, buf):
        return [
            send(
                src,
                buf.at[f],
                p_send.at[which, k - 1],
                p_recv.at[which, k - 1],
                spot.on_chip(spot.chip_ahead(k)),
            )
            for k in range(1, chips)
        ] + [send(src, buf.at[f], c_send.at[which, 0], c_recv.at[which, 0], spot.partner())]

    row_copies = spread(1, rows_in, out_rows)
    for copy in kept:
        copy.wait()
    for line in lines:
        line.start(0)

    pack_experts(spot, w_gate, w_up, w_down, (held_a, held_b), outgoing)

    def swap(part, held):
        return pltpu.make_async_remote_copy(
            src_ref=outgoing,
            dst_ref=held.at[pl.ds(0, 2)],
            send_sem=e_send.at[0],
            recv_sem=e_recv.at[0],
            device_id=spot.partner(),
            device_id_type=MESH,
        )

    for part, held in ((0, held_a), (1, held_b)):

        @pl.when(core == part)
        def _():
            swap(part, held).start()

    for copy in z_copies:
        copy.wait()
    weight_copies = spread(0, weights.at[f], weights)
    for part, held in ((0, held_a), (1, held_b)):

        @pl.when(core == part)
        def _():
            swap(part, held).wait_send()

        @pl.when(core == 1 - part)
        def _():
            swap(part, held).wait_recv()

    row, mid = spot.chip // 2, lax.rem(spot.chip, 2)
    expert_copies = [
        send(held_a, got_a, e_send.at[1], e_recv.at[1], spot.on_chip(row * 2 + (1 - mid)))
    ] + [
        send(
            held_b,
            got_b.at[s - 1],
            e_send.at[1 + s],
            e_recv.at[1 + s],
            spot.on_chip(lax.rem(row + s, chips // 2) * 2 + mid),
        )
        for s in range(1, chips // 2)
    ]
    stores = [
        pltpu.make_async_copy(held_a, parts_a, local.at[4]),
        pltpu.make_async_copy(held_b, parts_b, local.at[5]),
    ]
    for copy in stores:
        copy.start()
    waits = []
    for hop in range(ranks - 1):
        for line in lines:
            line.arrive(hop)
            if hop + 1 < line.hops:
                line.start(hop + 1)
    for k in range(1, chips):
        source = spot.chip_behind(k) * 2 + core
        for which, copies, buf in ((1, row_copies, out_rows), (0, weight_copies, weights)):
            copies[k - 1].wait()
            waits.append(
                send(
                    buf.at[source],
                    buf.at[source],
                    c_send.at[which, k],
                    c_recv.at[which, k],
                    spot.partner(),
                )
            )
    row_copies[-1].wait()
    weight_copies[-1].wait()
    for copy in waits + stores + expert_copies:
        copy.wait()
    for line in lines:
        line.drain()


def gather_weights(by_rank, rows_in, x_in, grads_in, w_gate, w_up, w_down, plane_size):
    ranks, rows, columns = by_rank.shape
    chips = plane_size // 2
    local, depth, width = w_gate.shape
    dma = pltpu.SemaphoreType.DMA
    half = (local, depth, width // 2)
    return pl.pallas_call(
        functools.partial(gather_weights_kernel, ranks, plane_size),
        in_specs=[VMEM] * 7,
        out_specs=[VMEM] * 4 + [ANY] * 4,
        out_shape=[
            shape_of((plane_size, ranks, rows, columns), BF16),
            shape_of((plane_size,) + rows_in.shape, BF16),
            shape_of((ranks,) + x_in.shape, BF16),
            shape_of((ranks,) + grads_in.shape, BF16),
            shape_of((3,) + half, BF16),
            shape_of((3,) + half, BF16),
            shape_of((3,) + half, BF16),
            shape_of((chips // 2 - 1, 3) + half, BF16),
        ],
        scratch_shapes=[
            pltpu.VMEM((3,) + half, BF16),
            pltpu.VMEM((3,) + half, BF16),
            pltpu.VMEM((2,) + half, BF16),
            dma((ranks - 1,)),
            dma((ranks - 1,)),
            dma((2, chips - 1)),
            dma((2, chips - 1)),
            dma((2, chips)),
            dma((2, chips)),
            dma((6,)),
            dma((1 + chips // 2,)),
            dma((1 + chips // 2,)),
        ]
        + [dma((2, ranks - 1))] * 4,
        compiler_params=remote(0),
        name="gather_weights",
    )(by_rank, rows_in, x_in, grads_in, w_gate, w_up, w_down)


def scatter_start(spot, refs, buf, send_sem, recv_sem):
    return [
        send(refs[s], buf.at[s - 1], send_sem.at[s - 1], recv_sem.at[s - 1], spot.behind(s))
        for s in range(1, spot.ranks)
    ]


class LineGather:
    def __init__(self, spot, buf, send_sem, recv_sem, part=0, parts=1):
        self.spot, self.buf, self.sems = spot, buf, (send_sem, recv_sem)
        count = buf.shape[1] // parts
        self.rows = pl.ds(part * count, count)
        me, n = spot.rank, spot.ranks
        self.hops = n - 1
        self.sends = [(me - h >= 0) & (me + 1 < n) for h in range(n - 1)], [
            (me + h < n) & (me >= 1) for h in range(n - 1)
        ]
        self.gets = [me - 1 - h >= 0 for h in range(n - 1)], [
            me + 1 + h < n for h in range(n - 1)
        ]

    def slots(self, way, h):
        n = self.spot.ranks
        return (h, h + 1) if way == 0 else ((n - h) % n, n - h - 1)

    def copy(self, way, h):
        source, target = self.slots(way, h)
        return pltpu.make_async_remote_copy(
            src_ref=self.buf.at[source, self.rows],
            dst_ref=self.buf.at[target, self.rows],
            send_sem=self.sems[0].at[way, h],
            recv_sem=self.sems[1].at[way, h],
            device_id=self.spot.ahead(1) if way == 0 else self.spot.behind(1),
            device_id_type=MESH,
        )

    def start(self, h):
        for way in range(2):

            @pl.when(self.sends[way][h])
            def _():
                self.copy(way, h).start()

    def arrive(self, h):
        for way in range(2):

            @pl.when(self.gets[way][h])
            def _():
                self.copy(way, h).wait_recv()

    def passed(self, h, then):
        for way in range(2):

            @pl.when(self.gets[way][h])
            def _():
                then(self.slots(way, h)[1])

    def drain(self):
        for h in range(self.hops):
            for way in range(2):

                @pl.when(self.sends[way][h])
                def _():
                    self.copy(way, h).wait_send()


class LineScatter:
    def __init__(self, spot, coming, going, send_sem, recv_sem):
        self.spot, self.coming, self.going, self.sems = spot, coming, going, (send_sem, recv_sem)
        me, n = spot.rank, spot.ranks
        self.more = me >= 1, me + 1 < n
        self.goes = [(me + t < n, me - t >= 0) for t in range(n)]

    def copy(self, way, t):
        return pltpu.make_async_remote_copy(
            src_ref=self.going.at[way, t - 1],
            dst_ref=self.coming.at[way, t - 1],
            send_sem=self.sems[0].at[way, t - 1],
            recv_sem=self.sems[1].at[way, t - 1],
            device_id=self.spot.ahead(1) if way == 0 else self.spot.behind(1),
            device_id_type=MESH,
        )

    def run(self, own, total):
        n = self.spot.ranks
        for t in range(n - 1, 0, -1):
            for way in range(2):
                slot = n - t if way == 0 else t

                @pl.when(self.goes[t][way])
                def _():
                    if t == n - 1:
                        self.going[way, t - 1] = own[slot].astype(BF16)
                    else:

                        @pl.when(self.more[way])
                        def _():
                            self.copy(way, t + 1).wait_recv()
                            self.going[way, t - 1] = (
                                own[slot] + self.coming[way, t].astype(F32)
                            ).astype(BF16)

                        @pl.when(jnp.logical_not(self.more[way]))
                        def _():
                            self.going[way, t - 1] = own[slot].astype(BF16)

                    self.copy(way, t).start()

        for way in range(2):

            @pl.when(self.more[way])
            def _():
                self.copy(way, 1).wait_recv()
                total[...] += self.coming[way, 0].astype(F32)

    def drain(self):
        for t in range(self.spot.ranks - 1, 0, -1):
            for way in range(2):

                @pl.when(self.goes[t][way])
                def _():
                    self.copy(way, t).wait_send()


def half_lines(spot, buf, send_sem, recv_sem):
    return [LineGather(spot, buf, send_sem.at[k], recv_sem.at[k], k, 2) for k in range(2)]


def attend_kernel(ranks, plane_size, kv_heads, gain_row, *refs):
    x_all, weights, out_weights, bias, cosine, sine, x = refs[:7]
    (extra_t, a1, qk, val, mixed, maxes, inverse, h_out, a2, gathered, other) = refs[7:18]
    mixed_t, sums, got, going, r_send, r_recv, g_send, g_recv, c_send, c_recv = refs[18:]
    extra_t[...] = weights[:, weights.shape[1] - LANES :].T
    gain = extra_t[gain_row : gain_row + 1, :].astype(F32)
    gain_two = extra_t[gain_row + 1 : gain_row + 2, :].astype(F32)
    spot = Spot(ranks, plane_size)
    peers = [spot.ahead(s) for s in range(1, ranks)] + [spot.partner()]
    greet(peers)
    rows = x_all.shape[1]
    rope_width = qk.shape[1]
    q_width = kv_heads * GROUP * HEAD_WIDTH
    for b in range(ranks):
        a1[b * rows : (b + 1) * rows, :] = (x_all[b].astype(F32) * gain).astype(BF16)
    linear = dot(a1[...], weights[:, : rope_width + val.shape[1]])
    for c in range(rope_width // LANES):
        part = linear[:, c * LANES : (c + 1) * LANES]
        qk[:, c * LANES : (c + 1) * LANES] = (
            part * cosine[...] + swap_halves(part) * sine[...]
        ).astype(BF16)
    val[...] = linear[:, rope_width:].astype(BF16)
    for g in range(kv_heads):
        key = head_slice(qk, q_width + g * HEAD_WIDTH)
        value_t = head_slice(val, g * HEAD_WIDTH).T
        for j in range(GROUP):
            h = g * GROUP + j
            scores = dot_nt(key, head_slice(qk, h * HEAD_WIDTH)) * SCORE_SCALE + bias[...]
            top = jnp.max(scores, axis=0, keepdims=True)
            weight = jnp.exp(scores - top)
            inv = 1.0 / jnp.sum(weight, axis=0, keepdims=True)
            maxes[h : h + 1, :] = top
            inverse[h : h + 1, :] = inv
            mixed_t[h * HEAD_WIDTH : (h + 1) * HEAD_WIDTH, :] = dot(
                value_t, (weight * inv).astype(BF16)
            )
    mixed[...] = mixed_t[...].T.astype(BF16)
    await_peers(peers)
    total = dot(mixed[...], out_weights[...])
    for b in range(ranks):
        sums[b] = total[b * rows : (b + 1) * rows, :]
    h_out[...] = x[...] + sums[0]
    scatter = LineScatter(spot, got, going, r_send, r_recv)
    scatter.run(sums, h_out)
    total = h_out[...]
    scale = lax.rsqrt(jnp.mean(total * total, axis=-1, keepdims=True) + EPSILON)
    low = (total * scale * gain_two).astype(BF16)
    gathered[0] = low
    lines = half_lines(spot, gathered, g_send, g_recv)
    for line in lines:
        line.start(0)

    def across(s, part):
        return pltpu.make_async_remote_copy(
            src_ref=gathered.at[s, lines[part].rows],
            dst_ref=other.at[s, lines[part].rows],
            send_sem=c_send.at[part, s],
            recv_sem=c_recv.at[part, s],
            device_id=spot.partner(),
            device_id_type=MESH,
        )

    for part in range(2):
        across(0, part).start()
    a2[...] = low
    for hop in range(ranks - 1):
        for part, line in enumerate(lines):
            line.arrive(hop)
            if hop + 1 < line.hops:
                line.start(hop + 1)
            line.passed(hop, lambda s: across(s, part).start())
    scatter.drain()
    for part, line in enumerate(lines):
        line.drain()
        for s in range(ranks):
            across(s, part).wait()


def attend(
    x_all, weights, out_weights, bias, cosine, sine, x, gain_row, kv_heads, rope_width, plane_size
):
    ranks, rows, model = x_all.shape
    seq = rows * ranks
    q_width = kv_heads * GROUP * HEAD_WIDTH
    value_width = weights.shape[1] - LANES - rope_width
    heads = kv_heads * GROUP
    stack = shape_of((ranks, rows, model), BF16)
    outs = [
        shape_of((LANES, model), BF16),
        shape_of((seq, model), BF16),
        shape_of((seq, rope_width), BF16),
        shape_of((seq, value_width), BF16),
        shape_of((seq, q_width), BF16),
        shape_of((heads, seq), F32),
        shape_of((heads, seq), F32),
        shape_of((rows, model), F32),
        shape_of((rows, model), BF16),
        stack,
        stack,
    ]
    dma = pltpu.SemaphoreType.DMA
    out = pl.pallas_call(
        functools.partial(attend_kernel, ranks, plane_size, kv_heads, gain_row),
        in_specs=[VMEM] * 7,
        out_specs=[VMEM] * len(outs),
        out_shape=outs,
        scratch_shapes=[
            pltpu.VMEM((q_width, seq), F32),
            pltpu.VMEM((ranks, rows, model), F32),
            pltpu.VMEM((2, ranks - 1, rows, model), BF16),
            pltpu.VMEM((2, ranks - 1, rows, model), BF16),
            dma((2, ranks - 1)),
            dma((2, ranks - 1)),
            dma((2, 2, ranks - 1)),
            dma((2, 2, ranks - 1)),
            dma((2, ranks)),
            dma((2, ranks)),
        ],
        compiler_params=remote(1),
        name="attend",
    )(x_all, weights, out_weights, bias, cosine, sine, x)
    return out[0], out[1:7], out[7:]


def rejoin_kernel(ranks, plane_size, gain_row, gates, h, dz, router_t, a2, *refs):
    parts = refs[:ranks]
    dh, gathered, extra, g_send, g_recv = refs[ranks:]
    model = h.shape[1]
    spot = Spot(ranks, plane_size)
    meet([spot.ahead(s) for s in range(1, ranks)])
    total = parts[0][...]
    for i in range(1, ranks):
        total = total + parts[i][...].astype(F32)
    tail = total[:, model:]
    dgates = tail + pltpu.roll(tail, LANES // 2, 1)
    gate = gates[...]
    mean = jnp.sum(gate * dgates, axis=1, keepdims=True)
    d_logits = (gate * (dgates - mean)).astype(BF16)
    da2 = total[:, :model] + dot(d_logits, router_t[...])
    value = h[...]
    scale = lax.rsqrt(jnp.mean(value * value, axis=-1, keepdims=True) + EPSILON)
    normed = value * scale
    gain = router_t[gain_row : gain_row + 1, :].astype(F32)
    weighted = da2 * gain
    grad = dz[...] + scale * (
        weighted - normed * jnp.mean(weighted * normed, axis=-1, keepdims=True)
    )
    gathered[0] = grad.astype(BF16)
    dh[...] = grad
    lines = half_lines(spot, gathered, g_send, g_recv)
    for line_out in lines:
        line_out.start(0)
    gain_grad = jnp.sum(da2 * normed, axis=0, keepdims=True)
    line = lax.broadcasted_iota(jnp.int32, (LANES, model), 0)
    extra[...] = jnp.where(line == gain_row, gain_grad, dot_tn(d_logits, a2[...]))
    for hop in range(ranks - 1):
        for line_out in lines:
            line_out.arrive(hop)
            if hop + 1 < line_out.hops:
                line_out.start(hop + 1)
    for line_out in lines:
        line_out.drain()


def rejoin(parts, gates, h, dz, router_t, a2, gain_row, plane_size):
    ranks = len(parts)
    dma = pltpu.SemaphoreType.DMA
    return pl.pallas_call(
        functools.partial(rejoin_kernel, ranks, plane_size, gain_row),
        in_specs=[VMEM] * (5 + ranks),
        out_specs=[VMEM] * 3,
        out_shape=[
            shape_of(h.shape, F32),
            shape_of((ranks,) + h.shape, BF16),
            shape_of((LANES, h.shape[1]), F32),
        ],
        scratch_shapes=[dma((2, 2, ranks - 1)), dma((2, 2, ranks - 1))],
        compiler_params=remote(2),
        cost_estimate=lasting(35),
        name="rejoin",
    )(gates, h, dz, router_t, a2, *parts)


def last_kernel(ranks, plane_size, gain_row, x, dh, extra_t, d_weights, d_rows, *refs):
    sums = refs[:ranks]
    out, columns_out, rows_out = refs[ranks : ranks + 3]
    (got, core_w, core_r, sum_w, sum_r, chip_w, chip_r, final) = refs[ranks + 3 : ranks + 11]
    r_send, r_recv, c_send, c_recv, p_send, p_recv, z_send, z_recv, local = refs[ranks + 11 :]
    spot = Spot(ranks, plane_size)
    chips, core, me = spot.chips, spot.core, spot.rank
    meet(
        [spot.ahead(s) for s in range(1, ranks)]
        + [spot.on_chip(spot.chip_ahead(k)) for k in range(1, chips)]
        + [spot.partner()]
    )
    z_copies = scatter_start(spot, sums, got, r_send, r_recv)
    pairs = ((0, d_weights, core_w, sum_w, chip_w), (1, d_rows, core_r, sum_r, chip_r))
    across = {}
    for k in range(chips):
        at = spot.chip_ahead(k)
        for which, src, buf, _, _ in pairs:
            across[k, which] = send(
                src.at[at, 1 - core],
                buf.at[k],
                c_send.at[which, k],
                c_recv.at[which, k],
                spot.partner(),
            )
    for k in list(range(1, chips)) + [0]:
        at = spot.chip_ahead(k)
        for which, src, buf, total, _ in pairs:
            across[k, which].wait()
            total[k] = (src[at, core].astype(F32) + buf[k].astype(F32)).astype(BF16)
    hops = {}
    for k in range(1, chips):
        for which, _, _, total, buf in pairs:
            hops[k, which] = send(
                total.at[k],
                buf.at[k - 1],
                p_send.at[which, k - 1],
                p_recv.at[which, k - 1],
                spot.on_chip(spot.chip_ahead(k)),
            )
    value = x[...]
    scale = lax.rsqrt(jnp.mean(value * value, axis=-1, keepdims=True) + EPSILON)
    normed = value * scale
    total = sums[0][...]
    for s in range(1, ranks):
        z_copies[s - 1].wait()
        total = total + got[s - 1].astype(F32)
    weighted = total * extra_t[gain_row : gain_row + 1, :].astype(F32)
    grad = scale * (weighted - normed * jnp.mean(weighted * normed, axis=-1, keepdims=True))
    for k in range(1, chips):
        for which in range(2):
            hops[k, which].wait()
    value = sum_w[0].astype(F32)
    for k in range(1, chips):
        value = value + chip_w[k - 1].astype(F32)
    final[...] = value.astype(BF16)
    out[...] = dh[...] + grad
    value = sum_r[0].astype(F32)
    for k in range(1, chips):
        value = value + chip_r[k - 1].astype(F32)
    rows_out[...] = value
    kept = pltpu.make_async_copy(final.at[me], columns_out.at[me], local.at[0])
    kept.start()
    copies = [
        send(
            final.at[lax.rem(me + s, ranks)],
            columns_out.at[me],
            z_send.at[s - 1],
            z_recv.at[s - 1],
            spot.ahead(s),
        )
        for s in range(1, ranks)
    ]
    for copy in copies:
        copy.wait()
    kept.wait()


def last(x, dh, extra_t, d_weights, d_rows, sums, gain_row):
    ranks = len(sums)
    chips, _, _, rows, columns = d_weights.shape
    dma = pltpu.SemaphoreType.DMA
    w_shape, r_shape = d_weights.shape[2:], d_rows.shape[2:]
    return pl.pallas_call(
        functools.partial(last_kernel, ranks, 2 * chips, gain_row),
        in_specs=[VMEM] * (5 + ranks),
        out_specs=[VMEM] * 3,
        out_shape=[shape_of(x.shape, F32), shape_of(w_shape, BF16), shape_of(r_shape, F32)],
        scratch_shapes=[
            pltpu.VMEM((ranks - 1,) + x.shape, BF16),
            pltpu.VMEM((chips,) + w_shape, BF16),
            pltpu.VMEM((chips,) + r_shape, BF16),
            pltpu.VMEM((chips,) + w_shape, BF16),
            pltpu.VMEM((chips,) + r_shape, BF16),
            pltpu.VMEM((chips - 1,) + w_shape, BF16),
            pltpu.VMEM((chips - 1,) + r_shape, BF16),
            pltpu.VMEM(w_shape, BF16),
            dma((ranks - 1,)),
            dma((ranks - 1,)),
            dma((2, chips)),
            dma((2, chips)),
            dma((2, chips - 1)),
            dma((2, chips - 1)),
            dma((ranks - 1,)),
            dma((ranks - 1,)),
            dma((1,)),
        ],
        compiler_params=remote(3),
        cost_estimate=lasting(60),
        name="last",
    )(x, dh, extra_t, d_weights, d_rows, *sums)


def piece_ids(position_index, starts):
    inside = (position_index[:, None] >= starts[None, :]) & (
        position_index[:, None] < starts[None, :] + PIECE
    )
    labels = jnp.arange(1, starts.shape[0] + 1, dtype=jnp.int32)[None, :]
    return jnp.sum(jnp.where(inside, labels, 0), axis=1, dtype=jnp.int32)


def on_device(
    inputs,
    cotangent,
    norm1_gain,
    w_query,
    key_projection,
    value_projection,
    w_output,
    norm2_gain,
    w_router,
    w_gate,
    w_up,
    w_down,
    routes,
    piece_starts,
):
    plane = Plane()
    ranks = lax.axis_size("expert")
    me = lax.axis_index("expert")
    rows, model = inputs.shape
    seq = rows * ranks
    weight_rows = w_query.shape[0]
    n_experts = w_router.shape[1]
    ff = w_gate.shape[2]
    kv_heads = KEY_VALUE_HEADS // ranks
    q_cols, kv_cols = kv_heads * GROUP * HEAD_WIDTH, kv_heads * HEAD_WIDTH
    rope_width = q_cols + kv_cols
    value_width = -(-kv_cols // LANES) * LANES
    columns = rope_width + value_width + LANES
    gain_one_row, gain_two_row = n_experts, n_experts + 1

    scale_one = lax.rsqrt(jnp.mean(inputs * inputs, axis=-1, keepdims=True) + EPSILON)
    x_own = (inputs * scale_one).astype(BF16)

    extra_cols = jnp.concatenate(
        [
            w_router,
            norm1_gain[:, None],
            norm2_gain[:, None],
            jnp.zeros((weight_rows, LANES - n_experts - 2), F32),
        ],
        axis=1,
    )
    by_rank = jnp.concatenate(
        [
            w_query.reshape(weight_rows, ranks, q_cols),
            key_projection.reshape(weight_rows, ranks, kv_cols),
            jnp.pad(
                value_projection.reshape(weight_rows, ranks, kv_cols),
                ((0, 0), (0, 0), (0, value_width - kv_cols)),
            ),
            jnp.broadcast_to(extra_cols[:, None, :], (weight_rows, ranks, LANES)),
        ],
        axis=2,
    ).astype(BF16)
    by_rank = jnp.transpose(by_rank, (1, 0, 2))

    axes = ("fsdp", "expert")
    total = plane.size * ranks
    move = [
        (j, (j % plane.size) * ranks + j // plane.size) for j in range(total)
    ]
    out_shard = lax.ppermute(w_output.astype(BF16), axes, move)

    lane_ids = jnp.arange(LANES, dtype=jnp.int32)
    routed = jnp.sum((routes[:, :, None] == lane_ids[None, None, :]).astype(F32), axis=1)
    grads_own = jnp.concatenate([cotangent, routed], axis=1).astype(BF16)

    core = plane.core.astype(jnp.int32)[None]
    weights, out_weights, x_all, grads, part_a, part_b, got_a, got_b = gather_weights(
        by_rank, out_shard, x_own, grads_own, w_gate, w_up, w_down, plane.size
    )
    grads = grads.reshape(seq, grads.shape[2])
    found = {(0, 0, 0): part_a, (0, 0, 1): part_b, (0, 1, 0): got_a}
    for s in range(1, plane.rows):
        found[s, 0, 1] = got_b[s - 1]
        for mid in range(2):
            found[s, mid, 0] = plane.next_row(found[0, mid, 0], s)
    for s in range(plane.rows):
        found[s, 1, 1] = plane.other_mid(found[s, 0, 1])
    place, pieces = tuple(found.keys()), list(found.values())
    sources = [
        ((plane.row - s) % plane.rows) * 2 + (plane.mid + mid) % 2
        for s in range(plane.rows)
        for mid in range(2)
    ]
    where = jnp.stack([me] + sources).astype(jnp.int32)

    weights = weights.reshape(model, columns)
    out_weights = out_weights.reshape(q_cols, model)

    block_ids = jnp.arange(seq, dtype=jnp.int32) // rows
    places = ((me - block_ids) % ranks) * rows + jnp.arange(seq, dtype=jnp.int32) % rows
    ids = piece_ids(places, piece_starts[0])
    visible = (places[:, None] <= places[None, :]) | (
        (ids[:, None] == ids[None, :]) & (ids[None, :] > 0)
    )
    bias = jnp.where(visible, 0.0, NEG_FILL).astype(F32)
    half = HEAD_WIDTH // 2
    inverse = 10000.0 ** (-(jnp.arange(half, dtype=F32) * 2.0 / HEAD_WIDTH))
    angles = places.astype(F32)[:, None] * inverse[None, :]
    cosine = jnp.tile(jnp.cos(angles), (1, LANES // half))
    sine = jnp.tile(jnp.sin(angles), (1, LANES // half)) * jnp.where(
        lane_ids % HEAD_WIDTH < half, -1.0, 1.0
    )
    extra_t, kept, (mid_rows, a2, own_a2, other_a2) = attend(
        x_all,
        weights,
        out_weights,
        bias,
        cosine,
        sine,
        inputs,
        gain_one_row,
        kv_heads,
        rope_width,
        plane.size,
    )

    other_grads = plane.other_core(grads)
    other_out, other_dx, _, *other_kept = experts(
        [other_a2.reshape(seq, model)], other_grads, extra_t, where, pieces, place, BF16
    )
    own_a2, other_out, other_dx = lax.optimization_barrier((own_a2, other_out, other_dx))
    out_all, dx_all, gates, *own_kept = experts(
        [own_a2.reshape(seq, model)], grads, extra_t, where, pieces, place, BF16
    )
    dx_all = dx_all.astype(F32) + plane.other_core(other_dx).astype(F32)
    dxs = [
        dx_all[b * rows : (b + 1) * rows].astype(F32 if b == 0 else BF16) for b in range(ranks)
    ]
    dxs, own_kept = lax.optimization_barrier((dxs, own_kept))
    dx_got = expert_scatter(dxs)
    chips = [
        ((plane.row + s) % plane.rows) * 2 + (plane.mid + mid) % 2
        for s in range(plane.rows)
        for mid in range(2)
    ]
    own_kept.insert(2, grads)
    other_kept.insert(2, other_grads)
    flat = expert_grads(
        jnp.stack(chips).astype(jnp.int32), own_kept, other_kept, plane.size, plane.rows
    )
    by_row, by_mid = flat[: plane.rows], flat[plane.rows :]

    def add(first, *others):
        value = first.astype(F32)
        for v in others:
            value = value + v.astype(F32)
        return value.astype(BF16)

    steps = range(1, plane.rows)
    a_first = [plane.next_row(by_row[s], s) for s in steps]
    b_first = plane.other_mid(by_mid[1])

    other_out = plane.other_core(other_out)
    out_all = out_all.astype(F32) + other_out.astype(F32)
    outs = [out_all[b * rows : (b + 1) * rows] for b in range(ranks)]
    outs = [outs[0]] + [v.astype(BF16) for v in outs[1:]]
    outs, dx_own = lax.optimization_barrier((outs, dxs[0]))
    dh, dh_stack, extra = rejoin(
        [dx_own] + dx_got, gates, mid_rows, cotangent, extra_t, a2, gain_two_row, plane.size
    )
    dh_stack, outs = lax.optimization_barrier((dh_stack, outs))
    out_got = expert_scatter(outs)

    d_weights, d_out_weights, da1 = attend_back(
        dh_stack,
        x_all,
        weights,
        out_weights,
        kept,
        bias,
        cosine,
        sine,
        extra,
        kv_heads,
        gain_one_row,
    )
    a_first, b_first, d_weights = lax.optimization_barrier((a_first, b_first, d_weights))
    a_next = add(by_row[0][1], *[v[1] for v in a_first])
    b_next = [add(by_mid[0][s], b_first[s]) for s in steps]
    a_got = plane.other_mid(a_next)
    b_got = [plane.next_row(v, s) for s, v in zip(steps, b_next)]
    a_next, b_next, d_weights, out_got = lax.optimization_barrier(
        (a_next, b_next, d_weights, out_got)
    )
    chip_count = plane.size // 2
    input_grad, by_rank, out_part = last(
        inputs,
        dh,
        extra_t,
        d_weights.reshape(chip_count, 2, ranks, weight_rows, columns),
        d_out_weights.reshape(chip_count, 2, weight_rows, model),
        da1,
        gain_one_row,
    )
    a_got, b_got, out_part = lax.optimization_barrier((a_got, b_got, out_part))
    parts_a = [by_row[0], *a_first, a_got]
    parts_b = [by_mid[0], b_first, *b_got]

    def total(parts):
        value = 0.0
        for v in parts:
            value = value + (v[0] if v.ndim == 5 else v)[:2].astype(F32)
        return value

    other = plane.other_core(
        jnp.where(plane.core == 0, total(parts_b), total(parts_a)).astype(BF16)
    )
    gate_grad, up_grad, down_grad = finish(
        core, parts_a, parts_b, other, w_down.shape[1], model, plane.size
    )
    output = mid_rows + outs[0]
    for v in out_got:
        output = output + v.astype(F32)

    w_output_grad = lax.ppermute(
        out_part.astype(BF16), axes, [(b, a) for a, b in move]
    ).astype(F32)
    by_rank = by_rank.astype(F32)

    def columns_of(start, width):
        piece = by_rank[:, :, start : start + width]
        return jnp.transpose(piece, (1, 0, 2)).reshape(weight_rows, ranks * width)

    extra_grad = jnp.sum(by_rank[:, :, columns - LANES :], axis=0)
    return (
        output,
        input_grad,
        extra_grad[:, gain_one_row],
        columns_of(0, q_cols),
        columns_of(q_cols, kv_cols),
        columns_of(rope_width, kv_cols),
        w_output_grad,
        extra_grad[:, gain_two_row],
        extra_grad[:, :n_experts],
        gate_grad,
        up_grad,
        down_grad,
    )


def solution(mesh):
    both = ("fsdp", "expert")
    rows, flat, stack = P(both, None), P(both), P("expert", "fsdp", None)
    weights = (flat, rows, rows, rows, rows, flat, rows, stack, stack, stack)
    return jax.shard_map(
        on_device,
        mesh=mesh,
        in_specs=(rows, rows) + weights + (rows, P("fsdp", None)),
        out_specs=(rows, rows) + weights,
        check_vma=False,
    )
```

```python
import functools

import jax
import jax.numpy as jnp
from jax import lax
from jax.experimental import pallas as pl
from jax.experimental.pallas import tpu as pltpu
from jax.sharding import PartitionSpec as P

QUERY_HEADS = 24
KEY_VALUE_HEADS = 8
GROUP = QUERY_HEADS // KEY_VALUE_HEADS
HEAD_WIDTH = 64
PIECE = 256
LANES = 128
DEVICE_ROWS = 128
EPSILON = 1e-05
NEG_FILL = -1e30
SCORE_SCALE = HEAD_WIDTH ** (-0.5)
F32 = jnp.float32
BF16 = jnp.bfloat16

VMEM = pl.BlockSpec(memory_space=pltpu.VMEM)
SMEM = pl.BlockSpec(memory_space=pltpu.SMEM)
ANY = pl.BlockSpec(memory_space=pl.ANY)
MESH = pl.DeviceIdType.MESH


def dot(a, b):
    return lax.dot_general(a, b, (((1,), (0,)), ((), ())), preferred_element_type=F32)


def dot_nt(a, b):
    return lax.dot_general(a, b, (((1,), (1,)), ((), ())), preferred_element_type=F32)


def dot_tn(a, b):
    return lax.dot_general(a, b, (((0,), (0,)), ((), ())), preferred_element_type=F32)


def shape_of(dims, dtype):
    return jax.ShapeDtypeStruct(tuple(dims), dtype)


def lasting(us):
    return pl.CostEstimate(flops=us * 10**9, bytes_accessed=us * 10**6, transcendentals=0)


def params(**kw):
    return pltpu.CompilerParams(vmem_limit_bytes=60 * 1024 * 1024, **kw)


class Plane:
    def __init__(self):
        self.size = lax.axis_size("fsdp")
        self.rows = self.size // 4
        index = lax.axis_index("fsdp")
        self.index = index
        self.core = index % 2
        self.mid = (index // 2) % 2
        self.row = index // 4

    def other_core(self, x):
        return lax.ppermute(x, "fsdp", [(i, i ^ 1) for i in range(self.size)])

    def other_mid(self, x):
        return lax.ppermute(x, "fsdp", [(i, i ^ 2) for i in range(self.size)])

    def next_row(self, x, step):
        return lax.ppermute(
            x, "fsdp", [(i, (i // 4 + step) % self.rows * 4 + i % 4) for i in range(self.size)]
        )


def expert_shift(x, step):
    count = lax.axis_size("expert")
    return lax.ppermute(x, "expert", [(i, (i + step) % count) for i in range(count)])


def expert_scatter(blocks):
    count = lax.axis_size("expert")
    return [expert_shift(blocks[s], count - s) for s in range(1, count)]


def chooser(width, blocks, part, dtype=BF16):
    n = width // blocks
    line = lax.broadcasted_iota(jnp.int32, (width // 2, width), 0)
    column = lax.broadcasted_iota(jnp.int32, (width // 2, width), 1)
    want = (2 * (line // n) + part) * n + line % n
    return jnp.where(column == want, 1.0, 0.0).astype(dtype)


def swap_halves(x):
    lane = lax.broadcasted_iota(jnp.int32, x.shape, 1)
    return jnp.where(
        lane % HEAD_WIDTH < HEAD_WIDTH // 2, pltpu.roll(x, LANES - 32, 1), pltpu.roll(x, 32, 1)
    )


def head_slice(ref, start):
    return ref[:, start : start + HEAD_WIDTH]


def experts_kernel(blocks, pieces, place, row_block, *refs):
    a2_in = refs[:blocks]
    grads_in, router_t, where_ref = refs[blocks : blocks + 3]
    piece_refs = refs[blocks + 3 : blocks + 3 + pieces]
    (out_all, dx_all, gates_out, a2_t, hidden_t, d_gate, d_up) = refs[
        blocks + 3 + pieces : blocks + 10 + pieces
    ]
    (a2, gate_w, up_w, down_w, out_sum, dx_sum, gates, dgates, in_sem, w_sem) = refs[
        blocks + 10 + pieces :
    ]
    step, steps = pl.program_id(0), pl.num_programs(0)
    rows = a2_in[0].shape[0]
    seq, model = a2.shape
    depth, width = piece_refs[0].shape[2], gate_w.shape[2]
    down_rows = depth * width // model
    slot = lax.rem(step, 2)

    def fetch(e, to):
        for i, (row_step, mid, part) in enumerate(place):
            source = where_ref[1 + row_step * 2 + mid] * 2 + part
            at = pl.multiple_of(source * depth, 32)
            for which, buf in ((0, gate_w), (1, up_w)):
                pltpu.make_async_copy(
                    piece_refs[i].at[which, e], buf.at[to, pl.ds(at, depth)], w_sem.at[which, to]
                ).start()
            at = pl.multiple_of(source * down_rows, 16)
            for j in range(model // width):
                pltpu.make_async_copy(
                    piece_refs[i].at[2, e, pl.ds(j * down_rows, down_rows)],
                    down_w.at[to, pl.ds(at, down_rows), pl.ds(j * width, width)],
                    w_sem.at[2, to],
                ).start()

    @pl.when(step == 0)
    def _():
        for b in range(blocks):
            pltpu.make_async_copy(
                a2_in[b], a2.at[pl.ds(b * rows, rows)], in_sem.at[0]
            ).start()
        fetch(0, 0)
        pltpu.make_async_copy(a2, a2, in_sem.at[0]).wait()
        logits = dot_nt(a2[...], router_t[...])
        routed = grads_in[:, model:].astype(F32) > 0.5
        top = jnp.max(jnp.where(routed, logits, NEG_FILL), axis=1, keepdims=True)
        weight = jnp.where(routed, jnp.exp(jnp.where(routed, logits, top) - top), 0.0)
        gates[...] = weight / jnp.sum(weight, axis=1, keepdims=True)
        gates_out[...] = gates[: gates_out.shape[0], :]
        dgates[...] = jnp.zeros_like(dgates)
        a2_t[...] = a2[...].T

    @pl.when(step + 1 < steps)
    def _():
        fetch(step + 1, 1 - slot)

    for which, buf in ((0, gate_w), (1, up_w), (2, down_w)):
        pltpu.make_async_copy(buf.at[slot], buf.at[slot], w_sem.at[which, slot]).wait()

    mine = where_ref[0] * steps + step

    def block(i, carry):
        at = pl.ds(pl.multiple_of(i * row_block, row_block), row_block)
        left = a2[at, :]
        gate_lin = dot(left, gate_w[slot])
        up_lin = dot(left, up_w[slot])
        back = dot_nt(grads_in[at, :model], down_w[slot])
        lane = lax.broadcasted_iota(jnp.int32, (row_block, LANES), 1)
        here = lane == mine
        gate = jnp.sum(jnp.where(here, gates[at, :], 0.0), axis=1, keepdims=True)
        sig = 1.0 / (1.0 + jnp.exp(-gate_lin))
        silu = gate_lin * sig
        hidden = silu * up_lin
        dgates[at, :] += jnp.where(here, jnp.sum(hidden * back, axis=1, keepdims=True), 0.0)
        hidden_low = (hidden * gate).astype(BF16)
        d_hidden = back * gate
        d_gate_low = (d_hidden * up_lin * (sig + silu * (1.0 - sig))).astype(BF16)
        d_up_low = (d_hidden * silu).astype(BF16)
        d_gate[at, :] = d_gate_low
        d_up[at, :] = d_up_low
        hidden_t[0, :, at] = hidden_low.T
        out_new = dot(hidden_low, down_w[slot])
        dx_new = dot_nt(d_gate_low, gate_w[slot]) + dot_nt(d_up_low, up_w[slot])

        @pl.when(step == 0)
        def _():
            out_sum[at, :] = out_new
            dx_sum[at, :] = dx_new

        @pl.when(step > 0)
        def _():
            out_sum[at, :] += out_new
            dx_sum[at, :] += dx_new

        return carry

    lax.fori_loop(0, seq // row_block, block, 0)

    @pl.when(step == steps - 1)
    def _():
        high = dgates[...].astype(BF16).astype(F32)
        low = dgates[...] - high
        lane = lax.broadcasted_iota(jnp.int32, high.shape, 1)
        tail = jnp.where(lane < LANES // 2, high, pltpu.roll(low, LANES // 2, 1))
        out_all[...] = out_sum[...].astype(out_all.dtype)
        dx_all[:, :model] = dx_sum[...].astype(dx_all.dtype)
        dx_all[:, model:] = tail.astype(dx_all.dtype)


def experts(a2_blocks, grads, router_t, where, pieces, place, dtype):
    blocks = len(a2_blocks)
    rows, model = a2_blocks[0].shape
    seq = rows * blocks
    local, depth, width = pieces[0].shape[1:]
    outs = [
        shape_of((seq, model), dtype),
        shape_of((seq, model + LANES), dtype),
        shape_of((DEVICE_ROWS, LANES), F32),
        shape_of((model, seq), BF16),
        shape_of((local, width, seq), BF16),
        shape_of((seq, local * width), BF16),
        shape_of((seq, local * width), BF16),
    ]
    whole = lambda dims: pl.BlockSpec(
        dims, lambda e: (0,) * len(dims), pipeline_mode=pl.Buffered(1)
    )
    out_specs = (
        [whole(o.shape) for o in outs[:4]]
        + [pl.BlockSpec((1, width, seq), lambda e: (e, 0, 0))]
        + [pl.BlockSpec((seq, width), lambda e: (0, e))] * 2
    )
    return pl.pallas_call(
        functools.partial(experts_kernel, blocks, len(pieces), place, 256),
        grid=(local,),
        in_specs=[ANY] * blocks
        + [whole(grads.shape), whole(router_t.shape), SMEM]
        + [ANY] * len(pieces),
        out_specs=out_specs,
        out_shape=outs,
        scratch_shapes=[
            pltpu.VMEM((seq, model), BF16),
            pltpu.VMEM((2, model, width), BF16),
            pltpu.VMEM((2, model, width), BF16),
            pltpu.VMEM((2, width, model), BF16),
            pltpu.VMEM((seq, model), F32),
            pltpu.VMEM((seq, model), F32),
            pltpu.VMEM((seq, LANES), F32),
            pltpu.VMEM((seq, LANES), F32),
            pltpu.SemaphoreType.DMA((1,)),
            pltpu.SemaphoreType.DMA((3, 2)),
        ],
        compiler_params=params(dimension_semantics=("arbitrary",)),
        name="experts",
    )(*a2_blocks, grads, router_t, where, *pieces)


def expert_grads_kernel(plane_rows, depth, down_rows, where_ref, *refs):
    (a2_t0, a2_t1, hid0, hid1, grads0, grads1, dg0, dg1, du0, du1) = refs[:10]
    row_outs, mid_outs = refs[10 : 10 + plane_rows], refs[10 + plane_rows : 12 + plane_rows]
    down_sum = refs[12 + plane_rows]
    model, width = a2_t0.shape[0], dg0.shape[1]
    down_sum[...] = (dot(hid0[0], grads0[...]) + dot(hid1[0], grads1[...])).astype(BF16)
    for s in range(plane_rows):
        for mid in range(2):
            source = where_ref[2 * s + mid]
            at = pl.ds(pl.multiple_of(source * 2 * depth, 32), 2 * depth)
            left0, left1 = a2_t0[at, :], a2_t1[at, :]
            gate = (dot(left0, dg0[...]) + dot(left1, dg1[...])).astype(BF16)
            up = (dot(left0, du0[...]) + dot(left1, du1[...])).astype(BF16)
            for part, out in ((0, row_outs[s].at[mid]), (1, mid_outs[mid].at[s])):
                out[0, 0] = gate[part * depth : (part + 1) * depth]
                out[1, 0] = up[part * depth : (part + 1) * depth]
                at = pl.ds(pl.multiple_of((source * 2 + part) * down_rows, 16), down_rows)
                down = down_sum[at, :]
                for j in range(model // width):
                    out[2, 0, j * down_rows : (j + 1) * down_rows, :] = down[
                        :, j * width : (j + 1) * width
                    ]


def expert_grads(where, first, second, plane_size, plane_rows):
    model, seq = first[0].shape
    local, width = first[1].shape[:2]
    depth, down_rows = model // plane_size, width // plane_size
    counts = [2] * plane_rows + [plane_rows] * 2
    once = lambda dims: pl.BlockSpec(dims, lambda e: (0, 0), pipeline_mode=pl.Buffered(1))
    specs = [
        once((model, seq)),
        pl.BlockSpec((1, width, seq), lambda e: (e, 0, 0)),
        once((seq, model)),
        pl.BlockSpec((seq, width), lambda e: (0, e)),
        pl.BlockSpec((seq, width), lambda e: (0, e)),
    ]
    operands = [v for pair in zip(first, second) for v in pair]
    return pl.pallas_call(
        functools.partial(expert_grads_kernel, plane_rows, depth, down_rows),
        grid=(local,),
        in_specs=[SMEM] + [spec for spec in specs for _ in range(2)],
        out_specs=[
            pl.BlockSpec((n, 3, 1, depth, width), lambda e: (0, 0, e, 0, 0)) for n in counts
        ],
        out_shape=[shape_of((n, 3, local, depth, width), BF16) for n in counts],
        scratch_shapes=[pltpu.VMEM((width, model), BF16)],
        compiler_params=params(),
        cost_estimate=lasting(18),
        name="expert_grads",
    )(where, *operands)


def finish_kernel(blocks, count_a, count_b, core, *refs):
    parts_a, parts_b = refs[:count_a], refs[count_a : count_a + count_b]
    other, gate, up, down, choose = refs[count_a + count_b :]
    width, wide = gate.shape[2], other.shape[3]

    @pl.when(pl.program_id(0) == 0)
    def _():
        choose[0] = chooser(width, blocks, core[0])
        choose[1] = chooser(width, blocks, 1 - core[0])

    mine, theirs = choose[0], choose[1]
    first = core[0] == 0

    def total(parts, place):
        value = parts[0][place, 0].astype(F32)
        for part in parts[1:]:
            value = value + part[place, 0].astype(F32)
        return value

    for place, out in ((0, gate), (1, up)):
        kept = jnp.where(first, total(parts_a[:-1], place), total(parts_b[:-1], place))
        got = jnp.where(
            first, parts_a[-1][place, 0].astype(F32), parts_b[-1][place, 0].astype(F32)
        )
        out[0] = (
            dot(kept.astype(BF16), mine)
            + dot(got.astype(BF16), mine)
            + dot(other[place, 0], theirs)
        )
    rows = down.shape[1] // 2
    for part, parts in ((0, parts_a), (1, parts_b)):
        value = total(parts, 2)
        for j in range(value.shape[0] // rows):
            down[0, part * rows : (part + 1) * rows, j * wide : (j + 1) * wide] = value[
                j * rows : (j + 1) * rows
            ]


def finish(core, parts_a, parts_b, other, down_rows, model, blocks):
    local, depth, wide = other.shape[1:]
    block = pl.BlockSpec((3, 1, depth, wide), lambda e: (0, e, 0, 0))
    front = pl.BlockSpec((None, 3, 1, depth, wide), lambda e: (0, 0, e, 0, 0))
    outs = [
        shape_of((local, depth, 2 * wide), F32),
        shape_of((local, depth, 2 * wide), F32),
        shape_of((local, down_rows, model), F32),
    ]
    parts = list(parts_a) + list(parts_b)
    return pl.pallas_call(
        functools.partial(finish_kernel, blocks, len(parts_a), len(parts_b)),
        grid=(local,),
        in_specs=[SMEM]
        + [front if v.ndim == 5 else block for v in parts]
        + [pl.BlockSpec((2, 1, depth, wide), lambda e: (0, e, 0, 0))],
        out_specs=[pl.BlockSpec((1,) + o.shape[1:], lambda e: (e, 0, 0)) for o in outs],
        out_shape=outs,
        scratch_shapes=[pltpu.VMEM((2, wide, 2 * wide), BF16)],
        name="finish",
    )(core, *parts, other)


def attend_back_kernel(blocks, kv_heads, gain_row, *refs):
    dh_ref, x_all = refs[:2]
    (weights, out_weights, a1, qk, val, mixed, maxes, inverse, bias, cosine, sine, extra) = refs[2:14]
    d_weights, d_out_weights = refs[14:16]
    sums = refs[16 : blocks + 16]
    grads, d_mixed, dq_t, d_qk, d_lin = refs[blocks + 16 :]
    rows = x_all.shape[1]
    rope_width, value_width = qk.shape[1], val.shape[1]
    q_width = kv_heads * GROUP * HEAD_WIDTH
    for b in range(blocks):
        grads[b * rows : (b + 1) * rows, :] = dh_ref[b]
    d_mixed[...] = dot_nt(grads[...], out_weights[...]).astype(BF16)
    d_out_weights[...] = dot_tn(mixed[...], grads[...]).astype(BF16)
    if value_width > kv_heads * HEAD_WIDTH:
        d_lin[:, rope_width:] = jnp.zeros((d_lin.shape[0], value_width), BF16)
    for g in range(kv_heads):
        key = head_slice(qk, q_width + g * HEAD_WIDTH)
        key_t = key.T
        value = head_slice(val, g * HEAD_WIDTH)
        d_key, d_value = None, None
        for j in range(GROUP):
            h = g * GROUP + j
            query = head_slice(qk, h * HEAD_WIDTH)
            grad = head_slice(d_mixed, h * HEAD_WIDTH)
            scores = dot_nt(key, query) * SCORE_SCALE + bias[...]
            prob = jnp.exp(scores - maxes[h : h + 1, :]) * inverse[h : h + 1, :]
            d_prob = dot_nt(value, grad)
            inner = jnp.sum(prob * d_prob, axis=0, keepdims=True)
            d_scores = (prob * (d_prob - inner)).astype(BF16)
            dk = dot(d_scores, query)
            dv = dot(prob.astype(BF16), grad)
            d_key = dk if d_key is None else d_key + dk
            d_value = dv if d_value is None else d_value + dv
            dq_t[h * HEAD_WIDTH : (h + 1) * HEAD_WIDTH, :] = dot(key_t, d_scores)
        start = q_width + g * HEAD_WIDTH
        d_qk[:, start : start + HEAD_WIDTH] = d_key * SCORE_SCALE
        start = rope_width + g * HEAD_WIDTH
        d_lin[:, start : start + HEAD_WIDTH] = d_value.astype(BF16)
    d_qk[:, :q_width] = dq_t[...].T * SCORE_SCALE
    for c in range(rope_width // LANES):
        at = slice(c * LANES, (c + 1) * LANES)
        x = d_qk[:, at]
        d_lin[:, at] = (x * cosine[...] - swap_halves(x) * sine[...]).astype(BF16)
    total = dot_nt(d_lin[...], weights[:, : rope_width + value_width])
    gain_grad = None
    for b in range(blocks):
        part = total[b * rows : (b + 1) * rows, :]
        sums[b][...] = part.astype(sums[b].dtype)
        new = jnp.sum(part * x_all[b].astype(F32), axis=0, keepdims=True)
        gain_grad = new if gain_grad is None else gain_grad + new
    d_weights[:, : rope_width + value_width] = dot_tn(a1[...], d_lin[...]).astype(BF16)
    line = lax.broadcasted_iota(jnp.int32, extra.shape, 0)
    tail = jnp.where(line == gain_row, gain_grad, extra[...])
    d_weights[:, rope_width + value_width :] = tail.T.astype(BF16)


def attend_back(
    dh_stack, x_all, weights, out_weights, kept, bias, cosine, sine, extra, kv_heads, gain_row
):
    blocks, rows, model = dh_stack.shape
    seq = rows * blocks
    q_width = out_weights.shape[0]
    rope_width, value_width = kept[1].shape[1], kept[2].shape[1]
    outs = [shape_of(weights.shape, BF16), shape_of(out_weights.shape, BF16)] + [
        shape_of((rows, model), F32 if b == 0 else BF16) for b in range(blocks)
    ]
    out = pl.pallas_call(
        functools.partial(attend_back_kernel, blocks, kv_heads, gain_row),
        in_specs=[VMEM] * 14,
        out_specs=[VMEM] * len(outs),
        out_shape=outs,
        scratch_shapes=[
            pltpu.VMEM((seq, model), BF16),
            pltpu.VMEM((seq, q_width), BF16),
            pltpu.VMEM((q_width, seq), F32),
            pltpu.VMEM((seq, rope_width), F32),
            pltpu.VMEM((seq, rope_width + value_width), BF16),
        ],
        compiler_params=params(),
        cost_estimate=lasting(16),
        name="attend_back",
    )(dh_stack, x_all, weights, out_weights, *kept, bias, cosine, sine, extra)
    return out[0], out[1], out[2:]


class Spot:
    def __init__(self, ranks, plane_size):
        self.ranks, self.chips = ranks, plane_size // 2
        self.rank = lax.axis_index("expert")
        self.index = lax.axis_index("fsdp")
        self.chip = self.index // 2
        self.core = self.index % 2

    def behind(self, s):
        return {"expert": lax.rem(self.rank - s + self.ranks, self.ranks)}

    def ahead(self, s):
        return {"expert": lax.rem(self.rank + s, self.ranks)}

    def partner(self):
        return {"fsdp": self.chip * 2 + (1 - self.core)}

    def chip_ahead(self, k):
        return lax.rem(self.chip + k, self.chips)

    def chip_behind(self, k):
        return lax.rem(self.chip - k + self.chips, self.chips)

    def on_chip(self, chip):
        return {"fsdp": chip * 2 + self.core}


def greet(peers):
    barrier = pltpu.get_barrier_semaphore()
    for peer in peers:
        pl.semaphore_signal(barrier, inc=1, device_id=peer, device_id_type=MESH)


def await_peers(peers):
    pl.semaphore_wait(pltpu.get_barrier_semaphore(), len(peers))


def meet(peers):
    greet(peers)
    await_peers(peers)


def send(src, dst, send_sem, recv_sem, peer):
    copy = pltpu.make_async_remote_copy(
        src_ref=src,
        dst_ref=dst,
        send_sem=send_sem,
        recv_sem=recv_sem,
        device_id=peer,
        device_id_type=MESH,
    )
    copy.start()
    return copy


def remote(collective_id):
    return params(collective_id=collective_id, has_side_effects=True)


def pack_experts(spot, w_gate, w_up, w_down, held, outgoing):
    local, width = w_gate.shape[0], w_gate.shape[2]
    mine = chooser(width, 2 * spot.chips, spot.core)
    theirs = chooser(width, 2 * spot.chips, 1 - spot.core)
    rows, wide = w_down.shape[1] // 2, width // 2

    def one(e, carry):
        for place, ref in ((0, w_gate), (1, w_up)):
            value = ref[e].astype(BF16)
            kept = dot_nt(value, mine).astype(BF16)
            for part in range(2):

                @pl.when(spot.core == part)
                def _():
                    held[part][place, e] = kept

            outgoing[place, e] = dot_nt(value, theirs).astype(BF16)
        value = w_down[e].astype(BF16)
        for part in range(2):
            for j in range(value.shape[1] // wide):
                held[part][2, e, j * rows : (j + 1) * rows] = value[
                    part * rows : (part + 1) * rows, j * wide : (j + 1) * wide
                ]
        return carry

    lax.fori_loop(0, local, one, 0)


def gather_weights_kernel(ranks, plane_size, *refs):
    by_rank, rows_in, x_in, grads_in, w_gate, w_up, w_down = refs[:7]
    weights, out_rows, x_all, grads_all, parts_a, parts_b, got_a, got_b = refs[7:15]
    held_a, held_b, outgoing = refs[15:18]
    z_send, z_recv, p_send, p_recv, c_send, c_recv, local, e_send, e_recv = refs[18:27]
    x_send, x_recv, grads_send, grads_recv = refs[27:]
    spot = Spot(ranks, plane_size)
    f, me, chips, core = spot.index, spot.rank, spot.chips, spot.core
    others = range(1, ranks)
    kept = [
        pltpu.make_async_copy(by_rank.at[me], weights.at[f, me], local.at[0]),
        pltpu.make_async_copy(rows_in, out_rows.at[f], local.at[1]),
        pltpu.make_async_copy(x_in, x_all.at[0], local.at[2]),
        pltpu.make_async_copy(grads_in, grads_all.at[0], local.at[3]),
    ]
    for copy in kept:
        copy.start()
    meet(
        [spot.ahead(s) for s in others]
        + [spot.on_chip(spot.chip_ahead(k)) for k in range(1, chips)]
        + [spot.partner()]
    )
    z_copies = [
        send(
            by_rank.at[lax.rem(me + s, ranks)],
            weights.at[f, me],
            z_send.at[s - 1],
            z_recv.at[s - 1],
            spot.ahead(s),
        )
        for s in others
    ]
    lines = [
        LineGather(spot, x_all, x_send, x_recv),
        LineGather(spot, grads_all, grads_send, grads_recv),
    ]

    def spread(which, src, buf):
        return [
            send(
                src,
                buf.at[f],
                p_send.at[which, k - 1],
                p_recv.at[which, k - 1],
                spot.on_chip(spot.chip_ahead(k)),
            )
            for k in range(1, chips)
        ] + [send(src, buf.at[f], c_send.at[which, 0], c_recv.at[which, 0], spot.partner())]

    row_copies = spread(1, rows_in, out_rows)
    for copy in kept:
        copy.wait()
    for line in lines:
        line.start(0)

    pack_experts(spot, w_gate, w_up, w_down, (held_a, held_b), outgoing)

    def swap(part, held):
        return pltpu.make_async_remote_copy(
            src_ref=outgoing,
            dst_ref=held.at[pl.ds(0, 2)],
            send_sem=e_send.at[0],
            recv_sem=e_recv.at[0],
            device_id=spot.partner(),
            device_id_type=MESH,
        )

    for part, held in ((0, held_a), (1, held_b)):

        @pl.when(core == part)
        def _():
            swap(part, held).start()

    for copy in z_copies:
        copy.wait()
    weight_copies = spread(0, weights.at[f], weights)
    for part, held in ((0, held_a), (1, held_b)):

        @pl.when(core == part)
        def _():
            swap(part, held).wait_send()

        @pl.when(core == 1 - part)
        def _():
            swap(part, held).wait_recv()

    row, mid = spot.chip // 2, lax.rem(spot.chip, 2)
    expert_copies = [
        send(held_a, got_a, e_send.at[1], e_recv.at[1], spot.on_chip(row * 2 + (1 - mid)))
    ] + [
        send(
            held_b,
            got_b.at[s - 1],
            e_send.at[1 + s],
            e_recv.at[1 + s],
            spot.on_chip(lax.rem(row + s, chips // 2) * 2 + mid),
        )
        for s in range(1, chips // 2)
    ]
    stores = [
        pltpu.make_async_copy(held_a, parts_a, local.at[4]),
        pltpu.make_async_copy(held_b, parts_b, local.at[5]),
    ]
    for copy in stores:
        copy.start()
    waits = []
    for hop in range(ranks - 1):
        for line in lines:
            line.arrive(hop)
            if hop + 1 < line.hops:
                line.start(hop + 1)
    for k in range(1, chips):
        source = spot.chip_behind(k) * 2 + core
        for which, copies, buf in ((1, row_copies, out_rows), (0, weight_copies, weights)):
            copies[k - 1].wait()
            waits.append(
                send(
                    buf.at[source],
                    buf.at[source],
                    c_send.at[which, k],
                    c_recv.at[which, k],
                    spot.partner(),
                )
            )
    row_copies[-1].wait()
    weight_copies[-1].wait()
    for copy in waits + stores + expert_copies:
        copy.wait()
    for line in lines:
        line.drain()


def gather_weights(by_rank, rows_in, x_in, grads_in, w_gate, w_up, w_down, plane_size):
    ranks, rows, columns = by_rank.shape
    chips = plane_size // 2
    local, depth, width = w_gate.shape
    dma = pltpu.SemaphoreType.DMA
    half = (local, depth, width // 2)
    return pl.pallas_call(
        functools.partial(gather_weights_kernel, ranks, plane_size),
        in_specs=[VMEM] * 7,
        out_specs=[VMEM] * 4 + [ANY] * 4,
        out_shape=[
            shape_of((plane_size, ranks, rows, columns), BF16),
            shape_of((plane_size,) + rows_in.shape, BF16),
            shape_of((ranks,) + x_in.shape, BF16),
            shape_of((ranks,) + grads_in.shape, BF16),
            shape_of((3,) + half, BF16),
            shape_of((3,) + half, BF16),
            shape_of((3,) + half, BF16),
            shape_of((chips // 2 - 1, 3) + half, BF16),
        ],
        scratch_shapes=[
            pltpu.VMEM((3,) + half, BF16),
            pltpu.VMEM((3,) + half, BF16),
            pltpu.VMEM((2,) + half, BF16),
            dma((ranks - 1,)),
            dma((ranks - 1,)),
            dma((2, chips - 1)),
            dma((2, chips - 1)),
            dma((2, chips)),
            dma((2, chips)),
            dma((6,)),
            dma((1 + chips // 2,)),
            dma((1 + chips // 2,)),
        ]
        + [dma((2, ranks - 1))] * 4,
        compiler_params=remote(0),
        name="gather_weights",
    )(by_rank, rows_in, x_in, grads_in, w_gate, w_up, w_down)


def scatter_start(spot, refs, buf, send_sem, recv_sem):
    return [
        send(refs[s], buf.at[s - 1], send_sem.at[s - 1], recv_sem.at[s - 1], spot.behind(s))
        for s in range(1, spot.ranks)
    ]


class LineGather:
    def __init__(self, spot, buf, send_sem, recv_sem, part=0, parts=1):
        self.spot, self.buf, self.sems = spot, buf, (send_sem, recv_sem)
        count = buf.shape[1] // parts
        self.rows = pl.ds(part * count, count)
        me, n = spot.rank, spot.ranks
        self.hops = n - 1
        self.sends = [(me - h >= 0) & (me + 1 < n) for h in range(n - 1)], [
            (me + h < n) & (me >= 1) for h in range(n - 1)
        ]
        self.gets = [me - 1 - h >= 0 for h in range(n - 1)], [
            me + 1 + h < n for h in range(n - 1)
        ]

    def slots(self, way, h):
        n = self.spot.ranks
        return (h, h + 1) if way == 0 else ((n - h) % n, n - h - 1)

    def copy(self, way, h):
        source, target = self.slots(way, h)
        return pltpu.make_async_remote_copy(
            src_ref=self.buf.at[source, self.rows],
            dst_ref=self.buf.at[target, self.rows],
            send_sem=self.sems[0].at[way, h],
            recv_sem=self.sems[1].at[way, h],
            device_id=self.spot.ahead(1) if way == 0 else self.spot.behind(1),
            device_id_type=MESH,
        )

    def start(self, h):
        for way in range(2):

            @pl.when(self.sends[way][h])
            def _():
                self.copy(way, h).start()

    def arrive(self, h):
        for way in range(2):

            @pl.when(self.gets[way][h])
            def _():
                self.copy(way, h).wait_recv()

    def passed(self, h, then):
        for way in range(2):

            @pl.when(self.gets[way][h])
            def _():
                then(self.slots(way, h)[1])

    def drain(self):
        for h in range(self.hops):
            for way in range(2):

                @pl.when(self.sends[way][h])
                def _():
                    self.copy(way, h).wait_send()


class LineScatter:
    def __init__(self, spot, coming, going, send_sem, recv_sem):
        self.spot, self.coming, self.going, self.sems = spot, coming, going, (send_sem, recv_sem)
        me, n = spot.rank, spot.ranks
        self.more = me >= 1, me + 1 < n
        self.goes = [(me + t < n, me - t >= 0) for t in range(n)]

    def copy(self, way, t):
        return pltpu.make_async_remote_copy(
            src_ref=self.going.at[way, t - 1],
            dst_ref=self.coming.at[way, t - 1],
            send_sem=self.sems[0].at[way, t - 1],
            recv_sem=self.sems[1].at[way, t - 1],
            device_id=self.spot.ahead(1) if way == 0 else self.spot.behind(1),
            device_id_type=MESH,
        )

    def run(self, own, total):
        n = self.spot.ranks
        for t in range(n - 1, 0, -1):
            for way in range(2):
                slot = n - t if way == 0 else t

                @pl.when(self.goes[t][way])
                def _():
                    if t == n - 1:
                        self.going[way, t - 1] = own[slot].astype(BF16)
                    else:

                        @pl.when(self.more[way])
                        def _():
                            self.copy(way, t + 1).wait_recv()
                            self.going[way, t - 1] = (
                                own[slot] + self.coming[way, t].astype(F32)
                            ).astype(BF16)

                        @pl.when(jnp.logical_not(self.more[way]))
                        def _():
                            self.going[way, t - 1] = own[slot].astype(BF16)

                    self.copy(way, t).start()

        for way in range(2):

            @pl.when(self.more[way])
            def _():
                self.copy(way, 1).wait_recv()
                total[...] += self.coming[way, 0].astype(F32)

    def drain(self):
        for t in range(self.spot.ranks - 1, 0, -1):
            for way in range(2):

                @pl.when(self.goes[t][way])
                def _():
                    self.copy(way, t).wait_send()


def half_lines(spot, buf, send_sem, recv_sem):
    return [LineGather(spot, buf, send_sem.at[k], recv_sem.at[k], k, 2) for k in range(2)]


def attend_kernel(ranks, plane_size, kv_heads, gain_row, *refs):
    x_all, weights, out_weights, bias, cosine, sine, x = refs[:7]
    (extra_t, a1, qk, val, mixed, maxes, inverse, h_out, a2, gathered, other) = refs[7:18]
    mixed_t, sums, got, going, r_send, r_recv, g_send, g_recv, c_send, c_recv = refs[18:]
    extra_t[...] = weights[:, weights.shape[1] - LANES :].T
    gain = extra_t[gain_row : gain_row + 1, :].astype(F32)
    gain_two = extra_t[gain_row + 1 : gain_row + 2, :].astype(F32)
    spot = Spot(ranks, plane_size)
    peers = [spot.ahead(s) for s in range(1, ranks)] + [spot.partner()]
    greet(peers)
    rows = x_all.shape[1]
    rope_width = qk.shape[1]
    q_width = kv_heads * GROUP * HEAD_WIDTH
    for b in range(ranks):
        a1[b * rows : (b + 1) * rows, :] = (x_all[b].astype(F32) * gain).astype(BF16)
    linear = dot(a1[...], weights[:, : rope_width + val.shape[1]])
    for c in range(rope_width // LANES):
        part = linear[:, c * LANES : (c + 1) * LANES]
        qk[:, c * LANES : (c + 1) * LANES] = (
            part * cosine[...] + swap_halves(part) * sine[...]
        ).astype(BF16)
    val[...] = linear[:, rope_width:].astype(BF16)
    for g in range(kv_heads):
        key = head_slice(qk, q_width + g * HEAD_WIDTH)
        value_t = head_slice(val, g * HEAD_WIDTH).T
        for j in range(GROUP):
            h = g * GROUP + j
            scores = dot_nt(key, head_slice(qk, h * HEAD_WIDTH)) * SCORE_SCALE + bias[...]
            top = jnp.max(scores, axis=0, keepdims=True)
            weight = jnp.exp(scores - top)
            inv = 1.0 / jnp.sum(weight, axis=0, keepdims=True)
            maxes[h : h + 1, :] = top
            inverse[h : h + 1, :] = inv
            mixed_t[h * HEAD_WIDTH : (h + 1) * HEAD_WIDTH, :] = dot(
                value_t, (weight * inv).astype(BF16)
            )
    mixed[...] = mixed_t[...].T.astype(BF16)
    await_peers(peers)
    total = dot(mixed[...], out_weights[...])
    for b in range(ranks):
        sums[b] = total[b * rows : (b + 1) * rows, :]
    h_out[...] = x[...] + sums[0]
    scatter = LineScatter(spot, got, going, r_send, r_recv)
    scatter.run(sums, h_out)
    total = h_out[...]
    scale = lax.rsqrt(jnp.mean(total * total, axis=-1, keepdims=True) + EPSILON)
    low = (total * scale * gain_two).astype(BF16)
    gathered[0] = low
    lines = half_lines(spot, gathered, g_send, g_recv)
    for line in lines:
        line.start(0)

    def across(s, part):
        return pltpu.make_async_remote_copy(
            src_ref=gathered.at[s, lines[part].rows],
            dst_ref=other.at[s, lines[part].rows],
            send_sem=c_send.at[part, s],
            recv_sem=c_recv.at[part, s],
            device_id=spot.partner(),
            device_id_type=MESH,
        )

    for part in range(2):
        across(0, part).start()
    a2[...] = low
    for hop in range(ranks - 1):
        for part, line in enumerate(lines):
            line.arrive(hop)
            if hop + 1 < line.hops:
                line.start(hop + 1)
            line.passed(hop, lambda s: across(s, part).start())
    scatter.drain()
    for part, line in enumerate(lines):
        line.drain()
        for s in range(ranks):
            across(s, part).wait()


def attend(
    x_all, weights, out_weights, bias, cosine, sine, x, gain_row, kv_heads, rope_width, plane_size
):
    ranks, rows, model = x_all.shape
    seq = rows * ranks
    q_width = kv_heads * GROUP * HEAD_WIDTH
    value_width = weights.shape[1] - LANES - rope_width
    heads = kv_heads * GROUP
    stack = shape_of((ranks, rows, model), BF16)
    outs = [
        shape_of((LANES, model), BF16),
        shape_of((seq, model), BF16),
        shape_of((seq, rope_width), BF16),
        shape_of((seq, value_width), BF16),
        shape_of((seq, q_width), BF16),
        shape_of((heads, seq), F32),
        shape_of((heads, seq), F32),
        shape_of((rows, model), F32),
        shape_of((rows, model), BF16),
        stack,
        stack,
    ]
    dma = pltpu.SemaphoreType.DMA
    out = pl.pallas_call(
        functools.partial(attend_kernel, ranks, plane_size, kv_heads, gain_row),
        in_specs=[VMEM] * 7,
        out_specs=[VMEM] * len(outs),
        out_shape=outs,
        scratch_shapes=[
            pltpu.VMEM((q_width, seq), F32),
            pltpu.VMEM((ranks, rows, model), F32),
            pltpu.VMEM((2, ranks - 1, rows, model), BF16),
            pltpu.VMEM((2, ranks - 1, rows, model), BF16),
            dma((2, ranks - 1)),
            dma((2, ranks - 1)),
            dma((2, 2, ranks - 1)),
            dma((2, 2, ranks - 1)),
            dma((2, ranks)),
            dma((2, ranks)),
        ],
        compiler_params=remote(1),
        name="attend",
    )(x_all, weights, out_weights, bias, cosine, sine, x)
    return out[0], out[1:7], out[7:]


def rejoin_kernel(ranks, plane_size, gain_row, gates, h, dz, router_t, a2, *refs):
    parts = refs[:ranks]
    dh, gathered, extra, g_send, g_recv = refs[ranks:]
    model = h.shape[1]
    spot = Spot(ranks, plane_size)
    meet([spot.ahead(s) for s in range(1, ranks)])
    total = parts[0][...]
    for i in range(1, ranks):
        total = total + parts[i][...].astype(F32)
    tail = total[:, model:]
    dgates = tail + pltpu.roll(tail, LANES // 2, 1)
    gate = gates[...]
    mean = jnp.sum(gate * dgates, axis=1, keepdims=True)
    d_logits = (gate * (dgates - mean)).astype(BF16)
    da2 = total[:, :model] + dot(d_logits, router_t[...])
    value = h[...]
    scale = lax.rsqrt(jnp.mean(value * value, axis=-1, keepdims=True) + EPSILON)
    normed = value * scale
    gain = router_t[gain_row : gain_row + 1, :].astype(F32)
    weighted = da2 * gain
    grad = dz[...] + scale * (
        weighted - normed * jnp.mean(weighted * normed, axis=-1, keepdims=True)
    )
    gathered[0] = grad.astype(BF16)
    dh[...] = grad
    lines = half_lines(spot, gathered, g_send, g_recv)
    for line_out in lines:
        line_out.start(0)
    gain_grad = jnp.sum(da2 * normed, axis=0, keepdims=True)
    line = lax.broadcasted_iota(jnp.int32, (LANES, model), 0)
    extra[...] = jnp.where(line == gain_row, gain_grad, dot_tn(d_logits, a2[...]))
    for hop in range(ranks - 1):
        for line_out in lines:
            line_out.arrive(hop)
            if hop + 1 < line_out.hops:
                line_out.start(hop + 1)
    for line_out in lines:
        line_out.drain()


def rejoin(parts, gates, h, dz, router_t, a2, gain_row, plane_size):
    ranks = len(parts)
    dma = pltpu.SemaphoreType.DMA
    return pl.pallas_call(
        functools.partial(rejoin_kernel, ranks, plane_size, gain_row),
        in_specs=[VMEM] * (5 + ranks),
        out_specs=[VMEM] * 3,
        out_shape=[
            shape_of(h.shape, F32),
            shape_of((ranks,) + h.shape, BF16),
            shape_of((LANES, h.shape[1]), F32),
        ],
        scratch_shapes=[dma((2, 2, ranks - 1)), dma((2, 2, ranks - 1))],
        compiler_params=remote(2),
        cost_estimate=lasting(35),
        name="rejoin",
    )(gates, h, dz, router_t, a2, *parts)


def last_kernel(ranks, plane_size, gain_row, x, dh, extra_t, d_weights, d_rows, *refs):
    sums = refs[:ranks]
    out, columns_out, rows_out = refs[ranks : ranks + 3]
    (got, core_w, core_r, sum_w, sum_r, chip_w, chip_r, final) = refs[ranks + 3 : ranks + 11]
    r_send, r_recv, c_send, c_recv, p_send, p_recv, z_send, z_recv, local = refs[ranks + 11 :]
    spot = Spot(ranks, plane_size)
    chips, core, me = spot.chips, spot.core, spot.rank
    meet(
        [spot.ahead(s) for s in range(1, ranks)]
        + [spot.on_chip(spot.chip_ahead(k)) for k in range(1, chips)]
        + [spot.partner()]
    )
    z_copies = scatter_start(spot, sums, got, r_send, r_recv)
    pairs = ((0, d_weights, core_w, sum_w, chip_w), (1, d_rows, core_r, sum_r, chip_r))
    across = {}
    for k in range(chips):
        at = spot.chip_ahead(k)
        for which, src, buf, _, _ in pairs:
            across[k, which] = send(
                src.at[at, 1 - core],
                buf.at[k],
                c_send.at[which, k],
                c_recv.at[which, k],
                spot.partner(),
            )
    for k in list(range(1, chips)) + [0]:
        at = spot.chip_ahead(k)
        for which, src, buf, total, _ in pairs:
            across[k, which].wait()
            total[k] = (src[at, core].astype(F32) + buf[k].astype(F32)).astype(BF16)
    hops = {}
    for k in range(1, chips):
        for which, _, _, total, buf in pairs:
            hops[k, which] = send(
                total.at[k],
                buf.at[k - 1],
                p_send.at[which, k - 1],
                p_recv.at[which, k - 1],
                spot.on_chip(spot.chip_ahead(k)),
            )
    value = x[...]
    scale = lax.rsqrt(jnp.mean(value * value, axis=-1, keepdims=True) + EPSILON)
    normed = value * scale
    total = sums[0][...]
    for s in range(1, ranks):
        z_copies[s - 1].wait()
        total = total + got[s - 1].astype(F32)
    weighted = total * extra_t[gain_row : gain_row + 1, :].astype(F32)
    grad = scale * (weighted - normed * jnp.mean(weighted * normed, axis=-1, keepdims=True))
    for k in range(1, chips):
        for which in range(2):
            hops[k, which].wait()
    value = sum_w[0].astype(F32)
    for k in range(1, chips):
        value = value + chip_w[k - 1].astype(F32)
    final[...] = value.astype(BF16)
    out[...] = dh[...] + grad
    value = sum_r[0].astype(F32)
    for k in range(1, chips):
        value = value + chip_r[k - 1].astype(F32)
    rows_out[...] = value.astype(BF16)
    kept = pltpu.make_async_copy(final.at[me], columns_out.at[me], local.at[0])
    kept.start()
    copies = [
        send(
            final.at[lax.rem(me + s, ranks)],
            columns_out.at[me],
            z_send.at[s - 1],
            z_recv.at[s - 1],
            spot.ahead(s),
        )
        for s in range(1, ranks)
    ]
    for copy in copies:
        copy.wait()
    kept.wait()


def last(x, dh, extra_t, d_weights, d_rows, sums, gain_row):
    ranks = len(sums)
    chips, _, _, rows, columns = d_weights.shape
    dma = pltpu.SemaphoreType.DMA
    w_shape, r_shape = d_weights.shape[2:], d_rows.shape[2:]
    return pl.pallas_call(
        functools.partial(last_kernel, ranks, 2 * chips, gain_row),
        in_specs=[VMEM] * (5 + ranks),
        out_specs=[VMEM] * 3,
        out_shape=[shape_of(x.shape, F32), shape_of(w_shape, BF16), shape_of(r_shape, BF16)],
        scratch_shapes=[
            pltpu.VMEM((ranks - 1,) + x.shape, BF16),
            pltpu.VMEM((chips,) + w_shape, BF16),
            pltpu.VMEM((chips,) + r_shape, BF16),
            pltpu.VMEM((chips,) + w_shape, BF16),
            pltpu.VMEM((chips,) + r_shape, BF16),
            pltpu.VMEM((chips - 1,) + w_shape, BF16),
            pltpu.VMEM((chips - 1,) + r_shape, BF16),
            pltpu.VMEM(w_shape, BF16),
            dma((ranks - 1,)),
            dma((ranks - 1,)),
            dma((2, chips)),
            dma((2, chips)),
            dma((2, chips - 1)),
            dma((2, chips - 1)),
            dma((ranks - 1,)),
            dma((ranks - 1,)),
            dma((1,)),
        ],
        compiler_params=remote(3),
        cost_estimate=lasting(60),
        name="last",
    )(x, dh, extra_t, d_weights, d_rows, *sums)


def piece_ids(position_index, starts):
    inside = (position_index[:, None] >= starts[None, :]) & (
        position_index[:, None] < starts[None, :] + PIECE
    )
    labels = jnp.arange(1, starts.shape[0] + 1, dtype=jnp.int32)[None, :]
    return jnp.sum(jnp.where(inside, labels, 0), axis=1, dtype=jnp.int32)


def on_device(
    inputs,
    cotangent,
    norm1_gain,
    w_query,
    key_projection,
    value_projection,
    w_output,
    norm2_gain,
    w_router,
    w_gate,
    w_up,
    w_down,
    routes,
    piece_starts,
):
    plane = Plane()
    ranks = lax.axis_size("expert")
    me = lax.axis_index("expert")
    rows, model = inputs.shape
    seq = rows * ranks
    weight_rows = w_query.shape[0]
    n_experts = w_router.shape[1]
    ff = w_gate.shape[2]
    kv_heads = KEY_VALUE_HEADS // ranks
    q_cols, kv_cols = kv_heads * GROUP * HEAD_WIDTH, kv_heads * HEAD_WIDTH
    rope_width = q_cols + kv_cols
    value_width = -(-kv_cols // LANES) * LANES
    columns = rope_width + value_width + LANES
    gain_one_row, gain_two_row = n_experts, n_experts + 1

    scale_one = lax.rsqrt(jnp.mean(inputs * inputs, axis=-1, keepdims=True) + EPSILON)
    x_own = (inputs * scale_one).astype(BF16)

    extra_cols = jnp.concatenate(
        [
            w_router,
            norm1_gain[:, None],
            norm2_gain[:, None],
            jnp.zeros((weight_rows, LANES - n_experts - 2), F32),
        ],
        axis=1,
    )
    by_rank = jnp.concatenate(
        [
            w_query.reshape(weight_rows, ranks, q_cols),
            key_projection.reshape(weight_rows, ranks, kv_cols),
            jnp.pad(
                value_projection.reshape(weight_rows, ranks, kv_cols),
                ((0, 0), (0, 0), (0, value_width - kv_cols)),
            ),
            jnp.broadcast_to(extra_cols[:, None, :], (weight_rows, ranks, LANES)),
        ],
        axis=2,
    ).astype(BF16)
    by_rank = jnp.transpose(by_rank, (1, 0, 2))

    axes = ("fsdp", "expert")
    total = plane.size * ranks
    move = [
        (j, (j % plane.size) * ranks + j // plane.size) for j in range(total)
    ]
    out_shard = lax.ppermute(w_output.astype(BF16), axes, move)

    lane_ids = jnp.arange(LANES, dtype=jnp.int32)
    routed = jnp.sum((routes[:, :, None] == lane_ids[None, None, :]).astype(F32), axis=1)
    grads_own = jnp.concatenate([cotangent, routed], axis=1).astype(BF16)

    core = plane.core.astype(jnp.int32)[None]
    weights, out_weights, x_all, grads, part_a, part_b, got_a, got_b = gather_weights(
        by_rank, out_shard, x_own, grads_own, w_gate, w_up, w_down, plane.size
    )
    grads = grads.reshape(seq, grads.shape[2])
    found = {(0, 0, 0): part_a, (0, 0, 1): part_b, (0, 1, 0): got_a}
    for s in range(1, plane.rows):
        found[s, 0, 1] = got_b[s - 1]
        for mid in range(2):
            found[s, mid, 0] = plane.next_row(found[0, mid, 0], s)
    for s in range(plane.rows):
        found[s, 1, 1] = plane.other_mid(found[s, 0, 1])
    place, pieces = tuple(found.keys()), list(found.values())
    sources = [
        ((plane.row - s) % plane.rows) * 2 + (plane.mid + mid) % 2
        for s in range(plane.rows)
        for mid in range(2)
    ]
    where = jnp.stack([me] + sources).astype(jnp.int32)

    weights = weights.reshape(model, columns)
    out_weights = out_weights.reshape(q_cols, model)

    block_ids = jnp.arange(seq, dtype=jnp.int32) // rows
    places = ((me - block_ids) % ranks) * rows + jnp.arange(seq, dtype=jnp.int32) % rows
    ids = piece_ids(places, piece_starts[0])
    visible = (places[:, None] <= places[None, :]) | (
        (ids[:, None] == ids[None, :]) & (ids[None, :] > 0)
    )
    bias = jnp.where(visible, 0.0, NEG_FILL).astype(F32)
    half = HEAD_WIDTH // 2
    inverse = 10000.0 ** (-(jnp.arange(half, dtype=F32) * 2.0 / HEAD_WIDTH))
    angles = places.astype(F32)[:, None] * inverse[None, :]
    cosine = jnp.tile(jnp.cos(angles), (1, LANES // half))
    sine = jnp.tile(jnp.sin(angles), (1, LANES // half)) * jnp.where(
        lane_ids % HEAD_WIDTH < half, -1.0, 1.0
    )
    extra_t, kept, (mid_rows, a2, own_a2, other_a2) = attend(
        x_all,
        weights,
        out_weights,
        bias,
        cosine,
        sine,
        inputs,
        gain_one_row,
        kv_heads,
        rope_width,
        plane.size,
    )

    other_grads = plane.other_core(grads)
    other_out, other_dx, _, *other_kept = experts(
        [other_a2.reshape(seq, model)], other_grads, extra_t, where, pieces, place, BF16
    )
    own_a2, other_out, other_dx = lax.optimization_barrier((own_a2, other_out, other_dx))
    out_all, dx_all, gates, *own_kept = experts(
        [own_a2.reshape(seq, model)], grads, extra_t, where, pieces, place, BF16
    )
    dx_all = dx_all.astype(F32) + plane.other_core(other_dx).astype(F32)
    dxs = [
        dx_all[b * rows : (b + 1) * rows].astype(F32 if b == 0 else BF16) for b in range(ranks)
    ]
    dxs, own_kept = lax.optimization_barrier((dxs, own_kept))
    dx_got = expert_scatter(dxs)
    chips = [
        ((plane.row + s) % plane.rows) * 2 + (plane.mid + mid) % 2
        for s in range(plane.rows)
        for mid in range(2)
    ]
    own_kept.insert(2, grads)
    other_kept.insert(2, other_grads)
    flat = expert_grads(
        jnp.stack(chips).astype(jnp.int32), own_kept, other_kept, plane.size, plane.rows
    )
    by_row, by_mid = flat[: plane.rows], flat[plane.rows :]

    def add(first, *others):
        value = first.astype(F32)
        for v in others:
            value = value + v.astype(F32)
        return value.astype(BF16)

    steps = range(1, plane.rows)
    a_first = [plane.next_row(by_row[s], s) for s in steps]
    b_first = plane.other_mid(by_mid[1])

    other_out = plane.other_core(other_out)
    out_all = out_all.astype(F32) + other_out.astype(F32)
    outs = [out_all[b * rows : (b + 1) * rows] for b in range(ranks)]
    outs = [outs[0]] + [v.astype(BF16) for v in outs[1:]]
    outs, dx_own = lax.optimization_barrier((outs, dxs[0]))
    dh, dh_stack, extra = rejoin(
        [dx_own] + dx_got, gates, mid_rows, cotangent, extra_t, a2, gain_two_row, plane.size
    )
    dh_stack, outs = lax.optimization_barrier((dh_stack, outs))
    out_got = expert_scatter(outs)

    d_weights, d_out_weights, da1 = attend_back(
        dh_stack,
        x_all,
        weights,
        out_weights,
        kept,
        bias,
        cosine,
        sine,
        extra,
        kv_heads,
        gain_one_row,
    )
    a_first, b_first, d_weights = lax.optimization_barrier((a_first, b_first, d_weights))
    a_next = add(by_row[0][1], *[v[1] for v in a_first])
    b_next = [add(by_mid[0][s], b_first[s]) for s in steps]
    a_got = plane.other_mid(a_next)
    b_got = [plane.next_row(v, s) for s, v in zip(steps, b_next)]
    a_next, b_next, d_weights, out_got = lax.optimization_barrier(
        (a_next, b_next, d_weights, out_got)
    )
    chip_count = plane.size // 2
    input_grad, by_rank, out_part = last(
        inputs,
        dh,
        extra_t,
        d_weights.reshape(chip_count, 2, ranks, weight_rows, columns),
        d_out_weights.reshape(chip_count, 2, weight_rows, model),
        da1,
        gain_one_row,
    )
    a_got, b_got, out_part = lax.optimization_barrier((a_got, b_got, out_part))
    parts_a = [by_row[0], *a_first, a_got]
    parts_b = [by_mid[0], b_first, *b_got]

    def total(parts):
        value = 0.0
        for v in parts:
            value = value + (v[0] if v.ndim == 5 else v)[:2].astype(F32)
        return value

    other = plane.other_core(
        jnp.where(plane.core == 0, total(parts_b), total(parts_a)).astype(BF16)
    )
    gate_grad, up_grad, down_grad = finish(
        core, parts_a, parts_b, other, w_down.shape[1], model, plane.size
    )
    output = mid_rows + outs[0]
    for v in out_got:
        output = output + v.astype(F32)

    w_output_grad = lax.ppermute(out_part, axes, [(b, a) for a, b in move]).astype(F32)
    by_rank = by_rank.astype(F32)

    def columns_of(start, width):
        piece = by_rank[:, :, start : start + width]
        return jnp.transpose(piece, (1, 0, 2)).reshape(weight_rows, ranks * width)

    extra_grad = jnp.sum(by_rank[:, :, columns - LANES :], axis=0)
    return (
        output,
        input_grad,
        extra_grad[:, gain_one_row],
        columns_of(0, q_cols),
        columns_of(q_cols, kv_cols),
        columns_of(rope_width, kv_cols),
        w_output_grad,
        extra_grad[:, gain_two_row],
        extra_grad[:, :n_experts],
        gate_grad,
        up_grad,
        down_grad,
    )


def solution(mesh):
    both = ("fsdp", "expert")
    rows, flat, stack = P(both, None), P(both), P("expert", "fsdp", None)
    weights = (flat, rows, rows, rows, rows, flat, rows, stack, stack, stack)
    return jax.shard_map(
        on_device,
        mesh=mesh,
        in_specs=(rows, rows) + weights + (rows, P("fsdp", None)),
        out_specs=(rows, rows) + weights,
        check_vma=False,
    )
```
